32 devices in a mesh: clip: 2 (over x), seq: 16 (over z, y, core).
Axes of the slice: x: 2, y: 2, z: 4, core: 2. Of those that a mesh axis runs over, the one named last changes fastest.
Arguments:
- tokens: bfloat16 [4, 2048, 1536], P('clip', 'seq'), may hold values from -6 to 6
- condition: float32 [4, 1024], replicated, may hold values from -6 to 6
- caption: bfloat16 [4, 256, 4096], P('clip', 'seq'), may hold values from -6 to 6
- caption_lengths: int32 [4], P('clip'), may hold values from 64 to 256
- positions: int32 [3, 4, 2048], P(None, 'clip', 'seq'), may hold values from 0 to 63
- modulation_weight: bfloat16 [1024, 9216], P(('clip', 'seq')), may hold values from -0.1875 to 0.1875
- modulation_bias: float32 [9216], replicated, may hold values from -3 to 3
- norm_gains: float32 [5, 1536], replicated, may hold values from 0.1 to 1.9
- cross_gate: float32 [24], replicated, may hold values from -0.5 to 0.5
- input_weight: bfloat16 [1536, 4608], P(('clip', 'seq')), may hold values from -0.15625 to 0.15625
- output_weight: bfloat16 [1536, 1536], P(('clip', 'seq')), may hold values from -4 to 4
- caption_key_weight: bfloat16 [4096, 1536], P(('clip', 'seq')), may hold values from -0.09375 to 0.09375
- caption_value_weight: bfloat16 [4096, 1536], P(('clip', 'seq')), may hold values from -0.09375 to 0.09375
- gate_weight: bfloat16 [1536, 4096], P(('clip', 'seq')), may hold values from -0.15625 to 0.15625
- up_weight: bfloat16 [1536, 4096], P(('clip', 'seq')), may hold values from -0.15625 to 0.15625
- down_weight: bfloat16 [4096, 1536], P(('clip', 'seq')), may hold values from -0.09375 to 0.09375
- cotangent: bfloat16 [4, 2048, 1536], P('clip', 'seq'), may hold values from -6 to 6
Outputs:
- output: bfloat16 [4, 2048, 1536], P('clip', 'seq')
- d_tokens: float32 [4, 2048, 1536], P('clip', 'seq')
- d_caption: float32 [4, 256, 4096], P('clip', 'seq')
- d_condition: float32 [4, 1024], replicated
- d_modulation_weight: float32 [1024, 9216], P(('clip', 'seq'))
- d_modulation_bias: float32 [9216], replicated
- d_norm_gains: float32 [5, 1536], replicated
- d_cross_gate: float32 [24], replicated
- d_input_weight: float32 [1536, 4608], P(('clip', 'seq'))
- d_output_weight: float32 [1536, 1536], P(('clip', 'seq'))
- d_caption_key_weight: float32 [4096, 1536], P(('clip', 'seq'))
- d_caption_value_weight: float32 [4096, 1536], P(('clip', 'seq'))
- d_gate_weight: float32 [1536, 4096], P(('clip', 'seq'))
- d_up_weight: float32 [1536, 4096], P(('clip', 'seq'))
- d_down_weight: float32 [4096, 1536], P(('clip', 'seq'))
The draws below stay inside these ranges and needn't reach their ends.
Inputs may be any that keep to these rules, and one draw needn't show every extreme that they name: `caption_lengths`: caption slots at or after a clip's length are padding.
All inputs are finite; a program needn't handle non-finite values.
Results may differ from the reference program's by a relative error of at most 0.023.
Values may be sent and summed in bfloat16 or wider, within the bound.
No kernel may reach another device: no remote copies, remote signals or barrier semaphores. Data moves between devices by JAX's collectives and lax.ppermute only.
A program may use at most 640 MiB of HBM per device.

```python
import jax
import jax.numpy as jnp
from jax import lax

D = 1536
HEADS = 24
FF = 4096
TEXT = 4096
COND = 1024
CAP = 256
LENGTH = 2048
CLIPS = 4


def plant(entries, own_key, low, top_value):
    longest = entries.shape.index(max(entries.shape))
    spots = []
    for shift in (0, 1):
        where = [jax.random.randint(jax.random.fold_in(own_key, axis), (), 0, length) for axis, length in enumerate(entries.shape)]
        where[longest] = (where[longest] + shift) % entries.shape[longest]
        spots.append(tuple(where))
    return entries.at[spots[0]].set(low).at[spots[1]].set(top_value)


def levels(stream_key, shape, cuts, least, top_value):
    factor_of, own = 1.0, jax.random.fold_in(stream_key, 6)
    for position, shards_of in cuts:
        heights = jnp.exp(jax.random.uniform(jax.random.fold_in(own, position), (shards_of,), jnp.float32, least / len(cuts), top_value / len(cuts)))
        factor_of = factor_of * jnp.repeat(heights, shape[position] // shards_of).reshape([-1 if axis == position else 1 for axis in range(len(shape))])
    return factor_of


def bell_draw(stream_key, dims, spread, limit, shards=(), held_as=jnp.bfloat16):
    drawn = jax.random.normal(stream_key, dims, jnp.float32) * spread
    if len(shards) > 0:
        drawn = levels(stream_key, dims, shards, -0.22, 0.18) * drawn
    return jnp.clip(drawn, min=-limit, max=limit).astype(held_as)


def setup_inputs(seed: int = 0) -> dict:
    arg_keys = jax.random.split(jax.random.key(seed), 18)
    return {
        "tokens": bell_draw(arg_keys[0], (CLIPS, LENGTH, D), 1.0, 6.0, ((0, 2), (1, 16))),
        "condition": bell_draw(arg_keys[1], (CLIPS, COND), 1.0, 6.0, (), jnp.float32),
        "caption": bell_draw(arg_keys[2], (CLIPS, CAP, TEXT), 1.0, 6.0, ((0, 2), (1, 16))),
        "caption_lengths": plant(jax.random.randint(arg_keys[3], (CLIPS,), CAP // 4, CAP + 1), jax.random.fold_in(arg_keys[3], 1), CAP // 4, CAP).astype(jnp.int32),
        "positions": plant(jax.random.randint(arg_keys[4], (3, CLIPS, LENGTH), 0, 64), jax.random.fold_in(arg_keys[4], 1), 0, 63).astype(jnp.int32),
        "modulation_weight": bell_draw(arg_keys[5], (COND, 6 * D), COND ** -0.5, 0.1875, ((0, 32),)),
        "modulation_bias": bell_draw(arg_keys[6], (6 * D,), 0.5, 3.0, (), jnp.float32),
        "norm_gains": jnp.clip(1.0 + 0.18 * jax.random.normal(arg_keys[7], (5, D), jnp.float32), 0.1, 1.9),
        "cross_gate": jnp.clip(jax.random.uniform(arg_keys[8], (HEADS,), jnp.float32, -0.5, 0.5), -0.5, 0.5),
        "input_weight": bell_draw(arg_keys[9], (D, 3 * D), D ** -0.5, 0.15625, ((0, 32),)),
        "output_weight": bell_draw(arg_keys[10], (D, D), (max(1, 3 * D // LENGTH)) ** -0.5, 4.0, ((0, 32),)),
        "caption_key_weight": bell_draw(arg_keys[11], (TEXT, D), TEXT ** -0.5, 0.09375, ((0, 32),)),
        "caption_value_weight": bell_draw(arg_keys[12], (TEXT, D), TEXT ** -0.5, 0.09375, ((0, 32),)),
        "gate_weight": bell_draw(arg_keys[13], (D, FF), D ** -0.5, 0.15625, ((0, 32),)),
        "up_weight": bell_draw(arg_keys[14], (D, FF), D ** -0.5, 0.15625, ((0, 32),)),
        "down_weight": bell_draw(arg_keys[15], (FF, D), FF ** -0.5, 0.09375, ((0, 32),)),
        "cotangent": bell_draw(arg_keys[16], (CLIPS, LENGTH, D), 1.0, 6.0, ((0, 2), (1, 16))),
    }


@jax.custom_vjp
def low(v):
    return lax.optimization_barrier(v.astype(jnp.bfloat16)).astype(jnp.float32)

@jax.custom_vjp
def low_back(v):
    return v

def low_keep(v):
    return (low(v), None)

def low_pass(kept, grad):
    return (grad,)

def back_keep(v):
    return (v, None)

def back_low(kept, grad):
    return (low(grad),)
low.defvjp(low_keep, low_pass)
low_back.defvjp(back_keep, back_low)
EPSILON = 1e-06
NEGATIVE = -1e+30
PRECISE = lax.Precision.HIGHEST

def rms_apply(values, scaling):
    return values * lax.rsqrt(lax.optimization_barrier(jnp.mean(values * values, axis=-1, keepdims=True)) + EPSILON) * scaling

def rope_tables(places, head_dim):
    pair_count = head_dim // 2
    lead_pairs = pair_count // 4
    mid_pairs = (pair_count - lead_pairs) // 2
    pair_index = jnp.arange(pair_count, dtype=jnp.int32)
    axis_pick = (pair_index >= lead_pairs).astype(jnp.int32) + (pair_index >= lead_pairs + mid_pairs).astype(jnp.int32)
    anchor = jnp.where(axis_pick == 0, 0, jnp.where(axis_pick == 1, lead_pairs, lead_pairs + mid_pairs))
    extent = jnp.where(axis_pick == 0, lead_pairs, jnp.where(axis_pick == 1, mid_pairs, pair_count - lead_pairs - mid_pairs))
    frequency = jnp.power(10000.0, -(pair_index - anchor).astype(jnp.float32) / extent.astype(jnp.float32))
    chosen = jnp.where(axis_pick == 0, places[0][..., None], jnp.where(axis_pick == 1, places[1][..., None], places[2][..., None]))
    angles = chosen.astype(jnp.float32) * frequency
    return (jnp.cos(angles), jnp.sin(angles))

def rope_apply(vectors, cosine, sine_part):
    half_width = vectors.shape[-1] // 2
    front_half = vectors[..., :half_width]
    back_half = vectors[..., half_width:]
    cosine = cosine[..., None, :]
    sine_part = sine_part[..., None, :]
    return jnp.concatenate([front_half * cosine - back_half * sine_part, front_half * sine_part + back_half * cosine], axis=-1)

def project_heads(query_raw, key_raw, query_gain, key_gain, cosine, sine_part, head_count):
    shape = query_raw.shape[:-1] + (head_count, query_raw.shape[-1] // head_count)
    queries = rope_apply(rms_apply(query_raw, query_gain).reshape(shape), cosine, sine_part)
    keys = rope_apply(rms_apply(key_raw, key_gain).reshape(shape), cosine, sine_part)
    return (queries, keys)

def self_attention(queries, keys, values):
    length = queries.shape[0]
    block_rows = min(512, length)
    score_scale = queries.shape[-1] ** (-0.5)
    stacked = queries.reshape((length // block_rows, block_rows) + queries.shape[1:])

    def one_block(query_block):
        scores = low_back(jnp.einsum('qhd,khd->qhk', query_block, keys, precision=PRECISE) * score_scale)
        log_total = jax.nn.logsumexp(scores, axis=-1, keepdims=True)
        probs = low(jnp.exp(scores - log_total))
        return jnp.einsum('qhk,khd->qhd', probs, values, precision=PRECISE)
    result = lax.map(jax.checkpoint(one_block), stacked)
    return result.reshape(queries.shape)

def cross_attention(queries, caption_keys, caption_values, live_count):
    score_scale = queries.shape[-1] ** (-0.5)
    scores = low_back(jnp.einsum('qhd,khd->qhk', queries, caption_keys, precision=PRECISE) * score_scale)
    key_valid = jnp.arange(caption_keys.shape[0], dtype=jnp.int32) < live_count
    scores = jnp.where(key_valid, scores, NEGATIVE)
    log_total = jax.nn.logsumexp(scores, axis=-1, keepdims=True)
    probs = low(jnp.exp(scores - log_total))
    return jnp.einsum('qhk,khd->qhd', probs, caption_values, precision=PRECISE)

def clip_forward(floats, inputs):
    mod_weight, mod_bias, gains, gate_heads, in_weight, out_weight, ckey_weight, cvalue_weight, gate_w, up_w, down_w = floats
    token_vals, condition_row, caption_vals, live_count, places = inputs
    width = token_vals.shape[-1]
    head_count = gate_heads.shape[0]
    head_dim = width // head_count
    silu_cond = low(jax.nn.silu(condition_row))
    modulation = low_back(jnp.dot(silu_cond, mod_weight, precision=PRECISE) + mod_bias)
    shift_a = modulation[0 * width:1 * width]
    scale_a = modulation[1 * width:2 * width]
    gate_a = modulation[2 * width:3 * width]
    shift_f = modulation[3 * width:4 * width]
    scale_f = modulation[4 * width:5 * width]
    gate_f = modulation[5 * width:6 * width]
    normed_a = rms_apply(token_vals, gains[0])
    attn_in = low(normed_a * (1.0 + scale_a) + shift_a)
    projected = low_back(jnp.dot(attn_in, in_weight, precision=PRECISE))
    cosine, sine_part = rope_tables(places, head_dim)
    query_f, key_f = project_heads(projected[:, :width], projected[:, width:2 * width], gains[1], gains[2], cosine, sine_part, head_count)
    queries = low(query_f)
    keys = low(key_f)
    values = low(projected[:, 2 * width:]).reshape(key_f.shape)
    caption_raw = low_back(jnp.dot(caption_vals, ckey_weight, precision=PRECISE))
    caption_keys = low(rms_apply(caption_raw, gains[3])).reshape(caption_raw.shape[0], head_count, head_dim)
    caption_values = low(low_back(jnp.dot(caption_vals, cvalue_weight, precision=PRECISE))).reshape(caption_raw.shape[0], head_count, head_dim)
    o_self = low_back(self_attention(queries, keys, values))
    o_cross = low_back(cross_attention(queries, caption_keys, caption_values, live_count))
    combined = low((o_self + jnp.tanh(gate_heads)[:, None] * o_cross).reshape(token_vals.shape))
    branch = low_back(jnp.dot(combined, out_weight, precision=PRECISE))
    middle = token_vals + gate_a * branch
    normed_f = rms_apply(middle, gains[4])
    ffn_in = low(normed_f * (1.0 + scale_f) + shift_f)
    gate_vals = low_back(jnp.dot(ffn_in, gate_w, precision=PRECISE))
    up_vals = low_back(jnp.dot(ffn_in, up_w, precision=PRECISE))
    hidden = low(jax.nn.silu(gate_vals) * up_vals)
    ffn_out = low_back(jnp.dot(hidden, down_w, precision=PRECISE))
    return middle + gate_f * ffn_out

def reference(tokens, condition, caption, caption_lengths, positions, modulation_weight, modulation_bias, norm_gains, cross_gate, input_weight, output_weight, caption_key_weight, caption_value_weight, gate_weight, up_weight, down_weight, cotangent):
    floats = (modulation_weight.astype(jnp.float32), modulation_bias, norm_gains, cross_gate, input_weight.astype(jnp.float32), output_weight.astype(jnp.float32), caption_key_weight.astype(jnp.float32), caption_value_weight.astype(jnp.float32), gate_weight.astype(jnp.float32), up_weight.astype(jnp.float32), down_weight.astype(jnp.float32))
    places = jnp.transpose(positions, (1, 0, 2))

    def forward(weights_in, tokens_in, condition_in, caption_in):

        def clip_step(loop_state, inputs):
            return (loop_state, clip_forward(weights_in, inputs))
        _, results = lax.scan(clip_step, None, (tokens_in, condition_in, caption_in, caption_lengths, places))
        return results
    result, backward = jax.vjp(forward, floats, tokens.astype(jnp.float32), condition, caption.astype(jnp.float32))
    grads, d_tokens, d_condition, d_caption = backward(cotangent.astype(jnp.float32))
    return (result.astype(jnp.bfloat16), d_tokens, d_caption, d_condition, grads[0], grads[1], grads[2], grads[3], grads[4], grads[5], grads[6], grads[7], grads[8], grads[9], grads[10])
```

```python
import jax
import jax.numpy as jnp
from jax import lax
from jax.sharding import Mesh
from jax.sharding import PartitionSpec as P

EPSILON = 1e-06
NEGATIVE = -1e30
BF = jnp.bfloat16
F32 = jnp.float32
SEQ = ("half", "rep", "tz", "ty", "tc")
GROUPS = ("clip", "half", "rep")
TEAM = ("tz", "ty", "tc")
EVERY = ("clip",) + SEQ


def swap(block, axis):
    return lax.ppermute(block, axis, [(0, 1), (1, 0)])


def dot(left, right, dims, out=F32):
    return lax.dot_general(left, right, (dims, ((), ())), preferred_element_type=out)


def mm(left, right):
    return dot(left, right, ((1,), (0,)))


def mm_t(left, right):
    return dot(left, right, ((1,), (1,)))


def t_mm(left, right):
    return dot(left, right, ((0,), (0,)))


def join(parts, axis=0):
    return jnp.concatenate(parts, axis=axis)


def gather_rows(block):
    half = block.shape[0] // 2
    first, second = block[:half], block[half:]
    first, second = join([first, swap(first, "ty")]), join([second, swap(second, "tz")])
    first, second = join([first, swap(first, "tz")]), join([second, swap(second, "ty")])
    both = join([first, second])
    return join([both, swap(both, "tc")])


def gathered_ids(rank, rows):
    half = rows // 2
    low = jnp.arange(half, dtype=jnp.int32)

    def place(who, part):
        return who * rows + part * half + low

    def chip(who):
        return join(
            [place(who, 0), place(who ^ 2, 0), place(who ^ 4, 0), place(who ^ 6, 0)]
            + [place(who, 1), place(who ^ 4, 1), place(who ^ 2, 1), place(who ^ 6, 1)]
        )

    return join([chip(rank), chip(rank ^ 1)])


def scatter_rows(make, count):
    mid = count // 2
    other = swap(make(mid, count).astype(BF), "tc")
    mine = make(0, mid) + other.astype(F32)
    first, second = mine[: mid // 2], mine[mid // 2 :]
    q = mid // 4
    a, b = swap(first[q:].astype(BF), "tz"), swap(second[q:].astype(BF), "ty")
    first, second = first[:q] + a.astype(F32), second[:q] + b.astype(F32)
    q = q // 2
    a, b = swap(first[q:].astype(BF), "ty"), swap(second[q:].astype(BF), "tz")
    return join([first[:q] + a.astype(F32), second[:q] + b.astype(F32)])


def split_places(rows_last):
    lead = rows_last.shape[:-1]
    half = rows_last.shape[-1] // 16
    tiled = rows_last.reshape(lead + (2, 2, 2, 2, half))
    second = jnp.swapaxes(tiled[..., :, 1, :, :, :], -3, -2)
    return jnp.stack([tiled[..., :, 0, :, :, :], second], axis=-4)


def merge_places(tiled):
    second = jnp.swapaxes(tiled[..., :, 1, :, :, :], -3, -2)
    tiled = jnp.stack([tiled[..., :, 0, :, :, :], second], axis=-4)
    return tiled.reshape(tiled.shape[:-5] + (-1,))


def team_row_sum(values):
    tiled = split_places(values)
    for axis, dim in (("tc", -5), ("ty", -2), ("tz", -3)):
        tiled = tiled + jnp.flip(swap(tiled, axis), dim)
    return merge_places(tiled)


def to_true_blocks(rows, bits):
    width = rows.shape[-1]
    half = rows.shape[0] // 16
    tiled = rows.reshape(2, 2, 2, 2, half, width)
    first = tiled[:, 0]
    second = jnp.swapaxes(tiled[:, 1], 1, 2)
    both = jnp.stack([first, second], axis=3)
    for dim, bit in zip((1, 2, 0), bits):
        both = jnp.where(bit == 1, jnp.flip(both, dim), both)
    return jnp.transpose(both, (1, 2, 0, 3, 4, 5)).reshape(8, 2 * half, width)


def from_true_blocks(blocks, bits):
    width = blocks.shape[-1]
    half = blocks.shape[1] // 2
    both = jnp.transpose(blocks.reshape(2, 2, 2, 2, half, width), (2, 0, 1, 3, 4, 5))
    for dim, bit in zip((1, 2, 0), bits):
        both = jnp.where(bit == 1, jnp.flip(both, dim), both)
    first = both[:, :, :, 0]
    second = jnp.swapaxes(both[:, :, :, 1], 1, 2)
    return jnp.stack([first, second], axis=1).reshape(16 * half, width)


def rms_factor(square_sum, width):
    return lax.rsqrt(square_sum / width + EPSILON)


def rms_apply(values, scaling):
    return values * lax.rsqrt(jnp.mean(values * values, axis=-1, keepdims=True) + EPSILON) * scaling


def rms_back(values, scaling, grad):
    factor = lax.rsqrt(jnp.mean(values * values, axis=-1, keepdims=True) + EPSILON)
    normed = values * factor
    scaled = grad * scaling
    inner = jnp.mean(scaled * normed, axis=-1, keepdims=True)
    return factor * (scaled - normed * inner), jnp.sum(grad * normed, axis=0)


def rope_tables(places, head_dim):
    pair_count = head_dim // 2
    lead_pairs = pair_count // 4
    mid_pairs = (pair_count - lead_pairs) // 2
    last_pairs = pair_count - lead_pairs - mid_pairs
    angles = []
    for which, extent in enumerate((lead_pairs, mid_pairs, last_pairs)):
        offsets = jnp.arange(extent, dtype=F32)
        angles.append(places[which][:, None] * jnp.power(10000.0, -offsets / extent))
    angles = join(angles, axis=1)
    cosine, sine = jnp.cos(angles), jnp.sin(angles)
    return join([cosine, cosine], axis=1), join([-sine, sine], axis=1)


def turn(vectors, cosine, sine):
    rows, width = vectors.shape
    head_dim = cosine.shape[-1]
    heads = vectors.reshape(rows, width // head_dim, head_dim)
    half = head_dim // 2
    crossed = join([heads[..., half:], heads[..., :half]], axis=-1)
    return (heads * cosine[:, None] + crossed * sine[:, None]).reshape(rows, width)


def self_forward(queries, keys, values, scale):
    scores = jnp.einsum("thd,shd->hts", queries, keys, preferred_element_type=F32) * scale
    peak = jnp.max(scores, axis=-1, keepdims=True)
    weights = jnp.exp(scores - peak)
    total = jnp.sum(weights, axis=-1, keepdims=True)
    out = jnp.einsum("hts,shd->htd", weights.astype(BF), values, preferred_element_type=F32)
    return out / total, peak + jnp.log(total)


def self_backward(queries, keys, values, grads, log_total, delta, scale):
    scores = jnp.einsum("thd,shd->hts", queries, keys, preferred_element_type=F32) * scale
    probs = jnp.exp(scores - log_total)
    dp = jnp.einsum("thd,shd->hts", grads, values, preferred_element_type=F32)
    ds = (probs * (dp - delta)).astype(BF)
    dq = jnp.einsum("hts,shd->thd", ds, keys, preferred_element_type=F32) * scale
    dk = jnp.einsum("hts,thd->shd", ds, queries, preferred_element_type=F32) * scale
    dv = jnp.einsum("hts,thd->shd", probs.astype(BF), grads, preferred_element_type=F32)
    return dq, dk, dv


def on_device(
    tokens,
    condition,
    caption,
    caption_lengths,
    positions,
    modulation_weight,
    modulation_bias,
    norm_gains,
    cross_gate,
    input_weight,
    output_weight,
    caption_key_weight,
    caption_value_weight,
    gate_weight,
    up_weight,
    down_weight,
    cotangent,
):
    clips_here, clip_rows, width = tokens.shape
    head_count = cross_gate.shape[0]
    head_dim = width // head_count
    scale = head_dim ** (-0.5)
    team = 8
    heads = head_count // team
    part = heads * head_dim
    groups = lax.axis_size(GROUPS)
    reps = lax.axis_size("rep")
    half = lax.axis_index("half")
    bits = tuple(lax.axis_index(axis) for axis in TEAM)
    rank = bits[0] * 4 + bits[1] * 2 + bits[2]
    clip_pair = lax.axis_index("clip")
    device = lax.axis_index(EVERY)

    def own_clip(block):
        kept = lax.dynamic_index_in_dim(block, half, 0, keepdims=False)
        sent = lax.dynamic_index_in_dim(block, 1 - half, 0, keepdims=False)
        return join([kept, swap(sent, "half")])

    def back_clip(block):
        rows = block.shape[0] // 2
        kept, other = block[:rows], block[rows:]
        other = swap(other.astype(BF), "half").astype(block.dtype)
        return jnp.where(half == 0, jnp.stack([kept, other]), jnp.stack([other, kept]))

    def own_columns(table):
        return lax.dynamic_slice_in_dim(table, rank * part, part, table.ndim - 1)

    shard_rows = modulation_weight.shape[0]
    silu_all = jax.nn.silu(condition).astype(BF)
    silu_rows = lax.dynamic_slice_in_dim(silu_all, device * shard_rows, shard_rows, 1)
    mod_part = mm(silu_rows, modulation_weight)
    mod_part = mod_part.reshape(lax.axis_size("clip"), clips_here, -1)
    mod_pair = lax.dynamic_index_in_dim(mod_part, clip_pair, 0, keepdims=False) + swap(
        lax.dynamic_index_in_dim(mod_part, 1 - clip_pair, 0, keepdims=False), "clip"
    )
    mod_own = lax.dynamic_index_in_dim(mod_pair, half, 0, keepdims=True) + swap(
        lax.dynamic_index_in_dim(mod_pair, 1 - half, 0, keepdims=True), "half"
    )
    if reps > 1:
        mod_own = lax.psum(mod_own, "rep")
    for axis in TEAM:
        mod_own = mod_own + swap(mod_own, axis)
    modulation = mod_own + modulation_bias
    shift_attn, scale_attn, gate_attn, shift_ffn, scale_ffn, gate_ffn = (
        modulation[:, i * width : (i + 1) * width] for i in range(6)
    )

    def team_slice(shard):
        by_rank = jnp.transpose(shard, (1, 0, 2))
        mine = lax.all_to_all(by_rank, TEAM, split_axis=0, concat_axis=0, tiled=True)
        mine = mine.reshape(-1, shard.shape[2])
        return lax.all_gather(mine, GROUPS, axis=0, tiled=True)

    rows_in = input_weight.shape[0]
    w_in = team_slice(
        jnp.transpose(input_weight.reshape(rows_in, 3, team, part), (0, 2, 1, 3)).reshape(
            rows_in, team, 3 * part
        )
    )
    rows_cap = caption_key_weight.shape[0]
    w_cap = team_slice(
        join(
            [
                caption_key_weight.reshape(rows_cap, team, part),
                caption_value_weight.reshape(rows_cap, team, part),
            ],
            axis=2,
        )
    )
    w_out = lax.all_gather(output_weight, EVERY, axis=0, tiled=True)
    ff_block = down_weight.shape[0]

    def ff_columns(weight):
        rows = weight.shape[0]
        tiled = weight.reshape(rows, groups, team, ff_block)
        return jnp.transpose(tiled, (0, 2, 1, 3)).reshape(rows, team, groups * ff_block)

    w_gate_up = team_slice(join([ff_columns(gate_weight), ff_columns(up_weight)], axis=2))
    w_down = lax.all_gather(down_weight, GROUPS, axis=0, tiled=True)
    ff_part = groups * ff_block
    w_gate, w_up = w_gate_up[:, :ff_part], w_gate_up[:, ff_part:]

    token_vals = own_clip(tokens).astype(F32)
    rows_here = token_vals.shape[0]
    team_rows = team * rows_here
    places = own_clip(jnp.transpose(positions, (1, 2, 0)))
    all_places = gather_rows(places)
    cosine, sine = rope_tables(all_places.astype(F32).T, head_dim)
    normed_attn = rms_apply(token_vals, norm_gains[0])
    attn_in = (normed_attn * (1.0 + scale_attn) + shift_attn).astype(BF)
    attn_all = gather_rows(attn_in)
    projected = mm(attn_all, w_in)
    raw_q, raw_k, raw_v = (projected[:, i * part : (i + 1) * part] for i in range(3))
    squares = jnp.stack([jnp.sum(raw_q * raw_q, axis=1), jnp.sum(raw_k * raw_k, axis=1)])
    factors = rms_factor(team_row_sum(squares), width)
    gain_q, gain_k, gain_c = (own_columns(norm_gains[i]) for i in (1, 2, 3))
    factor_q, factor_k = factors[0][:, None], factors[1][:, None]
    queries = turn(raw_q * factor_q * gain_q, cosine, sine).astype(BF)
    keys = turn(raw_k * factor_k * gain_k, cosine, sine).astype(BF)
    values = raw_v.astype(BF)

    cap_rows = own_clip(caption)
    slots_here = caption.shape[1]
    cap_all = gather_rows(cap_rows)
    ids = gathered_ids(rank, cap_rows.shape[0])
    own_rank, own_row = ids // cap_rows.shape[0], ids % cap_rows.shape[0]
    holder = jnp.where(own_row < slots_here, half, 1 - half) * reps + lax.axis_index("rep")
    slot = (holder * team + own_rank) * slots_here + own_row % slots_here
    craw = mm(cap_all, w_cap)
    craw_key, craw_value = craw[:, :part], craw[:, part:]
    factor_c = rms_factor(
        team_row_sum(jnp.sum(craw_key * craw_key, axis=1)[None]), width
    )[0][:, None]
    ckeys = (craw_key * factor_c * gain_c).astype(BF)
    cvalues = craw_value.astype(BF)
    all_keys, all_values, all_ckeys, all_cvalues, all_slots = keys, values, ckeys, cvalues, slot
    if reps > 1:
        all_keys, all_values, all_ckeys, all_cvalues = (
            lax.all_gather(v, "rep", axis=0, tiled=True)
            for v in (keys, values, ckeys, cvalues)
        )
        rep_step = lax.axis_index("rep")
        all_slots = join([slot + (r - rep_step) * team * slots_here for r in range(reps)])
    own_length = lax.dynamic_index_in_dim(caption_lengths, half, 0, keepdims=False)
    live = all_slots < own_length

    def by_head(block):
        return block.reshape(block.shape[0], heads, head_dim)

    q3, k3, v3 = by_head(queries), by_head(all_keys), by_head(all_values)
    ck3, cv3 = by_head(all_ckeys), by_head(all_cvalues)
    o_self, log_total = self_forward(q3, k3, v3, scale)
    cross_scores = jnp.einsum("thd,shd->hts", q3, ck3, preferred_element_type=F32) * scale
    cross_scores = jnp.where(live, cross_scores, NEGATIVE)
    cross_probs = jax.nn.softmax(cross_scores, axis=-1)
    cross_low = cross_probs.astype(BF)
    o_cross = jnp.einsum("hts,shd->htd", cross_low, cv3, preferred_element_type=F32)
    tanh_gate = jnp.tanh(lax.dynamic_slice_in_dim(cross_gate, rank * heads, heads))
    tanh_wide = tanh_gate[:, None, None]
    mixed = jnp.transpose(o_self + tanh_wide * o_cross, (1, 0, 2)).reshape(team_rows, part)
    mixed = to_true_blocks(mixed.astype(BF), bits)
    mixed = lax.all_to_all(mixed, TEAM, split_axis=0, concat_axis=0, tiled=True)
    combined = jnp.transpose(mixed, (1, 0, 2)).reshape(rows_here, width)

    branch = mm(combined, w_out)
    middle = token_vals + gate_attn * branch
    normed_ffn = rms_apply(middle, norm_gains[4])
    ffn_in = (normed_ffn * (1.0 + scale_ffn) + shift_ffn).astype(BF)
    grad_out = own_clip(cotangent).astype(F32)
    d_ffn = (gate_ffn * grad_out).astype(BF)
    d_ffn_all = gather_rows(d_ffn)
    ffn_all = gather_rows(ffn_in)
    gate_vals = mm(ffn_all, w_gate)
    up_vals = mm(ffn_all, w_up)
    hidden = (jax.nn.silu(gate_vals) * up_vals).astype(BF)
    d_hidden = mm_t(d_ffn_all, w_down)
    sig = jax.nn.sigmoid(gate_vals)
    silu_gate = gate_vals * sig
    d_gate = (d_hidden * up_vals * (sig + silu_gate * (1.0 - sig))).astype(BF)
    d_up = (d_hidden * silu_gate).astype(BF)
    d_ffn_in = scatter_rows(
        lambda lo, hi: mm_t(d_gate[lo:hi], w_gate) + mm_t(d_up[lo:hi], w_up), team_rows
    )
    ffn_out = scatter_rows(lambda lo, hi: mm(hidden[lo:hi], w_down), team_rows)
    result = back_clip((middle + gate_ffn * ffn_out).astype(BF))
    d_gate_ffn = jnp.sum(grad_out * ffn_out, axis=0)
    grad_down = t_mm(hidden, d_ffn_all)
    grad_gate = t_mm(ffn_all, d_gate)
    grad_up = t_mm(ffn_all, d_up)

    def own_rows(slice_grad):
        summed = lax.psum_scatter(slice_grad.astype(BF), GROUPS, scatter_dimension=0, tiled=True)
        by_rank = summed.reshape(team, -1, summed.shape[-1])
        by_rank = lax.all_to_all(by_rank, TEAM, split_axis=0, concat_axis=0, tiled=True)
        return jnp.transpose(by_rank, (1, 0, 2)).astype(F32)

    sum_down = lax.psum_scatter(
        grad_down.astype(BF), GROUPS, scatter_dimension=0, tiled=True
    ).astype(F32)
    sum_gate_up = own_rows(join([grad_gate, grad_up], axis=1))

    def ff_rows(block):
        rows = block.shape[0]
        tiled = block.reshape(rows, team, groups, ff_block)
        return jnp.transpose(tiled, (0, 2, 1, 3)).reshape(rows, -1)

    sum_gate, sum_up = ff_rows(sum_gate_up[..., :ff_part]), ff_rows(sum_gate_up[..., ff_part:])

    d_scale_ffn = jnp.sum(d_ffn_in * normed_ffn, axis=0)
    d_shift_ffn = jnp.sum(d_ffn_in, axis=0)
    d_middle_norm, d_gain_ffn = rms_back(middle, norm_gains[4], d_ffn_in * (1.0 + scale_ffn))
    d_middle = grad_out + d_middle_norm
    d_branch = (gate_attn * d_middle).astype(BF)
    d_gate_attn = jnp.sum(d_middle * branch, axis=0)
    d_combined = mm_t(d_branch, w_out).astype(BF)
    grad_output = t_mm(combined, d_branch)
    sum_output = lax.psum_scatter(
        grad_output.astype(BF), EVERY, scatter_dimension=0, tiled=True
    ).astype(F32)
    d_mixed = jnp.transpose(d_combined.reshape(rows_here, team, part), (1, 0, 2))
    d_mixed = lax.all_to_all(d_mixed, TEAM, split_axis=0, concat_axis=0, tiled=True)
    d_self = by_head(from_true_blocks(d_mixed, bits))
    d_self_f = jnp.transpose(d_self.astype(F32), (1, 0, 2))
    d_cross = jnp.transpose((tanh_wide * d_self_f).astype(BF), (1, 0, 2))

    d_cross_gate = jnp.sum(d_self_f * o_cross, axis=(1, 2)) * (1.0 - tanh_gate * tanh_gate)
    cross_dp = jnp.einsum("thd,shd->hts", d_cross, cv3, preferred_element_type=F32)
    cross_delta = jnp.sum(cross_probs * cross_dp, axis=-1, keepdims=True)
    cross_ds = (cross_probs * (cross_dp - cross_delta)).astype(BF)
    dq_cross = jnp.einsum("hts,shd->thd", cross_ds, ck3, preferred_element_type=F32) * scale
    d_ckeys = jnp.einsum("hts,thd->shd", cross_ds, q3, preferred_element_type=F32) * scale
    d_cvalues = jnp.einsum("hts,thd->shd", cross_low, d_cross, preferred_element_type=F32)
    delta = jnp.sum(d_self_f * o_self, axis=-1, keepdims=True)
    dq_self, dk, dv = self_backward(q3, k3, v3, d_self, log_total, delta, scale)
    dq = (dq_self + dq_cross).reshape(team_rows, part)
    dk, dv = dk.reshape(-1, part), dv.reshape(-1, part)
    d_ckeys, d_cvalues = d_ckeys.reshape(-1, part), d_cvalues.reshape(-1, part)
    if reps > 1:
        dk, dv, d_ckeys, d_cvalues = (
            lax.psum_scatter(v, "rep", scatter_dimension=0, tiled=True)
            for v in (dk, dv, d_ckeys, d_cvalues)
        )

    turned_q, turned_k = turn(dq, cosine, -sine), turn(dk, cosine, -sine)
    inner = jnp.stack(
        [
            jnp.sum(turned_q * gain_q * raw_q, axis=1),
            jnp.sum(turned_k * gain_k * raw_k, axis=1),
        ]
    )
    inner = team_row_sum(inner)

    def norm_back(grad, gain, raw, factor, row_sum):
        normed = raw * factor
        return (
            factor * (grad * gain - normed * (factor * row_sum[:, None] / width)),
            jnp.sum(grad * normed, axis=0),
        )

    d_raw_q, d_gain_q = norm_back(turned_q, gain_q, raw_q, factor_q, inner[0])
    d_raw_k, d_gain_k = norm_back(turned_k, gain_k, raw_k, factor_k, inner[1])
    d_projected = join([d_raw_q, d_raw_k, dv], axis=1).astype(BF)
    d_attn_in = scatter_rows(lambda lo, hi: mm_t(d_projected[lo:hi], w_in), team_rows)
    inner_c = team_row_sum(jnp.sum(d_ckeys * gain_c * craw_key, axis=1)[None])[0]
    d_craw, d_gain_c = norm_back(d_ckeys, gain_c, craw_key, factor_c, inner_c)
    d_cap_low = join([d_craw, d_cvalues], axis=1).astype(BF)
    d_caption = scatter_rows(lambda lo, hi: mm_t(d_cap_low[lo:hi], w_cap), cap_all.shape[0])
    d_caption = back_clip(d_caption)
    sum_input = own_rows(t_mm(attn_all, d_projected))
    sum_input = jnp.transpose(sum_input.reshape(rows_in, team, 3, part), (0, 2, 1, 3)).reshape(
        rows_in, -1
    )
    sum_cap = own_rows(t_mm(cap_all, d_cap_low))
    sum_ckey = sum_cap[..., :part].reshape(rows_cap, -1)
    sum_cvalue = sum_cap[..., part:].reshape(rows_cap, -1)

    d_scale_attn = jnp.sum(d_attn_in * normed_attn, axis=0)
    d_shift_attn = jnp.sum(d_attn_in, axis=0)
    d_tokens_norm, d_gain_attn = rms_back(token_vals, norm_gains[0], d_attn_in * (1.0 + scale_attn))
    d_tokens = back_clip(d_middle + d_tokens_norm)

    d_mod = join([d_shift_attn, d_scale_attn, d_gate_attn, d_shift_ffn, d_scale_ffn, d_gate_ffn])

    def placed(values, total, start):
        return lax.dynamic_update_slice_in_dim(jnp.zeros((total,), F32), values, start, 0)

    small = join(
        [d_gain_attn]
        + [placed(v, width, rank * part) for v in (d_gain_q, d_gain_k, d_gain_c)]
        + [d_gain_ffn, placed(d_cross_gate, 128, rank * heads)]
    )
    sums = join([d_mod, small])
    for axis in TEAM:
        sums = sums + swap(sums, axis)
    if reps > 1:
        sums = lax.psum(sums, "rep")
    mod_size = d_mod.shape[0]
    mod_low, small = sums[:mod_size].astype(BF)[None], sums[mod_size:]
    for axis, bit in (("half", half), ("clip", clip_pair)):
        other = swap(mod_low, axis)
        mod_low = jnp.where(bit == 0, join([mod_low, other]), join([other, mod_low]))
        small = small + swap(small, axis)
    gain_sum = small[: 5 * width].reshape(5, width)
    gate_sum = small[5 * width : 5 * width + head_count]
    d_bias = jnp.sum(mod_low.astype(F32), axis=0)
    grad_mod = t_mm(silu_rows, mod_low)
    d_silu = mm_t(mod_low, modulation_weight)
    d_silu = lax.dynamic_update_slice_in_dim(
        jnp.zeros(condition.shape, F32), d_silu, device * shard_rows, 1
    )
    if reps > 1:
        d_silu = lax.psum(d_silu, "rep")
    for axis in ("tc", "ty", "tz", "half", "clip"):
        d_silu = d_silu + swap(d_silu, axis)
    _, silu_back = jax.vjp(jax.nn.silu, condition)
    d_condition = silu_back(d_silu)[0]
    return (
        result,
        d_tokens,
        d_caption,
        d_condition,
        grad_mod,
        d_bias,
        gain_sum,
        gate_sum,
        sum_input,
        sum_output,
        sum_ckey,
        sum_cvalue,
        sum_gate,
        sum_up,
        sum_down,
    )


def solution(mesh):
    clip_count, seq_count = mesh.shape["clip"], mesh.shape["seq"]

    def program(*arrays):
        halves = arrays[0].shape[0] // clip_count
        shape = (clip_count, halves, seq_count // (halves * 8), 2, 2, 2)
        fine = Mesh(mesh.devices.reshape(shape), EVERY)
        rows = P("clip", SEQ, None)
        shard = P(EVERY, None)
        mapped = jax.shard_map(
            on_device,
            mesh=fine,
            in_specs=(
                rows,
                P(),
                rows,
                P("clip"),
                P(None, "clip", SEQ),
                shard,
                P(),
                P(),
                P(),
                shard,
                shard,
                shard,
                shard,
                shard,
                shard,
                shard,
                rows,
            ),
            out_specs=(rows, rows, rows, P(), shard, P(), P(), P()) + (shard,) * 7,
            check_vma=False,
        )
        return mapped(*arrays)

    return program
```

```python
import jax
import jax.numpy as jnp
from jax import lax
from jax.experimental import pallas as pl
from jax.experimental.pallas import tpu as pltpu
from jax.sharding import Mesh
from jax.sharding import PartitionSpec as P

EPSILON = 1e-06
NEGATIVE = -1e30
BF = jnp.bfloat16
F32 = jnp.float32
SEQ = ("half", "rep", "tz", "ty", "tc")
GROUPS = ("clip", "half", "rep")
TEAM = ("tz", "ty", "tc")
EVERY = ("clip",) + SEQ
KERNEL = pltpu.CompilerParams(
    vmem_limit_bytes=56 * 1024 * 1024, dimension_semantics=("arbitrary", "arbitrary")
)


def swap(block, axis):
    return lax.ppermute(block, axis, [(0, 1), (1, 0)])


def after(value, *others):
    return lax.optimization_barrier((value,) + others)[0]


def dot(left, right, left_dim, right_dim):
    dims = (((left_dim,), (right_dim,)), ((), ()))
    return lax.dot_general(left, right, dims, preferred_element_type=F32)


def join(parts, axis=0):
    return jnp.concatenate(parts, axis=axis)


def upright(block):
    return jnp.transpose(block.astype(F32)).astype(BF)


def self_forward_kernel(q_ref, k_ref, v_ref, o_ref, log_ref, k_rows):
    @pl.when(pl.program_id(1) == 0)
    def _():
        k_rows[...] = upright(k_ref[0])

    scores = dot(k_rows[...], q_ref[0], 1, 0)
    peak = jnp.max(scores, axis=0, keepdims=True)
    weights = jnp.exp(scores - peak)
    total = jnp.sum(weights, axis=0, keepdims=True)
    o_ref[0] = dot(v_ref[0], weights.astype(BF), 1, 0) / total
    log_ref[0] = peak + jnp.log(total)


def self_backward_kernel(
    q_ref, g_ref, log_ref, delta_ref, k_ref, v_ref, dq_ref, dk_ref, dv_ref, k_rows, v_rows, dk, dv
):
    step = pl.program_id(1)

    @pl.when(step == 0)
    def _():
        k_rows[...] = upright(k_ref[0])
        v_rows[...] = upright(v_ref[0])
        dk[...] = jnp.zeros_like(dk)
        dv[...] = jnp.zeros_like(dv)

    q, g = q_ref[0], g_ref[0]
    probs = jnp.exp(dot(k_rows[...], q, 1, 0) - log_ref[0])
    ds = (probs * (dot(v_rows[...], g, 1, 0) - delta_ref[0])).astype(BF)
    dv[...] += dot(probs.astype(BF), g, 1, 1)
    dk[...] += dot(ds, q, 1, 1)
    dq_ref[0] = dot(k_ref[0], ds, 1, 0)

    @pl.when(step == pl.num_programs(1) - 1)
    def _():
        dk_ref[0] = jnp.transpose(dk[...])
        dv_ref[0] = jnp.transpose(dv[...])


def cross_forward_kernel(q_ref, k_ref, v_ref, mask_ref, o_ref):
    scores = dot(upright(k_ref[0]), q_ref[0], 1, 0) + mask_ref[...]
    weights = jnp.exp(scores - jnp.max(scores, axis=0, keepdims=True))
    total = jnp.sum(weights, axis=0, keepdims=True)
    o_ref[0] = dot(v_ref[0], weights.astype(BF), 1, 0) / total


def cross_backward_kernel(
    q_ref, g_ref, k_ref, v_ref, mask_ref, gate_ref, dq_ref, dk_ref, dv_ref, dg_ref
):
    q, g, gate = q_ref[0], g_ref[0], gate_ref[0, 0:1, 0:1]
    scores = dot(upright(k_ref[0]), q, 1, 0) + mask_ref[...]
    weights = jnp.exp(scores - jnp.max(scores, axis=0, keepdims=True))
    probs = weights / jnp.sum(weights, axis=0, keepdims=True)
    dp = dot(upright(v_ref[0]), g, 1, 0)
    inner = jnp.sum(probs * dp, axis=0, keepdims=True)
    ds = (probs * (gate * (dp - inner))).astype(BF)
    dg_ref[0] = inner
    dq_ref[0] = dot(k_ref[0], ds, 1, 0)
    dk = dot(q, ds, 1, 1)
    dv = dot(g, probs.astype(BF), 1, 1) * gate

    @pl.when(pl.program_id(1) == 0)
    def _():
        dk_ref[0] = dk
        dv_ref[0] = dv

    @pl.when(pl.program_id(1) > 0)
    def _():
        dk_ref[0] += dk
        dv_ref[0] += dv


def by_query(rows, block):
    return pl.BlockSpec((1, rows, block), lambda h, i: (h, 0, i))


def whole_head(rows, columns):
    return pl.BlockSpec((1, rows, columns), lambda h, i: (h, 0, 0))


def mask_spec(rows):
    return pl.BlockSpec((rows, 1), lambda h, i: (0, 0))


def f32(*shape):
    return jax.ShapeDtypeStruct(shape, F32)


def query_block(rows, keys, most):
    block = rows
    while block > 128 and block * keys > most:
        block //= 2
    return block


def self_forward(q, k, v):
    heads, dim, rows = q.shape
    keys = k.shape[2]
    block = query_block(rows, keys, 1 << 21)
    return pl.pallas_call(
        self_forward_kernel,
        grid=(heads, rows // block),
        in_specs=[by_query(dim, block), whole_head(dim, keys), whole_head(dim, keys)],
        out_specs=[by_query(dim, block), by_query(1, block)],
        out_shape=[f32(heads, dim, rows), f32(heads, 1, rows)],
        scratch_shapes=[pltpu.VMEM((keys, dim), BF)],
        compiler_params=KERNEL,
    )(q, k, v)


def self_backward(q, g, log_total, delta, k, v):
    heads, dim, rows = q.shape
    keys = k.shape[2]
    block = query_block(rows, keys, 1 << 20)
    held = [pltpu.VMEM((keys, dim), t) for t in (BF, BF, F32, F32)]
    return pl.pallas_call(
        self_backward_kernel,
        grid=(heads, rows // block),
        in_specs=[by_query(dim, block)] * 2
        + [by_query(1, block)] * 2
        + [whole_head(dim, keys)] * 2,
        out_specs=[by_query(dim, block), whole_head(dim, keys), whole_head(dim, keys)],
        out_shape=[f32(heads, dim, rows), f32(heads, dim, keys), f32(heads, dim, keys)],
        scratch_shapes=held,
        compiler_params=KERNEL,
    )(q, g, log_total, delta, k, v)


def cross_forward(q, k, v, mask):
    heads, dim, rows = q.shape
    keys = k.shape[2]
    block = query_block(rows, keys, 1 << 19)
    return pl.pallas_call(
        cross_forward_kernel,
        grid=(heads, rows // block),
        in_specs=[
            by_query(dim, block),
            whole_head(dim, keys),
            whole_head(dim, keys),
            mask_spec(keys),
        ],
        out_specs=by_query(dim, block),
        out_shape=f32(heads, dim, rows),
        compiler_params=KERNEL,
    )(q, k, v, mask)


def cross_backward(q, g, k, v, mask, gate):
    heads, dim, rows = q.shape
    keys = k.shape[2]
    block = query_block(rows, keys, 1 << 19)
    return pl.pallas_call(
        cross_backward_kernel,
        grid=(heads, rows // block),
        in_specs=[
            by_query(dim, block),
            by_query(dim, block),
            whole_head(dim, keys),
            whole_head(dim, keys),
            mask_spec(keys),
            whole_head(8, 128),
        ],
        out_specs=[
            by_query(dim, block),
            whole_head(dim, keys),
            whole_head(dim, keys),
            by_query(1, block),
        ],
        out_shape=[
            f32(heads, dim, rows),
            f32(heads, dim, keys),
            f32(heads, dim, keys),
            f32(heads, 1, rows),
        ],
        compiler_params=KERNEL,
    )(q, g, k, v, mask, gate)


def gather_parts(first, second):
    first = jnp.stack([first, swap(first, "ty")])
    second = jnp.stack([second, swap(second, "tz")])
    first = jnp.stack([first, swap(first, "tz")])
    second = jnp.stack([second, swap(second, "ty")], axis=1)
    return jnp.stack([first, second])


def gather_rows(block):
    half = block.shape[0] // 2
    both = gather_parts(block[:half], block[half:])
    return jnp.stack([both, swap(both, "tc")]).reshape(-1, block.shape[1])


def scatter_rows(make, count):
    other = swap(make(1).astype(BF), "tc")
    mine = make(0) + other.astype(F32)
    first, second = mine[: count // 4], mine[count // 4 :]
    rows = count // 16
    second = second.reshape(2, 2, rows, -1)
    a, b = swap(first[2 * rows :].astype(BF), "tz"), swap(second[:, 1].astype(BF), "ty")
    first, second = first[: 2 * rows] + a.astype(F32), second[:, 0] + b.astype(F32)
    a, b = swap(first[rows:].astype(BF), "ty"), swap(second[1].astype(BF), "tz")
    return join([first[:rows] + a.astype(F32), second[0] + b.astype(F32)])


def team_row_sum(values):
    tiled = values.reshape(values.shape[0], 2, 2, 2, 2, -1)
    for axis, dim in (("tc", 1), ("ty", 4), ("tz", 3)):
        tiled = tiled + jnp.flip(swap(tiled, axis), dim)
    return tiled.reshape(values.shape)


def flip_by(tiled, bits):
    for dim, bit in enumerate(bits):
        tiled = jnp.where(bit == 1, jnp.flip(tiled, dim), tiled)
    return tiled


def to_ranks(columns, bits):
    width = columns.shape[0]
    tiled = columns.reshape(width, 2, 2, 2, 2, -1)
    tiled = flip_by(jnp.transpose(tiled, (3, 4, 1, 0, 2, 5)), bits)
    return tiled.reshape(8, width, -1)


def from_ranks(blocks, bits):
    width = blocks.shape[1]
    tiled = flip_by(blocks.reshape(2, 2, 2, width, 2, -1), bits)
    return jnp.transpose(tiled, (3, 2, 4, 0, 1, 5)).reshape(width, -1)


def row_factor(values):
    return lax.rsqrt(jnp.mean(values * values, axis=-1, keepdims=True) + EPSILON)


def rms_back(grad, gain, normed, factor, row_mean):
    return factor * (grad * gain - normed * row_mean)


def rope_tables(places, head_dim):
    pair_count = head_dim // 2
    lead_pairs = pair_count // 4
    mid_pairs = (pair_count - lead_pairs) // 2
    last_pairs = pair_count - lead_pairs - mid_pairs
    angles = []
    for which, extent in enumerate((lead_pairs, mid_pairs, last_pairs)):
        offsets = jnp.arange(extent, dtype=F32)
        angles.append(jnp.power(10000.0, -offsets / extent)[:, None] * places[which][None])
    angles = join(angles)
    cosine, sine = jnp.cos(angles), jnp.sin(angles)
    return join([cosine, cosine]), join([-sine, sine])


def turn(vectors, cosine, sine):
    half = vectors.shape[1] // 2
    crossed = join([vectors[:, half:], vectors[:, :half]], axis=1)
    return vectors * cosine + crossed * sine


def on_device(
    tokens,
    condition,
    caption,
    caption_lengths,
    positions,
    modulation_weight,
    modulation_bias,
    norm_gains,
    cross_gate,
    input_weight,
    output_weight,
    caption_key_weight,
    caption_value_weight,
    gate_weight,
    up_weight,
    down_weight,
    cotangent,
):
    clips_here, clip_rows, width = tokens.shape
    head_count = cross_gate.shape[0]
    head_dim = width // head_count
    scale = head_dim ** (-0.5)
    team = 8
    heads = head_count // team
    part = heads * head_dim
    groups = lax.axis_size(GROUPS)
    reps = lax.axis_size("rep")
    half = lax.axis_index("half")
    bits = tuple(lax.axis_index(axis) for axis in TEAM)
    rank = bits[0] * 4 + bits[1] * 2 + bits[2]
    clip_pair = lax.axis_index("clip")
    device = lax.axis_index(EVERY)

    def pick(block, index, dim=0, keep=False):
        return lax.dynamic_index_in_dim(block, index, dim, keepdims=keep)

    def own_clip(block):
        return pick(block, half), swap(pick(block, 1 - half), "half")

    def back_clip(block):
        rows = block.shape[0] // 2
        kept, other = block[:rows], block[rows:]
        other = swap(other.astype(BF), "half").astype(block.dtype)
        return jnp.where(half == 0, jnp.stack([kept, other]), jnp.stack([other, kept]))

    def own_columns(table):
        return lax.dynamic_slice_in_dim(table, rank * part, part, table.ndim - 1)

    places = jnp.pad(
        jnp.transpose(positions, (1, 0, 2)).astype(BF),
        ((0, 0), (0, 5), (0, width - clip_rows)),
    )
    kept, received = own_clip(join([tokens, places], axis=1))

    def chip_square(block):
        block = jnp.stack([block, swap(block, "tz")])
        return jnp.stack([block, swap(block, "ty")], axis=1)

    pieces = [chip_square(kept), chip_square(received)]
    pieces = pieces + [swap(piece, "tc") for piece in pieces]
    tokens_all = join([piece[:, :, :clip_rows].reshape(-1, width) for piece in pieces])
    all_places = join(
        [
            jnp.transpose(piece[:, :, clip_rows : clip_rows + 3, :clip_rows], (2, 0, 1, 3)).reshape(
                3, -1
            )
            for piece in pieces
        ],
        axis=1,
    ).astype(F32)
    token_vals = join([kept[:clip_rows], received[:clip_rows]]).astype(F32)
    rows_here = token_vals.shape[0]
    team_rows = team * rows_here

    shard_rows = modulation_weight.shape[0]
    silu_all = jax.nn.silu(condition).astype(BF)
    silu_rows = lax.dynamic_slice_in_dim(silu_all, device * shard_rows, shard_rows, 1)
    mod_part = dot(silu_rows, modulation_weight, 1, 0)
    mod_part = mod_part.reshape(lax.axis_size("clip"), clips_here, -1)
    mod_pair = pick(mod_part, clip_pair) + swap(pick(mod_part, 1 - clip_pair), "clip")
    mod_own = pick(mod_pair, half, keep=True) + swap(pick(mod_pair, 1 - half, keep=True), "half")
    if reps > 1:
        mod_own = lax.psum(mod_own, "rep")
    for axis in TEAM:
        mod_own = mod_own + swap(mod_own, axis)
    modulation = mod_own + modulation_bias
    shift_attn, scale_attn, gate_attn, shift_ffn, scale_ffn, gate_ffn = (
        modulation[:, i * width : (i + 1) * width] for i in range(6)
    )

    def team_slice(shard):
        by_rank = jnp.transpose(shard, (1, 0, 2))
        mine = lax.all_to_all(by_rank, TEAM, split_axis=0, concat_axis=0, tiled=True)
        mine = mine.reshape(-1, shard.shape[2])
        return lax.all_gather(mine, GROUPS, axis=0, tiled=True)

    rows_in = input_weight.shape[0]
    w_in = team_slice(
        jnp.transpose(input_weight.reshape(rows_in, 3, team, part), (0, 2, 1, 3)).reshape(
            rows_in, team, 3 * part
        )
    )
    later = after(
        (caption_key_weight, caption_value_weight, output_weight, gate_weight, up_weight), mod_own
    )
    caption_key_weight, caption_value_weight, output_weight, gate_weight, up_weight = later
    rows_cap = caption_key_weight.shape[0]
    w_cap = team_slice(
        join(
            [
                caption_key_weight.reshape(rows_cap, team, part),
                caption_value_weight.reshape(rows_cap, team, part),
            ],
            axis=2,
        )
    )

    def both_sides(block, axis, bit, dim):
        other = swap(block, axis)
        return jnp.where(
            bit == 0, jnp.stack([block, other], dim), jnp.stack([other, block], dim)
        )

    out_rows = output_weight.shape[0]
    w_out = both_sides(both_sides(output_weight, "half", half, 0), "clip", clip_pair, 0)
    if reps > 1:
        w_out = lax.all_gather(w_out, "rep", axis=2)
    else:
        w_out = w_out[:, :, None]
    for place, axis in enumerate(TEAM):
        w_out = both_sides(w_out, axis, bits[place], 3 + place)
    w_out = w_out.reshape(-1, width)
    ff_block = down_weight.shape[0]

    def ff_columns(weight):
        rows = weight.shape[0]
        tiled = weight.reshape(rows, groups, team, ff_block)
        return jnp.transpose(tiled, (0, 2, 1, 3)).reshape(rows, team, groups * ff_block)

    w_gate_up = team_slice(join([ff_columns(gate_weight), ff_columns(up_weight)], axis=2))
    w_down = lax.all_gather(after(down_weight, w_cap), GROUPS, axis=0, tiled=True)
    ff_part = groups * ff_block

    def by_head(block):
        return block.reshape(heads, head_dim, block.shape[-1])

    tokens_f = tokens_all.astype(F32)
    factor_all = row_factor(tokens_f)
    attn_all = (
        tokens_f * factor_all * (norm_gains[0] * (1.0 + scale_attn)) + shift_attn
    ).astype(BF)
    cosine, sine = rope_tables(all_places, head_dim)
    raw_qk = dot(w_in[:, : 2 * part], attn_all, 0, 1).reshape(2, heads, head_dim, team_rows)
    squares = jnp.sum(raw_qk * raw_qk, axis=(1, 2))
    factors = lax.rsqrt(team_row_sum(squares) / width + EPSILON)[:, None, None]
    values = by_head(dot(w_in[:, 2 * part :], attn_all, 0, 1).astype(BF))
    gains = jnp.stack([own_columns(norm_gains[i]) for i in (1, 2, 3)])
    gains = gains.reshape(3, heads, head_dim, 1)
    normed_qk = raw_qk * factors
    turned = normed_qk * gains[:2]
    queries = (turn(turned[0], cosine, sine) * scale).astype(BF)
    keys = turn(turned[1], cosine, sine).astype(BF)

    slots_here = caption.shape[1]
    cap_all = gather_rows(join(own_clip(after(caption, tokens_all))))
    source = jnp.arange(2, dtype=jnp.int32)

    def along(dim):
        return source.reshape([2 if i == dim else 1 for i in range(5)])

    from_rank = rank ^ (along(2) * 4 + along(3) * 2 + along(0))
    holder = (half ^ along(1)) * reps + lax.axis_index("rep")
    slots = (holder * team + from_rank) * slots_here + jnp.arange(slots_here, dtype=jnp.int32)
    slots = slots.reshape(-1)
    craw = dot(w_cap, cap_all, 0, 1)
    craw_key = by_head(craw[:part])
    factor_c = lax.rsqrt(
        team_row_sum(jnp.sum(craw_key * craw_key, axis=(0, 1))[None]) / width + EPSILON
    )[None]
    normed_c = craw_key * factor_c
    ckeys = (normed_c * gains[2]).astype(BF)
    cvalues = by_head(craw[part:]).astype(BF)
    all_keys, all_values, all_ckeys, all_cvalues = keys, values, ckeys, cvalues
    if reps > 1:
        all_keys, all_values, all_ckeys, all_cvalues = (
            lax.all_gather(v, "rep", axis=2, tiled=True) for v in (keys, values, ckeys, cvalues)
        )
        step = lax.axis_index("rep")
        slots = join([slots + (r - step) * team * slots_here for r in range(reps)])
    mask = jnp.where(slots < pick(caption_lengths, half), 0.0, NEGATIVE).astype(F32)[:, None]

    o_self, log_total = self_forward(queries, all_keys, all_values)
    o_cross = cross_forward(queries, all_ckeys, all_cvalues, mask)
    tanh_gate = jnp.tanh(lax.dynamic_slice_in_dim(cross_gate, rank * heads, heads))
    tanh_wide = tanh_gate[:, None, None]
    mixed = (o_self + tanh_wide * o_cross).astype(BF).reshape(part, team_rows)
    mixed = lax.all_to_all(
        to_ranks(mixed, bits), TEAM, split_axis=0, concat_axis=0, tiled=True
    )
    combined = mixed.reshape(width, rows_here)

    branch = dot(combined, w_out, 0, 0)
    middle = token_vals + gate_attn * branch
    factor_f = row_factor(middle)
    core_f = middle * factor_f
    ffn_in = (core_f * norm_gains[4] * (1.0 + scale_ffn) + shift_ffn).astype(BF)
    ffn_all = gather_rows(ffn_in)
    grad_out = join(own_clip(after(cotangent, tokens_all))).astype(F32)
    d_ffn_all = gather_rows((gate_ffn * grad_out).astype(BF))
    w_gate, w_up = w_gate_up[:, :ff_part], w_gate_up[:, ff_part:]
    gate_vals = dot(ffn_all, w_gate, 1, 0)
    up_vals = dot(ffn_all, w_up, 1, 0)
    d_hidden = dot(d_ffn_all, w_down, 1, 1)
    sig = jax.nn.sigmoid(gate_vals)
    silu_gate = gate_vals * sig
    hidden = (silu_gate * up_vals).astype(BF)
    d_gate = (d_hidden * up_vals * (sig + silu_gate * (1.0 - sig))).astype(BF)
    d_up = (d_hidden * silu_gate).astype(BF)

    def side(block, which, dim=0):
        count = block.shape[dim] // 2
        return lax.slice_in_dim(block, which * count, (which + 1) * count, axis=dim)

    d_ffn_in = scatter_rows(
        lambda s: dot(side(d_gate, s), w_gate, 1, 1) + dot(side(d_up, s), w_up, 1, 1), team_rows
    )
    ffn_out = scatter_rows(
        lambda s: dot(side(after(hidden, d_ffn_in), s), w_down, 1, 0), team_rows
    )
    result = back_clip((middle + gate_ffn * ffn_out).astype(BF))
    d_gate_ffn = jnp.sum(grad_out * ffn_out, axis=0)
    grad_down = dot(hidden, d_ffn_all, 0, 0)
    grad_gate = dot(ffn_all, d_gate, 0, 0)
    grad_up = dot(ffn_all, d_up, 0, 0)

    def own_rows(slice_grad):
        summed = lax.psum_scatter(slice_grad.astype(BF), GROUPS, scatter_dimension=0, tiled=True)
        by_rank = summed.reshape(team, -1, summed.shape[-1])
        by_rank = lax.all_to_all(by_rank, TEAM, split_axis=0, concat_axis=0, tiled=True)
        return jnp.transpose(by_rank, (1, 0, 2)).astype(F32)

    sum_down = lax.psum_scatter(
        grad_down.astype(BF), GROUPS, scatter_dimension=0, tiled=True
    ).astype(F32)
    sum_gate_up = own_rows(join([grad_gate, grad_up], axis=1))

    def ff_rows(block):
        rows = block.shape[0]
        tiled = block.reshape(rows, team, groups, ff_block)
        return jnp.transpose(tiled, (0, 2, 1, 3)).reshape(rows, -1)

    sum_gate, sum_up = ff_rows(sum_gate_up[..., :ff_part]), ff_rows(sum_gate_up[..., ff_part:])

    d_shift_ffn = jnp.sum(d_ffn_in, axis=0)
    moment_f = jnp.sum(d_ffn_in * core_f, axis=0)
    d_scale_ffn = moment_f * norm_gains[4]
    d_gain_ffn = moment_f * (1.0 + scale_ffn[0])
    d_core = d_ffn_in * (norm_gains[4] * (1.0 + scale_ffn))
    d_middle = grad_out + factor_f * (
        d_core - core_f * jnp.mean(d_core * core_f, axis=-1, keepdims=True)
    )
    d_branch = (gate_attn * d_middle).astype(BF)
    d_gate_attn = jnp.sum(d_middle * branch, axis=0)
    d_combined = dot(w_out, d_branch, 1, 1).astype(BF)
    d_mixed = lax.all_to_all(
        d_combined.reshape(team, part, rows_here), TEAM, split_axis=0, concat_axis=0, tiled=True
    )
    d_self = by_head(from_ranks(d_mixed, bits))

    def kept_sum(block, axis, bit, dim):
        other = swap(pick(block, 1 - bit, dim).astype(BF), axis)
        return pick(block, bit, dim) + other.astype(F32)

    sum_output = dot(combined, d_branch, 1, 0).reshape(
        lax.axis_size("clip"), clips_here, reps, 2, 2, 2, out_rows, width
    )
    for place in (2, 1, 0):
        sum_output = kept_sum(sum_output, TEAM[place], bits[place], 3 + place)
    if reps > 1:
        sum_output = lax.psum_scatter(sum_output, "rep", scatter_dimension=2, tiled=True)
    sum_output = sum_output[:, :, 0]
    sum_output = kept_sum(sum_output, "clip", clip_pair, 0)
    sum_output = kept_sum(sum_output, "half", half, 0)

    gate_tile = jnp.broadcast_to(tanh_wide, (heads, 8, 128))
    dq_cross, d_ckeys, d_cvalues, gate_rows = cross_backward(
        queries, d_self, all_ckeys, all_cvalues, mask, gate_tile
    )
    d_cross_gate = jnp.sum(gate_rows, axis=(1, 2)) * (1.0 - tanh_gate * tanh_gate)
    if reps > 1:
        d_ckeys, d_cvalues = (
            lax.psum_scatter(v, "rep", scatter_dimension=2, tiled=True)
            for v in (d_ckeys, d_cvalues)
        )

    def team_mean(block):
        return jnp.sum(block, axis=(-3, -2))

    scaled_c = d_ckeys * gains[2]
    mean_c = team_row_sum(team_mean(scaled_c * normed_c)[None])[None] / width
    d_craw = factor_c * (scaled_c - normed_c * mean_c)
    d_gain_c = jnp.sum(d_ckeys * normed_c, axis=2).reshape(part)
    d_cap_low = join([d_craw, d_cvalues]).reshape(2 * part, -1).astype(BF)
    sum_cap = own_rows(dot(cap_all, d_cap_low, 0, 1))
    sum_ckey = sum_cap[..., :part].reshape(rows_cap, -1)
    sum_cvalue = sum_cap[..., part:].reshape(rows_cap, -1)
    d_caption = back_clip(
        scatter_rows(lambda s: dot(side(d_cap_low, s, 1), w_cap, 0, 1), cap_all.shape[0])
    )

    delta = jnp.sum(d_self.astype(F32) * o_self, axis=1, keepdims=True)
    dq_self, dk, dv = self_backward(queries, d_self, log_total, delta, all_keys, all_values)
    if reps > 1:
        dk, dv = (lax.psum_scatter(v, "rep", scatter_dimension=2, tiled=True) for v in (dk, dv))

    turned_grad = jnp.stack(
        [turn((dq_self + dq_cross) * scale, cosine, -sine), turn(dk, cosine, -sine)]
    )
    scaled_qk = turned_grad * gains[:2]
    mean_qk = team_row_sum(team_mean(scaled_qk * normed_qk))[:, None, None] / width
    d_gain_qk = jnp.sum(turned_grad * normed_qk, axis=3).reshape(2, part)
    d_qk = (factors * (scaled_qk - normed_qk * mean_qk)).reshape(2 * part, team_rows)
    d_projected = join([d_qk, dv.reshape(part, team_rows)]).astype(BF)
    sum_input = own_rows(dot(attn_all, d_projected, 0, 1))
    sum_input = jnp.transpose(sum_input.reshape(rows_in, team, 3, part), (0, 2, 1, 3)).reshape(
        rows_in, -1
    )
    sides = [dot(side(d_projected, s, 1), w_in, 0, 1) for s in (0, 1)]
    d_attn_in = scatter_rows(lambda s: sides[s], team_rows)

    d_shift_attn = sum(jnp.sum(block, axis=0) for block in sides)
    moment_a = sum(
        jnp.sum(sides[s] * (side(tokens_f, s) * side(factor_all, s)), axis=0) for s in (0, 1)
    )
    d_scale_attn = moment_a * norm_gains[0]
    d_gain_attn = moment_a * (1.0 + scale_attn[0])
    factor_a = row_factor(token_vals)
    core_a = token_vals * factor_a
    d_core = d_attn_in * (norm_gains[0] * (1.0 + scale_attn))
    d_tokens = back_clip(
        d_middle
        + factor_a * (d_core - core_a * jnp.mean(d_core * core_a, axis=-1, keepdims=True))
    )

    d_mod = join([d_shift_attn, d_scale_attn, d_gate_attn, d_shift_ffn, d_scale_ffn, d_gate_ffn])

    def placed(values, total, start):
        return lax.dynamic_update_slice_in_dim(jnp.zeros((total,), F32), values, start, 0)

    small = join(
        [d_gain_attn]
        + [placed(v, width, rank * part) for v in (d_gain_qk[0], d_gain_qk[1], d_gain_c)]
        + [d_gain_ffn, placed(d_cross_gate, 128, rank * heads)]
    )
    sums = join([d_mod, small])
    for axis in TEAM:
        sums = sums + swap(sums, axis)
    if reps > 1:
        sums = lax.psum(sums, "rep")
    mod_size = d_mod.shape[0]
    mod_low, small = sums[:mod_size].astype(BF)[None], sums[mod_size:]
    for axis, bit in (("half", half), ("clip", clip_pair)):
        other = swap(mod_low, axis)
        mod_low = jnp.where(bit == 0, join([mod_low, other]), join([other, mod_low]))
        small = small + swap(small, axis)
    gain_sum = small[: 5 * width].reshape(5, width)
    gate_sum = small[5 * width : 5 * width + head_count]
    d_bias = jnp.sum(mod_low.astype(F32), axis=0)
    grad_mod = dot(silu_rows, mod_low, 0, 0)
    d_silu = dot(mod_low, modulation_weight, 1, 1)
    d_silu = lax.dynamic_update_slice_in_dim(
        jnp.zeros(condition.shape, F32), d_silu, device * shard_rows, 1
    )
    if reps > 1:
        d_silu = lax.psum(d_silu, "rep")
    for axis in ("tc", "ty", "tz", "half", "clip"):
        d_silu = d_silu + swap(d_silu, axis)
    _, silu_back = jax.vjp(jax.nn.silu, condition)
    d_condition = silu_back(d_silu)[0]
    return (
        result,
        d_tokens,
        d_caption,
        d_condition,
        grad_mod,
        d_bias,
        gain_sum,
        gate_sum,
        sum_input,
        sum_output,
        sum_ckey,
        sum_cvalue,
        sum_gate,
        sum_up,
        sum_down,
    )


def solution(mesh):
    clip_count, seq_count = mesh.shape["clip"], mesh.shape["seq"]

    def program(*arrays):
        halves = arrays[0].shape[0] // clip_count
        shape = (clip_count, halves, seq_count // (halves * 8), 2, 2, 2)
        fine = Mesh(mesh.devices.reshape(shape), EVERY)
        rows = P("clip", SEQ, None)
        shard = P(EVERY, None)
        mapped = jax.shard_map(
            on_device,
            mesh=fine,
            in_specs=(
                rows,
                P(),
                rows,
                P("clip"),
                P(None, "clip", SEQ),
                shard,
                P(),
                P(),
                P(),
                shard,
                shard,
                shard,
                shard,
                shard,
                shard,
                shard,
                rows,
            ),
            out_specs=(rows, rows, rows, P(), shard, P(), P(), P()) + (shard,) * 7,
            check_vma=False,
        )
        return mapped(*arrays)

    return program
```

```python
import jax
import jax.numpy as jnp
from jax import lax
from jax.experimental import pallas as pl
from jax.experimental.pallas import tpu as pltpu
from jax.sharding import Mesh
from jax.sharding import PartitionSpec as P

EPSILON = 1e-06
NEGATIVE = -1e30
BF = jnp.bfloat16
F32 = jnp.float32
SEQ = ("half", "rep", "tz", "ty", "tc")
GROUPS = ("clip", "half", "rep")
TEAM = ("tc", "tz", "ty")
SHARDS = ("tz", "ty", "tc")
EVERY = ("clip",) + SEQ
KERNEL = pltpu.CompilerParams(
    vmem_limit_bytes=56 * 1024 * 1024, dimension_semantics=("arbitrary", "arbitrary")
)


def swap(block, axis):
    return lax.ppermute(block, axis, [(0, 1), (1, 0)])


def together(*values):
    return lax.optimization_barrier(values)


def after(value, *others):
    return lax.optimization_barrier((value,) + others)[0]


def dot(left, right, left_dim, right_dim):
    dims = (((left_dim,), (right_dim,)), ((), ()))
    return lax.dot_general(left, right, dims, preferred_element_type=F32)


def join(parts, axis=0):
    return jnp.concatenate(parts, axis=axis)


def upright(block):
    return jnp.transpose(block.astype(F32)).astype(BF)


def self_forward_kernel(q_ref, k_ref, v_ref, o_ref, log_ref, k_rows):
    @pl.when(pl.program_id(1) == 0)
    def _():
        k_rows[...] = upright(k_ref[0])

    scores = dot(k_rows[...], q_ref[0], 1, 0)
    peak = jnp.max(scores, axis=0, keepdims=True)
    weights = jnp.exp(scores - peak)
    total = jnp.sum(weights, axis=0, keepdims=True)
    o_ref[0] = dot(v_ref[0], weights.astype(BF), 1, 0) / total
    log_ref[0] = peak + jnp.log(total)


def self_backward_kernel(
    q_ref, g_ref, log_ref, delta_ref, k_ref, v_ref, dq_ref, dk_ref, dv_ref, k_rows, v_rows, dk, dv
):
    step = pl.program_id(1)

    @pl.when(step == 0)
    def _():
        k_rows[...] = upright(k_ref[0])
        v_rows[...] = upright(v_ref[0])
        dk[...] = jnp.zeros_like(dk)
        dv[...] = jnp.zeros_like(dv)

    q, g = q_ref[0], g_ref[0]
    probs = jnp.exp(dot(k_rows[...], q, 1, 0) - log_ref[0])
    ds = (probs * (dot(v_rows[...], g, 1, 0) - delta_ref[0])).astype(BF)
    dv[...] += dot(probs.astype(BF), g, 1, 1)
    dk[...] += dot(ds, q, 1, 1)
    dq_ref[0] = dot(k_ref[0], ds, 1, 0)

    @pl.when(step == pl.num_programs(1) - 1)
    def _():
        dk_ref[0] = jnp.transpose(dk[...])
        dv_ref[0] = jnp.transpose(dv[...])


def cross_forward_kernel(q_ref, k_ref, v_ref, mask_ref, o_ref):
    scores = dot(upright(k_ref[0]), q_ref[0], 1, 0) + mask_ref[...]
    weights = jnp.exp(scores - jnp.max(scores, axis=0, keepdims=True))
    total = jnp.sum(weights, axis=0, keepdims=True)
    o_ref[0] = dot(v_ref[0], weights.astype(BF), 1, 0) / total


def cross_backward_kernel(
    q_ref, g_ref, k_ref, v_ref, mask_ref, gate_ref, dq_ref, dk_ref, dv_ref, dg_ref
):
    q, g, gate = q_ref[0], g_ref[0], gate_ref[0, 0:1, 0:1]
    scores = dot(upright(k_ref[0]), q, 1, 0) + mask_ref[...]
    weights = jnp.exp(scores - jnp.max(scores, axis=0, keepdims=True))
    probs = weights / jnp.sum(weights, axis=0, keepdims=True)
    dp = dot(upright(v_ref[0]), g, 1, 0)
    inner = jnp.sum(probs * dp, axis=0, keepdims=True)
    ds = (probs * (gate * (dp - inner))).astype(BF)
    dg_ref[0] = inner
    dq_ref[0] = dot(k_ref[0], ds, 1, 0)
    dk = dot(q, ds, 1, 1)
    dv = dot(g, probs.astype(BF), 1, 1) * gate

    @pl.when(pl.program_id(1) == 0)
    def _():
        dk_ref[0] = dk
        dv_ref[0] = dv

    @pl.when(pl.program_id(1) > 0)
    def _():
        dk_ref[0] += dk
        dv_ref[0] += dv


def place_weight_kernel(bit_ref, mine_ref, other_ref, scale_ref, shift_ref, w_ref, scaled_ref, bias_ref):
    step = pl.program_id(0)

    def run(ref):
        values = ref[...].astype(F32)
        w_ref[...] = ref[...]
        scaled_ref[...] = (values * scale_ref[...]).astype(BF)
        bias = jnp.sum(values * shift_ref[...], axis=0, keepdims=True)

        @pl.when(step == 0)
        def _():
            bias_ref[...] = bias

        @pl.when(step > 0)
        def _():
            bias_ref[...] += bias

    @pl.when(step == bit_ref[0])
    def _():
        run(mine_ref)

    @pl.when(step != bit_ref[0])
    def _():
        run(other_ref)


def place_weight(bit, mine, other, scale, shift):
    rows, columns = mine.shape
    part = pl.BlockSpec((rows, columns), lambda i: (0, 0))
    out = pl.BlockSpec((rows, columns), lambda i: (i, 0))
    column = pl.BlockSpec((rows, 1), lambda i: (i, 0))
    return pl.pallas_call(
        place_weight_kernel,
        grid=(2,),
        in_specs=[pl.BlockSpec(memory_space=pltpu.SMEM), part, part, column, column],
        out_specs=[out, out, pl.BlockSpec((1, columns), lambda i: (0, 0))],
        out_shape=[
            jax.ShapeDtypeStruct((2 * rows, columns), BF),
            jax.ShapeDtypeStruct((2 * rows, columns), BF),
            f32(1, columns),
        ],
        compiler_params=pltpu.CompilerParams(vmem_limit_bytes=48 * 1024 * 1024),
    )(jnp.reshape(bit, (1,)).astype(jnp.int32), mine, other, scale, shift)


def norm_rows_kernel(rows_ref, core_ref, places_ref):
    rows = core_ref.shape[0] // 2
    for part in (0, 1):
        start = part * (rows + 8)
        values = rows_ref[start : start + rows].astype(F32)
        square = jnp.mean(values * values, axis=-1, keepdims=True)
        core_ref[part * rows : (part + 1) * rows] = (values * lax.rsqrt(square + EPSILON)).astype(BF)
        places_ref[0, part] = rows_ref[start + rows : start + rows + 8, :rows].astype(F32)


def norm_rows(blocks, rows):
    width = blocks.shape[1]
    pair = 2 * (rows + 8)
    count = blocks.shape[0] // pair
    return pl.pallas_call(
        norm_rows_kernel,
        grid=(count,),
        in_specs=[pl.BlockSpec((pair, width), lambda i: (i, 0))],
        out_specs=[
            pl.BlockSpec((2 * rows, width), lambda i: (i, 0)),
            pl.BlockSpec((1, 2, 8, rows), lambda i: (i, 0, 0, 0)),
        ],
        out_shape=[
            jax.ShapeDtypeStruct((2 * count * rows, width), BF),
            f32(count, 2, 8, rows),
        ],
        compiler_params=pltpu.CompilerParams(vmem_limit_bytes=32 * 1024 * 1024),
    )(blocks)


def by_query(rows, block, first=0):
    return pl.BlockSpec((1, rows, block), lambda h, i: (h + first, 0, i))


def whole_head(rows, columns, first=0):
    return pl.BlockSpec((1, rows, columns), lambda h, i: (h + first, 0, 0))


def mask_spec(rows):
    return pl.BlockSpec((rows, 1), lambda h, i: (0, 0))


def f32(*shape):
    return jax.ShapeDtypeStruct(shape, F32)


def query_block(rows, keys, most):
    block = rows
    while block > 128 and block * keys > most:
        block //= 2
    return block


def attention_cost(scores, products, heads=1):
    return pl.CostEstimate(
        flops=heads * scores * products * 2 * 256,
        transcendentals=heads * scores,
        bytes_accessed=heads * scores // 2,
    )


def one_head(kernel, head, kept, inputs, in_specs, out_specs, out_shape, scratch, steps, cost):
    extra = len(kept) if kept else 0

    def body(*refs):
        kernel(*refs[: len(inputs)], *refs[len(inputs) + extra :])

    return pl.pallas_call(
        body,
        grid=(1, steps),
        in_specs=in_specs + [pl.BlockSpec(memory_space=pl.ANY)] * extra,
        out_specs=out_specs,
        out_shape=out_shape,
        scratch_shapes=scratch,
        input_output_aliases={len(inputs) + i: i for i in range(extra)},
        compiler_params=KERNEL,
        cost_estimate=cost,
    )(*inputs, *(kept or ()))


def self_forward(q, k, v, head, kept):
    heads, dim, rows = q.shape
    keys = k.shape[2]
    block = query_block(rows, keys, 1 << 21)
    return one_head(
        self_forward_kernel,
        head,
        kept,
        (q, k, v),
        [by_query(dim, block, head), whole_head(dim, keys, head), whole_head(dim, keys, head)],
        [by_query(dim, block, head), by_query(1, block, head)],
        [f32(heads, dim, rows), f32(heads, 1, rows)],
        [pltpu.VMEM((keys, dim), BF)],
        rows // block,
        attention_cost(rows * keys, 2),
    )


def self_backward(q, g, log_total, delta, k, v, head, kept):
    heads, dim, rows = q.shape
    keys = k.shape[2]
    block = query_block(rows, keys, 1 << 20)
    return one_head(
        self_backward_kernel,
        head,
        kept,
        (q, g, log_total, delta, k, v),
        [by_query(dim, block, head)] * 2
        + [by_query(1, block, head)] * 2
        + [whole_head(dim, keys, head)] * 2,
        [by_query(dim, block, head), whole_head(dim, keys, head), whole_head(dim, keys, head)],
        [f32(heads, dim, rows), f32(heads, dim, keys), f32(heads, dim, keys)],
        [pltpu.VMEM((keys, dim), t) for t in (BF, BF, F32, F32)],
        rows // block,
        attention_cost(rows * keys, 5),
    )


def cross_forward(q, k, v, mask):
    heads, dim, rows = q.shape
    keys = k.shape[2]
    block = query_block(rows, keys, 1 << 19)
    return pl.pallas_call(
        cross_forward_kernel,
        grid=(heads, rows // block),
        in_specs=[
            by_query(dim, block),
            whole_head(dim, keys),
            whole_head(dim, keys),
            mask_spec(keys),
        ],
        out_specs=by_query(dim, block),
        out_shape=f32(heads, dim, rows),
        compiler_params=KERNEL,
        cost_estimate=attention_cost(rows * keys, 2, heads),
    )(q, k, v, mask)


def cross_backward(q, g, k, v, mask, gate):
    heads, dim, rows = q.shape
    keys = k.shape[2]
    block = query_block(rows, keys, 1 << 19)
    return pl.pallas_call(
        cross_backward_kernel,
        grid=(heads, rows // block),
        in_specs=[
            by_query(dim, block),
            by_query(dim, block),
            whole_head(dim, keys),
            whole_head(dim, keys),
            mask_spec(keys),
            whole_head(8, 128),
        ],
        out_specs=[
            by_query(dim, block),
            whole_head(dim, keys),
            whole_head(dim, keys),
            by_query(1, block),
        ],
        out_shape=[
            f32(heads, dim, rows),
            f32(heads, dim, keys),
            f32(heads, dim, keys),
            f32(heads, 1, rows),
        ],
        compiler_params=KERNEL,
        cost_estimate=attention_cost(rows * keys, 5, heads),
    )(q, g, k, v, mask, gate)


def halves(block):
    half = block.shape[0] // 2
    return block[:half], block[half:]


def pick(block, index, dim=0, keep=False):
    return lax.dynamic_index_in_dim(block, index, dim, keepdims=keep)


def both_sides(block, axis, bit, dim):
    other = swap(block, axis)
    return jnp.where(bit == 0, jnp.stack([block, other], dim), jnp.stack([other, block], dim))


def kept_sum(block, axis, bit, dim):
    other = swap(pick(block, 1 - bit, dim).astype(BF), axis)
    return pick(block, bit, dim).astype(F32) + other.astype(F32)


def team_sum(values):
    for axis in TEAM:
        values = values + swap(values, axis)
    return values


def chips_first(first, second, bits):
    return kept_sum(first, "tz", bits[0], 0), kept_sum(second, "ty", bits[1], 1)


def chips_last(first, second, bits):
    return kept_sum(first, "ty", bits[1], 0), kept_sum(second, "tz", bits[0], 0)


def row_factor(values):
    return lax.rsqrt(jnp.mean(values * values, axis=-1, keepdims=True) + EPSILON)


def rope_tables(places, head_dim):
    pair_count = head_dim // 2
    lead_pairs = pair_count // 4
    mid_pairs = (pair_count - lead_pairs) // 2
    last_pairs = pair_count - lead_pairs - mid_pairs
    angles = []
    for which, extent in enumerate((lead_pairs, mid_pairs, last_pairs)):
        offsets = jnp.arange(extent, dtype=F32)
        angles.append(jnp.power(10000.0, -offsets / extent)[:, None] * places[which][None])
    angles = join(angles)
    cosine, sine = jnp.cos(angles), jnp.sin(angles)
    return join([cosine, cosine]), join([-sine, sine])


def turn(vectors, cosine, sine):
    half = vectors.shape[1] // 2
    crossed = join([vectors[:, half:], vectors[:, :half]], axis=1)
    return vectors * cosine + crossed * sine


def on_device(
    tokens,
    condition,
    caption,
    caption_lengths,
    positions,
    modulation_weight,
    modulation_bias,
    norm_gains,
    cross_gate,
    input_weight,
    output_weight,
    caption_key_weight,
    caption_value_weight,
    gate_weight,
    up_weight,
    down_weight,
    cotangent,
):
    clips_here, clip_rows, width = tokens.shape
    head_count = cross_gate.shape[0]
    head_dim = width // head_count
    scale = head_dim ** (-0.5)
    team = 8
    heads = head_count // team
    rows_in = input_weight.shape[0]
    part = heads * head_dim
    groups = lax.axis_size(GROUPS)
    reps = lax.axis_size("rep")
    half = lax.axis_index("half")
    bits = tuple(lax.axis_index(axis) for axis in SHARDS)
    rank = lax.axis_index(TEAM)
    clip_pair = lax.axis_index("clip")
    device = lax.axis_index(EVERY)

    def own_clip(block):
        return pick(block, half), swap(pick(block, 1 - half), "half")

    def back_clip(block):
        rows = block.shape[0] // 2
        kept, other = block[:rows], block[rows:]
        other = swap(other.astype(BF), "half").astype(block.dtype)
        return jnp.where(half == 0, jnp.stack([kept, other]), jnp.stack([other, kept]))

    def own_columns(table):
        return lax.dynamic_slice_in_dim(table, rank * part, part, table.ndim - 1)

    def by_rank(weight, split, by_shard=False):
        rows = weight.shape[0]
        if by_shard:
            tiled = weight.reshape(rows, split, team, -1)
            return jnp.transpose(tiled, (2, 0, 1, 3)).reshape(team, rows, -1)
        tiled = weight.reshape(rows, split, 2, 2, 2, -1)
        return jnp.transpose(tiled, (3, 4, 2, 0, 1, 5)).reshape(team, rows, -1)

    def from_team(blocks):
        mine = lax.all_to_all(blocks, SHARDS, split_axis=0, concat_axis=0, tiled=True)
        return mine.reshape(-1, blocks.shape[2])

    def all_reps(block):
        return lax.all_gather(block, "rep", axis=0, tiled=True) if reps > 1 else block

    def across_half(block):
        return both_sides(all_reps(block), "half", half, 0)

    def across_clip(block):
        return both_sides(block, "clip", clip_pair, 0).reshape(-1, block.shape[-1])

    places = jnp.pad(
        jnp.transpose(positions, (1, 0, 2)).astype(BF),
        ((0, 0), (0, 5), (0, width - clip_rows)),
    )
    rows_a, rows_b = own_clip(join([tokens, places], axis=1))
    in_team = from_team(by_rank(input_weight, 3))
    shard_rows = modulation_weight.shape[0]
    silu_all = jax.nn.silu(condition).astype(BF)
    silu_rows = lax.dynamic_slice_in_dim(silu_all, device * shard_rows, shard_rows, 1)
    mod_part = dot(silu_rows, modulation_weight, 1, 0)
    mod_part = mod_part.reshape(lax.axis_size("clip"), clips_here, -1)
    mod_pair = pick(mod_part, clip_pair) + swap(pick(mod_part, 1 - clip_pair), "clip")
    mod_own = pick(mod_pair, half, keep=True) + swap(pick(mod_pair, 1 - half, keep=True), "half")
    rows_a, rows_b, mod_own, in_team = together(rows_a, rows_b, mod_own, in_team)

    rows_all = lax.all_gather(join([rows_a, rows_b]), TEAM, axis=0, tiled=True)
    in_half = across_half(in_team).reshape(-1, 3 * part)
    if reps > 1:
        mod_own = lax.psum(mod_own, "rep")
    mod_own = team_sum(mod_own)
    in_half, mod_own, caption = together(in_half, mod_own, caption)

    in_other = swap(in_half, "clip")
    rows_cap = caption_key_weight.shape[0]
    slots_here = caption.shape[1]
    cap_a, cap_b = own_clip(caption)
    modulation = mod_own + modulation_bias
    shift_attn, scale_attn, gate_attn, shift_ffn, scale_ffn, gate_ffn = (
        modulation[:, i * width : (i + 1) * width] for i in range(6)
    )
    token_vals = join([rows_a[:clip_rows], rows_b[:clip_rows]]).astype(F32)
    rows_here = token_vals.shape[0]
    team_rows = team * rows_here
    row_scale = (norm_gains[0] * (1.0 + scale_attn)).reshape(width, 1)
    row_shift = shift_attn.reshape(width, 1)
    w_in, w_scaled, bias = place_weight(clip_pair, in_half, in_other, row_scale, row_shift)
    bias = bias.reshape(3 * part, 1)
    w_scaled, bias, rows_all, cap_a, cap_b, out_shard, ckey_weight, cvalue_weight = together(
        w_scaled,
        bias,
        rows_all,
        cap_a,
        cap_b,
        output_weight,
        caption_key_weight,
        caption_value_weight,
    )
    cap_team = from_team(join([by_rank(ckey_weight, 1), by_rank(cvalue_weight, 1)], axis=2))
    w_out = both_sides(out_shard, "half", half, 0)
    cap_rows = jnp.where(half == 0, join([cap_a, cap_b]), join([cap_b, cap_a]))
    core_all, all_places = norm_rows(rows_all, clip_rows)
    all_places = jnp.transpose(all_places[:, :, :3], (2, 0, 1, 3)).reshape(3, team_rows)

    def by_head(block):
        return block.reshape(heads, head_dim, block.shape[-1])

    raw_qk = dot(w_scaled[:, : 2 * part], core_all, 0, 1) + bias[: 2 * part]
    raw_qk = raw_qk.reshape(2, heads, head_dim, team_rows)
    squares = jnp.sum(raw_qk * raw_qk, axis=(1, 2))
    squares, raw_qk, cap_team, cap_rows, cotangent, w_out = together(
        team_sum(squares), raw_qk, cap_team, cap_rows, cotangent, w_out
    )
    cap_half = across_half(cap_team)
    cap_all = lax.all_gather(cap_rows, TEAM, axis=0, tiled=True)
    cot_a, cot_b = own_clip(cotangent)
    w_out = both_sides(w_out, "clip", clip_pair, 0)
    w_out = lax.all_gather(w_out, "rep", axis=2) if reps > 1 else w_out[:, :, None]
    factors = lax.rsqrt(squares / width + EPSILON)[:, None, None]
    cosine, sine = rope_tables(all_places, head_dim)
    values = by_head((dot(w_scaled[:, 2 * part :], core_all, 0, 1) + bias[2 * part :]).astype(BF))
    gains = jnp.stack([own_columns(norm_gains[i]) for i in (1, 2, 3)])
    gains = gains.reshape(3, heads, head_dim, 1)
    normed_qk = raw_qk * factors
    turned = normed_qk * gains[:2]
    queries = (turn(turned[0], cosine, sine) * scale).astype(BF)
    keys = turn(turned[1], cosine, sine).astype(BF)
    all_keys, all_values = keys, values
    if reps > 1:
        all_keys, all_values = (lax.all_gather(v, "rep", axis=2, tiled=True) for v in (keys, values))

    queries, all_keys, all_values, gate_shard, up_shard, w_out = together(
        queries, all_keys, all_values, gate_weight, up_weight, w_out
    )
    w_out = both_sides(w_out, "tz", bits[0], 3)
    ff_block = down_weight.shape[0]
    ff_part = groups * ff_block
    up_team = from_team(
        join([by_rank(gate_shard, groups, True), by_rank(up_shard, groups, True)], axis=2)
    )
    o_self, logs = self_forward(queries, all_keys, all_values, 0, None)
    o_self, logs = self_forward(queries, all_keys, all_values, 1, (o_self, logs))
    o_self, logs, cap_half, cot_a, cot_b, up_team, w_out, cap_all = together(
        o_self, logs, cap_half, cot_a, cot_b, up_team, w_out, cap_all
    )
    w_cap = across_clip(cap_half)
    grad_out = join([cot_a, cot_b]).astype(F32)
    d_ffn = (gate_ffn * grad_out).astype(BF)
    d_ffn_all = lax.all_gather(d_ffn, TEAM, axis=0, tiled=True)
    up_half = across_half(up_team)
    w_out = both_sides(w_out, "ty", bits[1], 4)
    o_self, logs = self_forward(queries, all_keys, all_values, 2, (o_self, logs))
    o_self, w_cap, down_shard = together(o_self, w_cap, down_weight)
    craw = dot(w_cap, cap_all, 0, 1)
    craw_key = by_head(craw[:part])
    square_c = jnp.sum(craw_key * craw_key, axis=(0, 1))[None]
    square_c = team_sum(square_c)
    factor_c = lax.rsqrt(square_c / width + EPSILON)[None]
    normed_c = craw_key * factor_c
    ckeys = (normed_c * gains[2]).astype(BF)
    cvalues = by_head(craw[part:]).astype(BF)
    all_ckeys, all_cvalues = ckeys, cvalues
    step = lax.axis_index("rep")
    order = jnp.arange(team * clips_here * slots_here, dtype=jnp.int32)
    in_rank = order // slots_here % clips_here
    from_rank = order // (slots_here * clips_here)
    from_shard = from_rank % 4 * 2 + from_rank // 4
    slots = ((in_rank * reps + step) * team + from_shard) * slots_here + order % slots_here
    if reps > 1:
        all_ckeys, all_cvalues = (
            lax.all_gather(v, "rep", axis=2, tiled=True) for v in (ckeys, cvalues)
        )
        slots = join([slots + (r - step) * team * slots_here for r in range(reps)])
    mask = jnp.where(slots < pick(caption_lengths, half), 0.0, NEGATIVE).astype(F32)[:, None]
    o_cross = cross_forward(queries, all_ckeys, all_cvalues, mask)
    tanh_gate = jnp.tanh(lax.dynamic_slice_in_dim(cross_gate, rank * heads, heads))
    tanh_wide = tanh_gate[:, None, None]
    mixed = (o_self + tanh_wide * o_cross).astype(BF).reshape(part, team, rows_here)
    mixed, w_out, up_half, d_ffn_all = together(
        jnp.transpose(mixed, (1, 0, 2)), w_out, up_half, d_ffn_all
    )
    w_gate_up = lax.all_gather(up_half.reshape(-1, 2 * ff_part), "clip", axis=0, tiled=True)
    down_half = across_half(down_shard)
    w_out = both_sides(w_out, "tc", bits[2], 5)
    mixed = lax.all_to_all(mixed, TEAM, split_axis=0, concat_axis=0, tiled=True)
    mixed, w_out, down_half = together(mixed, w_out, down_half)
    combined = mixed.reshape(width, rows_here)
    w_out = w_out.reshape(-1, width)
    w_down = across_clip(down_half)

    branch = dot(combined, w_out, 0, 0)
    middle = token_vals + gate_attn * branch
    factor_f = row_factor(middle)
    core_f = middle * factor_f
    ffn_in = (core_f * norm_gains[4] * (1.0 + scale_ffn) + shift_ffn).astype(BF)
    ffn_all = lax.all_gather(after(ffn_in, w_gate_up), TEAM, axis=0, tiled=True)
    w_gate_up, w_down, ffn_all = together(w_gate_up, w_down, ffn_all)
    gate_up = dot(ffn_all, w_gate_up, 1, 0)
    gate_vals, up_vals = gate_up[:, :ff_part], gate_up[:, ff_part:]
    d_hidden = dot(d_ffn_all, w_down, 1, 1)
    sig = jax.nn.sigmoid(gate_vals)
    silu_gate = gate_vals * sig
    hidden = (silu_gate * up_vals).astype(BF)
    d_gate = (d_hidden * up_vals * (sig + silu_gate * (1.0 - sig))).astype(BF)
    d_up = (d_hidden * silu_gate).astype(BF)
    d_gate_up = join([d_gate, d_up], axis=1)

    def core_side(block, which, dim=0):
        count = block.shape[dim] // 2
        return lax.dynamic_slice_in_dim(block, which * count, count, dim)

    def ffn_side(which):
        return dot(core_side(d_gate_up, which), w_gate_up, 1, 1).astype(BF)

    def by_chip(mine):
        tiled = mine.reshape(2, 2, 2, clip_rows, width)
        return tiled[:, :, 0], tiled[:, :, 1]

    def add_core(kept, sent):
        return (kept.astype(F32) + swap(sent, "tc").astype(F32)).astype(BF)

    def team_parts(slice_grad):
        tiled = slice_grad.reshape(lax.axis_size("clip"), clips_here, -1, slice_grad.shape[-1])
        return kept_sum(tiled, "clip", clip_pair, 0).astype(BF)

    def half_parts(tiled):
        summed = kept_sum(tiled, "half", half, 0)
        if reps > 1:
            summed = lax.psum_scatter(summed, "rep", scatter_dimension=0, tiled=True)
        return summed

    def to_shards(summed):
        ranked = summed.astype(BF).reshape(team, -1, summed.shape[-1])
        return lax.all_to_all(ranked, SHARDS, split_axis=0, concat_axis=0, tiled=True)

    def head_columns(blocks, split):
        rows = blocks.shape[1]
        tiled = blocks.reshape(2, 2, 2, rows, split, part)
        return jnp.transpose(tiled, (3, 4, 2, 0, 1, 5)).reshape(rows, -1).astype(F32)

    def ff_columns(blocks):
        rows = blocks.shape[1]
        tiled = blocks.reshape(team, rows, groups, ff_block)
        return jnp.transpose(tiled, (1, 2, 0, 3)).reshape(rows, -1).astype(F32)

    def all_parts(slice_grad):
        return lax.psum_scatter(slice_grad, GROUPS, scatter_dimension=0, tiled=True)

    side_sent = ffn_side(1 - bits[2])
    mine = add_core(ffn_side(bits[2]), side_sent)
    pair = chips_first(*by_chip(mine), bits)
    grad_down = dot(after(hidden, mine), d_ffn_all, 0, 0).astype(BF)
    *pair, grad_down = together(*pair, grad_down)
    sum_down = all_parts(grad_down)
    d_ffn_in = join(chips_last(*pair, bits))
    late_hidden = after(hidden, grad_down)
    out_sent = dot(core_side(late_hidden, 1 - bits[2]), w_down, 1, 0).astype(BF)
    out_kept = dot(core_side(late_hidden, bits[2]), w_down, 1, 0).astype(BF)
    d_ffn_in, out_sent, out_kept = together(d_ffn_in, out_sent, out_kept)

    out_mine = add_core(out_kept, out_sent)
    d_shift_ffn = jnp.sum(d_ffn_in, axis=0, keepdims=True)
    moment_f = jnp.sum(d_ffn_in * core_f, axis=0, keepdims=True)
    d_scale_ffn = moment_f * norm_gains[4]
    d_gain_ffn = moment_f * (1.0 + scale_ffn)
    d_core = d_ffn_in * (norm_gains[4] * (1.0 + scale_ffn))
    d_middle = grad_out + factor_f * (
        d_core - core_f * jnp.mean(d_core * core_f, axis=-1, keepdims=True)
    )
    d_branch = (gate_attn * d_middle).astype(BF)
    d_gate_attn = jnp.sum(d_middle * branch, axis=0, keepdims=True)
    d_combined = dot(w_out, d_branch, 1, 1).astype(BF)
    d_mixed = lax.all_to_all(
        d_combined.reshape(team, part, rows_here), TEAM, split_axis=0, concat_axis=0, tiled=True
    )
    late_ffn, late_gate, out_mine = together(ffn_all, d_gate_up, out_mine, d_combined)[:3]
    grad_gate_up = dot(late_ffn, late_gate, 0, 0).astype(BF)
    d_mixed, grad_gate_up = together(d_mixed, grad_gate_up)
    up_rows = all_parts(grad_gate_up)
    d_self = by_head(jnp.transpose(d_mixed, (1, 0, 2)).reshape(part, team_rows))

    out_pair = chips_first(*by_chip(out_mine), bits)
    gate_tile = jnp.broadcast_to(tanh_wide, (heads, 8, 128))
    dq_cross, d_ckeys, d_cvalues, gate_rows = cross_backward(
        queries, d_self, all_ckeys, all_cvalues, mask, gate_tile
    )
    d_cross_gate = jnp.sum(gate_rows, axis=(1, 2)) * (1.0 - tanh_gate * tanh_gate)
    if reps > 1:
        d_ckeys, d_cvalues = (
            lax.psum_scatter(v, "rep", scatter_dimension=2, tiled=True)
            for v in (d_ckeys, d_cvalues)
        )

    def team_mean(block):
        return jnp.sum(block, axis=(-3, -2))

    scaled_c = d_ckeys * gains[2]
    mean_c = team_mean(scaled_c * normed_c)[None]
    mean_c = mean_c + swap(mean_c, "tc")
    grad_output = dot(after(combined, dq_cross), d_branch, 1, 0).astype(BF)
    delta = jnp.sum(d_self.astype(F32) * o_self, axis=1, keepdims=True)
    delta, grad_output, mean_c, *out_pair = together(delta, grad_output, mean_c, *out_pair)
    sum_output = lax.psum_scatter(
        after(grad_output, up_rows), EVERY, scatter_dimension=0, tiled=True
    )
    ffn_out = join(chips_last(*out_pair, bits))
    mean_c = mean_c + swap(mean_c, "ty")
    mean_c = mean_c + swap(mean_c, "tz")
    backs = self_backward(queries, d_self, logs, delta, all_keys, all_values, 0, None)
    *backs, delta, mean_c, ffn_out = together(*backs, delta, mean_c, ffn_out)
    result = back_clip((middle + gate_ffn * ffn_out).astype(BF))
    d_gate_ffn = jnp.sum(grad_out * ffn_out, axis=0, keepdims=True)
    mean_c = mean_c[None] / width
    d_craw = factor_c * (scaled_c - normed_c * mean_c)
    d_gain_c = jnp.sum(d_ckeys * normed_c, axis=2).reshape(1, part)
    cap_low = join([d_craw, d_cvalues]).reshape(2 * part, -1).astype(BF)
    cap_half = team_parts(dot(cap_all, cap_low, 0, 1).astype(BF))
    d_cap = dot(cap_low, w_cap, 0, 1).astype(BF)
    d_cap = lax.psum_scatter(d_cap, TEAM, scatter_dimension=0, tiled=True).astype(F32)
    backs = self_backward(queries, d_self, logs, delta, all_keys, all_values, 1, backs)
    *backs, delta, up_rows = together(*backs, delta, up_rows)
    sum_gate_up = to_shards(up_rows)
    backs = self_backward(queries, d_self, logs, delta, all_keys, all_values, 2, backs)
    *backs, result, sum_gate_up, cap_half = together(*backs, result, sum_gate_up, cap_half)
    cap_rows = half_parts(cap_half)
    dq_self, dk, dv = backs
    if reps > 1:
        dk, dv = (lax.psum_scatter(v, "rep", scatter_dimension=2, tiled=True) for v in (dk, dv))

    turned_grad = jnp.stack(
        [turn((dq_self + dq_cross) * scale, cosine, -sine), turn(dk, cosine, -sine)]
    )
    scaled_qk = turned_grad * gains[:2]
    mean_qk = team_sum(team_mean(scaled_qk * normed_qk))[:, None, None] / width
    d_gain_qk = jnp.sum(turned_grad * normed_qk, axis=3).reshape(2, part)
    d_qk = (factors * (scaled_qk - normed_qk * mean_qk)).reshape(2 * part, team_rows)
    d_projected = join([d_qk, dv.reshape(part, team_rows)]).astype(BF)
    d_projected, cap_rows = together(d_projected, cap_rows)

    def attn_side(which):
        return dot(core_side(d_projected, which, 1), w_in, 0, 1).astype(BF)

    side_sent = attn_side(1 - bits[2])
    mine = add_core(attn_side(bits[2]), side_sent)
    core_grad = dot(core_all, d_projected, 0, 1)
    column_sum = dot(d_projected, jnp.ones((team_rows, 128), BF), 1, 0)[:, 0][None]
    mine, core_grad = together(mine, core_grad)
    pair = chips_first(*by_chip(mine), bits)
    in_half = team_parts((core_grad * row_scale + row_shift * column_sum).astype(BF))
    w_in_f = w_in.astype(F32)
    d_shift_attn = jnp.sum(column_sum * w_in_f, axis=1)[None]
    moment_a = jnp.sum(core_grad * w_in_f, axis=1)[None]
    d_scale_attn = moment_a * norm_gains[0]
    d_gain_attn = moment_a * (1.0 + scale_attn)

    def placed(values):
        wide = jnp.tile(values, (1, width // values.shape[1]))
        spot = jnp.arange(width, dtype=jnp.int32) // values.shape[1]
        return jnp.where(spot == rank, wide, 0.0)

    gate_row = jnp.pad(d_cross_gate[None], ((0, 0), (0, width // team - heads)))
    sums = join(
        [
            d_shift_attn,
            d_scale_attn,
            d_gate_attn,
            d_shift_ffn,
            d_scale_ffn,
            d_gate_ffn,
            d_gain_attn,
            d_gain_ffn,
            placed(join([d_gain_qk, d_gain_c, gate_row])),
        ]
    )
    sums = sums + swap(sums, "tc")
    sums = both_sides(sums, "clip", clip_pair, 0)
    *pair, sums, in_half = together(*pair, sums, in_half)
    d_attn_in = join(chips_last(*pair, bits))
    for axis in ("ty", "tz"):
        sums = sums + swap(sums, axis)
    if reps > 1:
        sums = lax.psum(sums, "rep")
    sums = both_sides(sums, "half", half, 1)
    d_attn_in, sums = together(d_attn_in, sums)
    sum_gate, sum_up = ff_columns(sum_gate_up[..., :ff_part]), ff_columns(sum_gate_up[..., ff_part:])
    in_rows = half_parts(in_half)
    sum_cap = to_shards(cap_rows)
    factor_a = row_factor(token_vals)
    core_a = token_vals * factor_a
    d_core = d_attn_in * (norm_gains[0] * (1.0 + scale_attn))
    d_tokens = back_clip(
        d_middle
        + factor_a * (d_core - core_a * jnp.mean(d_core * core_a, axis=-1, keepdims=True))
    )
    mod_low = sums[:, :, :6].astype(BF).reshape(condition.shape[0], -1)
    small = jnp.sum(sums[:, :, 6:], axis=(0, 1))
    gain_sum = join([small[:1], small[2:5], small[1:2]])
    gate_sum = small[5].reshape(team, -1)[:, :heads].reshape(-1)
    d_bias = jnp.sum(mod_low.astype(F32), axis=0)
    d_silu = dot(mod_low, modulation_weight, 1, 1)
    d_silu = lax.dynamic_update_slice_in_dim(
        jnp.zeros(condition.shape, F32), d_silu, device * shard_rows, 1
    )
    sum_input = to_shards(in_rows)
    if reps > 1:
        d_silu = lax.psum(d_silu, "rep")
    for axis in ("tc", "ty", "tz", "half", "clip"):
        d_silu = d_silu + swap(d_silu, axis)
    _, silu_back = jax.vjp(jax.nn.silu, condition)
    d_condition = silu_back(d_silu)[0]
    grad_mod = dot(silu_rows, mod_low, 0, 0)

    sum_input = head_columns(sum_input, 3)
    sum_ckey = head_columns(sum_cap[..., :part], 1)
    sum_cvalue = head_columns(sum_cap[..., part:], 1)
    sum_down, sum_output, d_cap = together(sum_down, sum_output, d_cap, d_attn_in)[:3]
    sum_down, sum_output = sum_down.astype(F32), sum_output.astype(F32)
    d_cap = d_cap.reshape(clips_here, slots_here, -1)
    d_caption = back_clip(join([pick(d_cap, half), pick(d_cap, 1 - half)]))
    return (
        result,
        d_tokens,
        d_caption,
        d_condition,
        grad_mod,
        d_bias,
        gain_sum,
        gate_sum,
        sum_input,
        sum_output,
        sum_ckey,
        sum_cvalue,
        sum_gate,
        sum_up,
        sum_down,
    )


def solution(mesh):
    clip_count, seq_count = mesh.shape["clip"], mesh.shape["seq"]

    def program(*arrays):
        halves = arrays[0].shape[0] // clip_count
        shape = (clip_count, halves, seq_count // (halves * 8), 2, 2, 2)
        fine = Mesh(mesh.devices.reshape(shape), EVERY)
        rows = P("clip", SEQ, None)
        shard = P(EVERY, None)
        mapped = jax.shard_map(
            on_device,
            mesh=fine,
            in_specs=(
                rows,
                P(),
                rows,
                P("clip"),
                P(None, "clip", SEQ),
                shard,
                P(),
                P(),
                P(),
                shard,
                shard,
                shard,
                shard,
                shard,
                shard,
                shard,
                rows,
            ),
            out_specs=(rows, rows, rows, P(), shard, P(), P(), P()) + (shard,) * 7,
            check_vma=False,
        )
        return mapped(*arrays)

    return program
```

```python
import jax
import jax.numpy as jnp
from jax import lax
from jax.experimental import pallas as pl
from jax.experimental.pallas import tpu as pltpu
from jax.sharding import Mesh
from jax.sharding import PartitionSpec as P

EPSILON = 1e-06
NEGATIVE = -1e30
BF = jnp.bfloat16
F32 = jnp.float32
SEQ = ("half", "rep", "tz", "ty", "tc")
GROUPS = ("clip", "half", "rep")
TEAM = ("tc", "tz", "ty")
SHARDS = ("tz", "ty", "tc")
EVERY = ("clip",) + SEQ
KERNEL = pltpu.CompilerParams(
    vmem_limit_bytes=56 * 1024 * 1024, dimension_semantics=("arbitrary", "arbitrary")
)


def swap(block, axis):
    return lax.ppermute(block, axis, [(0, 1), (1, 0)])


def together(*values):
    return lax.optimization_barrier(values)


def after(value, *others):
    return lax.optimization_barrier((value,) + others)[0]


def dot(left, right, left_dim, right_dim):
    dims = (((left_dim,), (right_dim,)), ((), ()))
    return lax.dot_general(left, right, dims, preferred_element_type=F32)


def join(parts, axis=0):
    return jnp.concatenate(parts, axis=axis)


def upright(block):
    return jnp.transpose(block.astype(F32)).astype(BF)


def self_forward_kernel(q_ref, k_ref, v_ref, o_ref, log_ref, k_rows):
    @pl.when(pl.program_id(1) == 0)
    def _():
        k_rows[...] = upright(k_ref[0])

    scores = dot(k_rows[...], q_ref[0], 1, 0)
    peak = jnp.max(scores, axis=0, keepdims=True)
    weights = jnp.exp(scores - peak)
    total = jnp.sum(weights, axis=0, keepdims=True)
    o_ref[0] = dot(v_ref[0], weights.astype(BF), 1, 0) / total
    log_ref[0] = peak + jnp.log(total)


def self_backward_kernel(
    q_ref, g_ref, log_ref, delta_ref, k_ref, v_ref, dq_ref, dk_ref, dv_ref, k_rows, v_rows, dk, dv
):
    step = pl.program_id(1)

    @pl.when(step == 0)
    def _():
        k_rows[...] = upright(k_ref[0])
        v_rows[...] = upright(v_ref[0])
        dk[...] = jnp.zeros_like(dk)
        dv[...] = jnp.zeros_like(dv)

    q, g = q_ref[0], g_ref[0]
    probs = jnp.exp(dot(k_rows[...], q, 1, 0) - log_ref[0])
    ds = (probs * (dot(v_rows[...], g, 1, 0) - delta_ref[0])).astype(BF)
    dv[...] += dot(probs.astype(BF), g, 1, 1)
    dk[...] += dot(ds, q, 1, 1)
    dq_ref[0] = dot(k_ref[0], ds, 1, 0)

    @pl.when(step == pl.num_programs(1) - 1)
    def _():
        dk_ref[0] = jnp.transpose(dk[...])
        dv_ref[0] = jnp.transpose(dv[...])


def cross_forward_kernel(q_ref, k_ref, v_ref, mask_ref, o_ref):
    scores = dot(upright(k_ref[0]), q_ref[0], 1, 0) + mask_ref[...]
    weights = jnp.exp(scores - jnp.max(scores, axis=0, keepdims=True))
    total = jnp.sum(weights, axis=0, keepdims=True)
    o_ref[0] = dot(v_ref[0], weights.astype(BF), 1, 0) / total


def cross_backward_kernel(
    q_ref, g_ref, k_ref, v_ref, mask_ref, gate_ref, dq_ref, dk_ref, dv_ref, dg_ref
):
    q, g, gate = q_ref[0], g_ref[0], gate_ref[0, 0:1, 0:1]
    scores = dot(upright(k_ref[0]), q, 1, 0) + mask_ref[...]
    weights = jnp.exp(scores - jnp.max(scores, axis=0, keepdims=True))
    probs = weights / jnp.sum(weights, axis=0, keepdims=True)
    dp = dot(upright(v_ref[0]), g, 1, 0)
    inner = jnp.sum(probs * dp, axis=0, keepdims=True)
    ds = (probs * (gate * (dp - inner))).astype(BF)
    dg_ref[0] = inner
    dq_ref[0] = dot(k_ref[0], ds, 1, 0)
    dk = dot(q, ds, 1, 1)
    dv = dot(g, probs.astype(BF), 1, 1) * gate

    @pl.when(pl.program_id(1) == 0)
    def _():
        dk_ref[0] = dk
        dv_ref[0] = dv

    @pl.when(pl.program_id(1) > 0)
    def _():
        dk_ref[0] += dk
        dv_ref[0] += dv


def place_weight_kernel(bit_ref, mine_ref, other_ref, scale_ref, shift_ref, w_ref, scaled_ref, bias_ref):
    step = pl.program_id(0)

    def run(ref):
        values = ref[...].astype(F32)
        w_ref[...] = ref[...]
        scaled_ref[...] = (values * scale_ref[...]).astype(BF)
        bias = jnp.sum(values * shift_ref[...], axis=0, keepdims=True)

        @pl.when(step == 0)
        def _():
            bias_ref[...] = bias

        @pl.when(step > 0)
        def _():
            bias_ref[...] += bias

    @pl.when(step == bit_ref[0])
    def _():
        run(mine_ref)

    @pl.when(step != bit_ref[0])
    def _():
        run(other_ref)


def place_weight(bit, mine, other, scale, shift):
    rows, columns = mine.shape
    part = pl.BlockSpec((rows, columns), lambda i: (0, 0))
    out = pl.BlockSpec((rows, columns), lambda i: (i, 0))
    column = pl.BlockSpec((rows, 1), lambda i: (i, 0))
    return pl.pallas_call(
        place_weight_kernel,
        grid=(2,),
        in_specs=[pl.BlockSpec(memory_space=pltpu.SMEM), part, part, column, column],
        out_specs=[out, out, pl.BlockSpec((1, columns), lambda i: (0, 0))],
        out_shape=[
            jax.ShapeDtypeStruct((2 * rows, columns), BF),
            jax.ShapeDtypeStruct((2 * rows, columns), BF),
            f32(1, columns),
        ],
        compiler_params=pltpu.CompilerParams(vmem_limit_bytes=48 * 1024 * 1024),
    )(jnp.reshape(bit, (1,)).astype(jnp.int32), mine, other, scale, shift)


def norm_rows_kernel(rows_ref, core_ref, places_ref):
    rows = core_ref.shape[0] // 2
    for part in (0, 1):
        start = part * (rows + 8)
        values = rows_ref[start : start + rows].astype(F32)
        square = jnp.mean(values * values, axis=-1, keepdims=True)
        core_ref[part * rows : (part + 1) * rows] = (values * lax.rsqrt(square + EPSILON)).astype(BF)
        places_ref[0, part] = rows_ref[start + rows : start + rows + 8, :rows].astype(F32)


def norm_rows(blocks, rows):
    width = blocks.shape[1]
    pair = 2 * (rows + 8)
    count = blocks.shape[0] // pair
    return pl.pallas_call(
        norm_rows_kernel,
        grid=(count,),
        in_specs=[pl.BlockSpec((pair, width), lambda i: (i, 0))],
        out_specs=[
            pl.BlockSpec((2 * rows, width), lambda i: (i, 0)),
            pl.BlockSpec((1, 2, 8, rows), lambda i: (i, 0, 0, 0)),
        ],
        out_shape=[
            jax.ShapeDtypeStruct((2 * count * rows, width), BF),
            f32(count, 2, 8, rows),
        ],
        compiler_params=pltpu.CompilerParams(vmem_limit_bytes=32 * 1024 * 1024),
    )(blocks)


def by_query(rows, block, first=0):
    return pl.BlockSpec((1, rows, block), lambda h, i: (h + first, 0, i))


def whole_head(rows, columns, first=0):
    return pl.BlockSpec((1, rows, columns), lambda h, i: (h + first, 0, 0))


def mask_spec(rows):
    return pl.BlockSpec((rows, 1), lambda h, i: (0, 0))


def f32(*shape):
    return jax.ShapeDtypeStruct(shape, F32)


def query_block(rows, keys, most):
    block = rows
    while block > 128 and block * keys > most:
        block //= 2
    return block


def attention_cost(scores, products, heads=1):
    return pl.CostEstimate(
        flops=heads * scores * products * 2 * 256,
        transcendentals=heads * scores,
        bytes_accessed=heads * scores // 2,
    )


def one_head(kernel, head, kept, inputs, in_specs, out_specs, out_shape, scratch, steps, cost):
    extra = len(kept) if kept else 0

    def body(*refs):
        kernel(*refs[: len(inputs)], *refs[len(inputs) + extra :])

    return pl.pallas_call(
        body,
        grid=(1, steps),
        in_specs=in_specs + [pl.BlockSpec(memory_space=pl.ANY)] * extra,
        out_specs=out_specs,
        out_shape=out_shape,
        scratch_shapes=scratch,
        input_output_aliases={len(inputs) + i: i for i in range(extra)},
        compiler_params=KERNEL,
        cost_estimate=cost,
    )(*inputs, *(kept or ()))


def self_forward(q, k, v, head, kept):
    heads, dim, rows = q.shape
    keys = k.shape[2]
    block = query_block(rows, keys, 1 << 21)
    return one_head(
        self_forward_kernel,
        head,
        kept,
        (q, k, v),
        [by_query(dim, block, head), whole_head(dim, keys, head), whole_head(dim, keys, head)],
        [by_query(dim, block, head), by_query(1, block, head)],
        [f32(heads, dim, rows), f32(heads, 1, rows)],
        [pltpu.VMEM((keys, dim), BF)],
        rows // block,
        attention_cost(rows * keys, 2),
    )


def self_backward(q, g, log_total, delta, k, v, head, kept):
    heads, dim, rows = q.shape
    keys = k.shape[2]
    block = query_block(rows, keys, 1 << 20)
    return one_head(
        self_backward_kernel,
        head,
        kept,
        (q, g, log_total, delta, k, v),
        [by_query(dim, block, head)] * 2
        + [by_query(1, block, head)] * 2
        + [whole_head(dim, keys, head)] * 2,
        [by_query(dim, block, head), whole_head(dim, keys, head), whole_head(dim, keys, head)],
        [f32(heads, dim, rows), f32(heads, dim, keys), f32(heads, dim, keys)],
        [pltpu.VMEM((keys, dim), t) for t in (BF, BF, F32, F32)],
        rows // block,
        attention_cost(rows * keys, 5),
    )


def cross_forward(q, k, v, mask):
    heads, dim, rows = q.shape
    keys = k.shape[2]
    block = query_block(rows, keys, 1 << 19)
    return pl.pallas_call(
        cross_forward_kernel,
        grid=(heads, rows // block),
        in_specs=[
            by_query(dim, block),
            whole_head(dim, keys),
            whole_head(dim, keys),
            mask_spec(keys),
        ],
        out_specs=by_query(dim, block),
        out_shape=f32(heads, dim, rows),
        compiler_params=KERNEL,
        cost_estimate=attention_cost(rows * keys, 2, heads),
    )(q, k, v, mask)


def cross_backward(q, g, k, v, mask, gate):
    heads, dim, rows = q.shape
    keys = k.shape[2]
    block = query_block(rows, keys, 1 << 19)
    return pl.pallas_call(
        cross_backward_kernel,
        grid=(heads, rows // block),
        in_specs=[
            by_query(dim, block),
            by_query(dim, block),
            whole_head(dim, keys),
            whole_head(dim, keys),
            mask_spec(keys),
            whole_head(8, 128),
        ],
        out_specs=[
            by_query(dim, block),
            whole_head(dim, keys),
            whole_head(dim, keys),
            by_query(1, block),
        ],
        out_shape=[
            f32(heads, dim, rows),
            f32(heads, dim, keys),
            f32(heads, dim, keys),
            f32(heads, 1, rows),
        ],
        compiler_params=KERNEL,
        cost_estimate=attention_cost(rows * keys, 5, heads),
    )(q, g, k, v, mask, gate)


def halves(block):
    half = block.shape[0] // 2
    return block[:half], block[half:]


def pick(block, index, dim=0, keep=False):
    return lax.dynamic_index_in_dim(block, index, dim, keepdims=keep)


def both_sides(block, axis, bit, dim):
    other = swap(block, axis)
    return jnp.where(bit == 0, jnp.stack([block, other], dim), jnp.stack([other, block], dim))


def kept_sum(block, axis, bit, dim):
    other = swap(pick(block, 1 - bit, dim).astype(BF), axis)
    return pick(block, bit, dim).astype(F32) + other.astype(F32)


def team_sum(values):
    for axis in TEAM:
        values = values + swap(values, axis)
    return values


def chips_first(first, second, bits):
    return kept_sum(first, "tz", bits[0], 0), kept_sum(second, "ty", bits[1], 1)


def chips_last(first, second, bits):
    return kept_sum(first, "ty", bits[1], 0), kept_sum(second, "tz", bits[0], 0)


def row_factor(values):
    return lax.rsqrt(jnp.mean(values * values, axis=-1, keepdims=True) + EPSILON)


def rope_tables(places, head_dim):
    pair_count = head_dim // 2
    lead_pairs = pair_count // 4
    mid_pairs = (pair_count - lead_pairs) // 2
    last_pairs = pair_count - lead_pairs - mid_pairs
    angles = []
    for which, extent in enumerate((lead_pairs, mid_pairs, last_pairs)):
        offsets = jnp.arange(extent, dtype=F32)
        angles.append(jnp.power(10000.0, -offsets / extent)[:, None] * places[which][None])
    angles = join(angles)
    cosine, sine = jnp.cos(angles), jnp.sin(angles)
    return join([cosine, cosine]), join([-sine, sine])


def turn(vectors, cosine, sine):
    half = vectors.shape[1] // 2
    crossed = join([vectors[:, half:], vectors[:, :half]], axis=1)
    return vectors * cosine + crossed * sine


def on_device(
    tokens,
    condition,
    caption,
    caption_lengths,
    positions,
    modulation_weight,
    modulation_bias,
    norm_gains,
    cross_gate,
    input_weight,
    output_weight,
    caption_key_weight,
    caption_value_weight,
    gate_weight,
    up_weight,
    down_weight,
    cotangent,
):
    clips_here, clip_rows, width = tokens.shape
    head_count = cross_gate.shape[0]
    head_dim = width // head_count
    scale = head_dim ** (-0.5)
    team = 8
    heads = head_count // team
    rows_in = input_weight.shape[0]
    part = heads * head_dim
    groups = lax.axis_size(GROUPS)
    reps = lax.axis_size("rep")
    half = lax.axis_index("half")
    bits = tuple(lax.axis_index(axis) for axis in SHARDS)
    rank = lax.axis_index(TEAM)
    clip_pair = lax.axis_index("clip")
    device = lax.axis_index(EVERY)

    def own_clip(block):
        return pick(block, half), swap(pick(block, 1 - half), "half")

    def back_clip(block):
        rows = block.shape[0] // 2
        kept, other = block[:rows], block[rows:]
        other = swap(other.astype(BF), "half").astype(block.dtype)
        return jnp.where(half == 0, jnp.stack([kept, other]), jnp.stack([other, kept]))

    def own_columns(table):
        return lax.dynamic_slice_in_dim(table, rank * part, part, table.ndim - 1)

    def by_rank(weight, split, by_shard=False):
        rows = weight.shape[0]
        if by_shard:
            tiled = weight.reshape(rows, split, team, -1)
            return jnp.transpose(tiled, (2, 0, 1, 3)).reshape(team, rows, -1)
        tiled = weight.reshape(rows, split, 2, 2, 2, -1)
        return jnp.transpose(tiled, (3, 4, 2, 0, 1, 5)).reshape(team, rows, -1)

    def from_team(blocks):
        mine = lax.all_to_all(blocks, SHARDS, split_axis=0, concat_axis=0, tiled=True)
        return mine.reshape(-1, blocks.shape[2])

    def all_reps(block):
        return lax.all_gather(block, "rep", axis=0, tiled=True) if reps > 1 else block

    def across_half(block):
        return both_sides(all_reps(block), "half", half, 0)

    def across_clip(block):
        return both_sides(block, "clip", clip_pair, 0).reshape(-1, block.shape[-1])

    places = jnp.pad(
        jnp.transpose(positions, (1, 0, 2)).astype(BF),
        ((0, 0), (0, 5), (0, width - clip_rows)),
    )
    rows_a, rows_b = own_clip(join([tokens, places], axis=1))
    in_team = from_team(by_rank(input_weight, 3))
    shard_rows = modulation_weight.shape[0]
    silu_all = jax.nn.silu(condition).astype(BF)
    silu_rows = lax.dynamic_slice_in_dim(silu_all, device * shard_rows, shard_rows, 1)
    mod_part = dot(silu_rows, modulation_weight, 1, 0)
    mod_part = mod_part.reshape(lax.axis_size("clip"), clips_here, -1)
    mod_pair = pick(mod_part, clip_pair) + swap(pick(mod_part, 1 - clip_pair), "clip")
    mod_own = pick(mod_pair, half, keep=True) + swap(pick(mod_pair, 1 - half, keep=True), "half")
    rows_a, rows_b, mod_own, in_team = together(rows_a, rows_b, mod_own, in_team)

    rows_all = lax.all_gather(join([rows_a, rows_b]), TEAM, axis=0, tiled=True)
    in_half = across_half(in_team).reshape(-1, 3 * part)
    if reps > 1:
        mod_own = lax.psum(mod_own, "rep")
    mod_own = team_sum(mod_own)
    in_half, mod_own, caption = together(in_half, mod_own, caption)

    in_other = swap(in_half, "clip")
    rows_cap = caption_key_weight.shape[0]
    slots_here = caption.shape[1]
    cap_a, cap_b = own_clip(caption)
    modulation = mod_own + modulation_bias
    shift_attn, scale_attn, gate_attn, shift_ffn, scale_ffn, gate_ffn = (
        modulation[:, i * width : (i + 1) * width] for i in range(6)
    )
    token_vals = join([rows_a[:clip_rows], rows_b[:clip_rows]]).astype(F32)
    rows_here = token_vals.shape[0]
    team_rows = team * rows_here
    row_scale = (norm_gains[0] * (1.0 + scale_attn)).reshape(width, 1)
    row_shift = shift_attn.reshape(width, 1)
    w_in, w_scaled, bias = place_weight(clip_pair, in_half, in_other, row_scale, row_shift)
    bias = bias.reshape(3 * part, 1)
    w_scaled, bias, rows_all, cap_a, cap_b, out_shard, ckey_weight, cvalue_weight = together(
        w_scaled,
        bias,
        rows_all,
        cap_a,
        cap_b,
        output_weight,
        caption_key_weight,
        caption_value_weight,
    )
    cap_team = from_team(join([by_rank(ckey_weight, 1), by_rank(cvalue_weight, 1)], axis=2))
    w_out = across_half(out_shard)
    cap_rows = jnp.where(half == 0, join([cap_a, cap_b]), join([cap_b, cap_a]))
    core_all, all_places = norm_rows(rows_all, clip_rows)
    all_places = jnp.transpose(all_places[:, :, :3], (2, 0, 1, 3)).reshape(3, team_rows)

    def by_head(block):
        return block.reshape(heads, head_dim, block.shape[-1])

    raw_qk = dot(w_scaled[:, : 2 * part], core_all, 0, 1) + bias[: 2 * part]
    raw_qk = raw_qk.reshape(2, heads, head_dim, team_rows)
    squares = jnp.sum(raw_qk * raw_qk, axis=(1, 2))
    squares, raw_qk, cap_team, cap_rows, cotangent, w_out = together(
        team_sum(squares), raw_qk, cap_team, cap_rows, cotangent, w_out
    )
    cap_half = across_half(cap_team)
    cap_all = lax.all_gather(cap_rows, TEAM, axis=0, tiled=True)
    cot_a, cot_b = own_clip(cotangent)
    w_out = both_sides(w_out, "clip", clip_pair, 0).reshape(-1, width)
    factors = lax.rsqrt(squares / width + EPSILON)[:, None, None]
    cosine, sine = rope_tables(all_places, head_dim)
    values = by_head((dot(w_scaled[:, 2 * part :], core_all, 0, 1) + bias[2 * part :]).astype(BF))
    gains = jnp.stack([own_columns(norm_gains[i]) for i in (1, 2, 3)])
    gains = gains.reshape(3, heads, head_dim, 1)
    normed_qk = raw_qk * factors
    turned = normed_qk * gains[:2]
    queries = (turn(turned[0], cosine, sine) * scale).astype(BF)
    keys = turn(turned[1], cosine, sine).astype(BF)
    all_keys, all_values = keys, values
    if reps > 1:
        all_keys, all_values = (lax.all_gather(v, "rep", axis=2, tiled=True) for v in (keys, values))

    queries, all_keys, all_values, gate_shard, up_shard, w_out = together(
        queries, all_keys, all_values, gate_weight, up_weight, w_out
    )
    w_out = lax.all_gather(w_out, SHARDS, axis=0, tiled=True)
    ff_block = down_weight.shape[0]
    ff_part = groups * ff_block
    up_team = from_team(
        join([by_rank(gate_shard, groups, True), by_rank(up_shard, groups, True)], axis=2)
    )
    o_self, logs = self_forward(queries, all_keys, all_values, 0, None)
    o_self, logs = self_forward(queries, all_keys, all_values, 1, (o_self, logs))
    o_self, logs, cap_half, cot_a, cot_b, up_team, cap_all = together(
        o_self, logs, cap_half, cot_a, cot_b, up_team, cap_all
    )
    w_cap = across_clip(cap_half)
    grad_out = join([cot_a, cot_b]).astype(F32)
    d_ffn = (gate_ffn * grad_out).astype(BF)
    d_ffn_all = lax.all_gather(d_ffn, TEAM, axis=0, tiled=True)
    up_half = across_half(up_team)
    o_self, logs = self_forward(queries, all_keys, all_values, 2, (o_self, logs))
    o_self, w_cap, down_shard = together(o_self, w_cap, down_weight)
    craw = dot(w_cap, cap_all, 0, 1)
    craw_key = by_head(craw[:part])
    square_c = jnp.sum(craw_key * craw_key, axis=(0, 1))[None]
    square_c = team_sum(square_c)
    factor_c = lax.rsqrt(square_c / width + EPSILON)[None]
    normed_c = craw_key * factor_c
    ckeys = (normed_c * gains[2]).astype(BF)
    cvalues = by_head(craw[part:]).astype(BF)
    all_ckeys, all_cvalues = ckeys, cvalues
    step = lax.axis_index("rep")
    order = jnp.arange(team * clips_here * slots_here, dtype=jnp.int32)
    in_rank = order // slots_here % clips_here
    from_rank = order // (slots_here * clips_here)
    from_shard = from_rank % 4 * 2 + from_rank // 4
    slots = ((in_rank * reps + step) * team + from_shard) * slots_here + order % slots_here
    if reps > 1:
        all_ckeys, all_cvalues = (
            lax.all_gather(v, "rep", axis=2, tiled=True) for v in (ckeys, cvalues)
        )
        slots = join([slots + (r - step) * team * slots_here for r in range(reps)])
    mask = jnp.where(slots < pick(caption_lengths, half), 0.0, NEGATIVE).astype(F32)[:, None]
    o_cross = cross_forward(queries, all_ckeys, all_cvalues, mask)
    tanh_gate = jnp.tanh(lax.dynamic_slice_in_dim(cross_gate, rank * heads, heads))
    tanh_wide = tanh_gate[:, None, None]
    mixed = (o_self + tanh_wide * o_cross).astype(BF).reshape(part, team, rows_here)
    mixed, up_half, w_out = together(jnp.transpose(mixed, (1, 0, 2)), up_half, w_out)
    w_gate_up = across_clip(up_half)
    down_half = across_half(down_shard)
    mixed = lax.all_to_all(mixed, TEAM, split_axis=0, concat_axis=0, tiled=True)
    out_rows = output_weight.shape[0]

    def by_shard(features):
        tiled = features.reshape(groups, team, out_rows, -1)
        return jnp.transpose(tiled, (1, 0, 2, 3)).reshape(width, -1)

    def by_group(features):
        tiled = features.reshape(team, groups, out_rows, -1)
        return jnp.transpose(tiled, (1, 0, 2, 3)).reshape(width, -1)

    combined = by_shard(mixed.reshape(width, rows_here))

    branch = dot(combined, w_out, 0, 0)
    middle = token_vals + gate_attn * branch
    factor_f = row_factor(middle)
    core_f = middle * factor_f
    ffn_in = (core_f * norm_gains[4] * (1.0 + scale_ffn) + shift_ffn).astype(BF)
    ffn_in, down_half, d_ffn_all = together(ffn_in, down_half, d_ffn_all)
    ffn_all = lax.all_gather(ffn_in, TEAM, axis=0, tiled=True)
    w_down = across_clip(down_half)
    w_gate_up, w_down, ffn_all = together(w_gate_up, w_down, ffn_all)
    gate_up = dot(ffn_all, w_gate_up, 1, 0)
    gate_vals, up_vals = gate_up[:, :ff_part], gate_up[:, ff_part:]
    d_hidden = dot(d_ffn_all, w_down, 1, 1)
    sig = jax.nn.sigmoid(gate_vals)
    silu_gate = gate_vals * sig
    hidden = (silu_gate * up_vals).astype(BF)
    d_gate = (d_hidden * up_vals * (sig + silu_gate * (1.0 - sig))).astype(BF)
    d_up = (d_hidden * silu_gate).astype(BF)
    d_gate_up = join([d_gate, d_up], axis=1)

    def core_side(block, which, dim=0):
        count = block.shape[dim] // 2
        return lax.dynamic_slice_in_dim(block, which * count, count, dim)

    def ffn_side(which):
        return dot(core_side(d_gate_up, which), w_gate_up, 1, 1).astype(BF)

    def by_chip(mine):
        tiled = mine.reshape(2, 2, 2, clip_rows, width)
        return tiled[:, :, 0], tiled[:, :, 1]

    def add_core(kept, sent):
        return (kept.astype(F32) + swap(sent, "tc").astype(F32)).astype(BF)

    def team_parts(slice_grad):
        tiled = slice_grad.reshape(lax.axis_size("clip"), clips_here, -1, slice_grad.shape[-1])
        return kept_sum(tiled, "clip", clip_pair, 0).astype(BF)

    def half_parts(tiled):
        summed = kept_sum(tiled, "half", half, 0)
        if reps > 1:
            summed = lax.psum_scatter(summed, "rep", scatter_dimension=0, tiled=True)
        return summed

    def to_shards(summed):
        ranked = summed.astype(BF).reshape(team, -1, summed.shape[-1])
        return lax.all_to_all(ranked, SHARDS, split_axis=0, concat_axis=0, tiled=True)

    def head_columns(blocks, split):
        rows = blocks.shape[1]
        tiled = blocks.reshape(2, 2, 2, rows, split, part)
        return jnp.transpose(tiled, (3, 4, 2, 0, 1, 5)).reshape(rows, -1).astype(F32)

    def ff_columns(blocks):
        rows = blocks.shape[1]
        tiled = blocks.reshape(team, rows, groups, ff_block)
        return jnp.transpose(tiled, (1, 2, 0, 3)).reshape(rows, -1).astype(F32)

    def all_parts(slice_grad):
        return lax.psum_scatter(slice_grad, GROUPS, scatter_dimension=0, tiled=True)

    side_sent = ffn_side(1 - bits[2])
    mine = add_core(ffn_side(bits[2]), side_sent)
    pair = chips_first(*by_chip(mine), bits)
    grad_down = dot(after(hidden, mine), d_ffn_all, 0, 0).astype(BF)
    *pair, grad_down = together(*pair, grad_down)
    sum_down = all_parts(grad_down)
    d_ffn_in = join(chips_last(*pair, bits))
    late_hidden = after(hidden, grad_down)
    out_sent = dot(core_side(late_hidden, 1 - bits[2]), w_down, 1, 0).astype(BF)
    out_kept = dot(core_side(late_hidden, bits[2]), w_down, 1, 0).astype(BF)
    d_ffn_in, out_sent, out_kept = together(d_ffn_in, out_sent, out_kept)

    out_mine = add_core(out_kept, out_sent)
    d_shift_ffn = jnp.sum(d_ffn_in, axis=0, keepdims=True)
    moment_f = jnp.sum(d_ffn_in * core_f, axis=0, keepdims=True)
    d_scale_ffn = moment_f * norm_gains[4]
    d_gain_ffn = moment_f * (1.0 + scale_ffn)
    d_core = d_ffn_in * (norm_gains[4] * (1.0 + scale_ffn))
    d_middle = grad_out + factor_f * (
        d_core - core_f * jnp.mean(d_core * core_f, axis=-1, keepdims=True)
    )
    d_branch = (gate_attn * d_middle).astype(BF)
    d_gate_attn = jnp.sum(d_middle * branch, axis=0, keepdims=True)
    d_combined = by_group(dot(w_out, d_branch, 1, 1).astype(BF))
    d_mixed = lax.all_to_all(
        d_combined.reshape(team, part, rows_here), TEAM, split_axis=0, concat_axis=0, tiled=True
    )
    late_ffn, late_gate, out_mine = together(ffn_all, d_gate_up, out_mine, d_combined)[:3]
    grad_gate_up = dot(late_ffn, late_gate, 0, 0).astype(BF)
    d_mixed, grad_gate_up = together(d_mixed, grad_gate_up)
    up_rows = all_parts(grad_gate_up)
    d_self = by_head(jnp.transpose(d_mixed, (1, 0, 2)).reshape(part, team_rows))

    out_pair = chips_first(*by_chip(out_mine), bits)
    gate_tile = jnp.broadcast_to(tanh_wide, (heads, 8, 128))
    dq_cross, d_ckeys, d_cvalues, gate_rows = cross_backward(
        queries, d_self, all_ckeys, all_cvalues, mask, gate_tile
    )
    d_cross_gate = jnp.sum(gate_rows, axis=(1, 2)) * (1.0 - tanh_gate * tanh_gate)
    if reps > 1:
        d_ckeys, d_cvalues = (
            lax.psum_scatter(v, "rep", scatter_dimension=2, tiled=True)
            for v in (d_ckeys, d_cvalues)
        )

    def team_mean(block):
        return jnp.sum(block, axis=(-3, -2))

    scaled_c = d_ckeys * gains[2]
    mean_c = team_mean(scaled_c * normed_c)[None]
    mean_c = mean_c + swap(mean_c, "tc")
    grad_output = dot(after(combined, dq_cross), d_branch, 1, 0).astype(BF)
    delta = jnp.sum(d_self.astype(F32) * o_self, axis=1, keepdims=True)
    delta, grad_output, mean_c, *out_pair = together(delta, grad_output, mean_c, *out_pair)
    sum_output = lax.psum_scatter(grad_output, SHARDS, scatter_dimension=0, tiled=True)
    ffn_out = join(chips_last(*out_pair, bits))
    mean_c = mean_c + swap(mean_c, "ty")
    mean_c = mean_c + swap(mean_c, "tz")
    backs = self_backward(queries, d_self, logs, delta, all_keys, all_values, 0, None)
    *backs, delta, mean_c, ffn_out = together(*backs, delta, mean_c, ffn_out)
    result = back_clip((middle + gate_ffn * ffn_out).astype(BF))
    d_gate_ffn = jnp.sum(grad_out * ffn_out, axis=0, keepdims=True)
    mean_c = mean_c[None] / width
    d_craw = factor_c * (scaled_c - normed_c * mean_c)
    d_gain_c = jnp.sum(d_ckeys * normed_c, axis=2).reshape(1, part)
    cap_low = join([d_craw, d_cvalues]).reshape(2 * part, -1).astype(BF)
    cap_half = team_parts(dot(cap_all, cap_low, 0, 1).astype(BF))
    d_cap = dot(cap_low, w_cap, 0, 1).astype(BF)
    backs = self_backward(queries, d_self, logs, delta, all_keys, all_values, 1, backs)
    *backs, delta, up_rows = together(*backs, delta, up_rows)
    sum_gate_up = to_shards(up_rows)
    backs = self_backward(queries, d_self, logs, delta, all_keys, all_values, 2, backs)
    *backs, result, sum_gate_up, sum_output, cap_half = together(
        *backs, result, sum_gate_up, sum_output, cap_half
    )
    cap_rows = half_parts(cap_half)
    sum_output = sum_output.reshape(lax.axis_size("clip"), clips_here, -1, width)
    sum_output = kept_sum(sum_output, "clip", clip_pair, 0)
    dq_self, dk, dv = backs
    if reps > 1:
        dk, dv = (lax.psum_scatter(v, "rep", scatter_dimension=2, tiled=True) for v in (dk, dv))

    turned_grad = jnp.stack(
        [turn((dq_self + dq_cross) * scale, cosine, -sine), turn(dk, cosine, -sine)]
    )
    scaled_qk = turned_grad * gains[:2]
    mean_qk = team_sum(team_mean(scaled_qk * normed_qk))[:, None, None] / width
    d_gain_qk = jnp.sum(turned_grad * normed_qk, axis=3).reshape(2, part)
    d_qk = (factors * (scaled_qk - normed_qk * mean_qk)).reshape(2 * part, team_rows)
    d_projected = join([d_qk, dv.reshape(part, team_rows)]).astype(BF)
    d_projected, sum_output = together(d_projected, sum_output)
    sum_output = half_parts(sum_output)

    def attn_side(which):
        return dot(core_side(d_projected, which, 1), w_in, 0, 1).astype(BF)

    side_sent = attn_side(1 - bits[2])
    mine = add_core(attn_side(bits[2]), side_sent)
    core_grad = dot(core_all, d_projected, 0, 1)
    column_sum = dot(d_projected, jnp.ones((team_rows, 128), BF), 1, 0)[:, 0][None]
    mine, core_grad = together(mine, core_grad)
    pair = chips_first(*by_chip(mine), bits)
    in_half = team_parts((core_grad * row_scale + row_shift * column_sum).astype(BF))
    w_in_f = w_in.astype(F32)
    d_shift_attn = jnp.sum(column_sum * w_in_f, axis=1)[None]
    moment_a = jnp.sum(core_grad * w_in_f, axis=1)[None]
    d_scale_attn = moment_a * norm_gains[0]
    d_gain_attn = moment_a * (1.0 + scale_attn)

    def placed(values):
        wide = jnp.tile(values, (1, width // values.shape[1]))
        spot = jnp.arange(width, dtype=jnp.int32) // values.shape[1]
        return jnp.where(spot == rank, wide, 0.0)

    gate_row = jnp.pad(d_cross_gate[None], ((0, 0), (0, width // team - heads)))
    sums = join(
        [
            d_shift_attn,
            d_scale_attn,
            d_gate_attn,
            d_shift_ffn,
            d_scale_ffn,
            d_gate_ffn,
            d_gain_attn,
            d_gain_ffn,
            placed(join([d_gain_qk, d_gain_c, gate_row])),
        ]
    )
    sums = sums + swap(sums, "tc")
    sums = both_sides(sums, "clip", clip_pair, 0)
    *pair, sums, in_half = together(*pair, sums, in_half)
    d_attn_in = join(chips_last(*pair, bits))
    d_cap = lax.psum_scatter(after(d_cap, *pair), TEAM, scatter_dimension=0, tiled=True)
    for axis in ("ty", "tz"):
        sums = sums + swap(sums, axis)
    if reps > 1:
        sums = lax.psum(sums, "rep")
    sums = both_sides(sums, "half", half, 1)
    d_attn_in, sums, sum_gate_up = together(d_attn_in, sums, sum_gate_up)
    sum_gate, sum_up = ff_columns(sum_gate_up[..., :ff_part]), ff_columns(sum_gate_up[..., ff_part:])
    in_rows = half_parts(in_half)
    sum_cap = to_shards(cap_rows)
    factor_a = row_factor(token_vals)
    core_a = token_vals * factor_a
    d_core = d_attn_in * (norm_gains[0] * (1.0 + scale_attn))
    d_tokens = back_clip(
        d_middle
        + factor_a * (d_core - core_a * jnp.mean(d_core * core_a, axis=-1, keepdims=True))
    )
    mod_low = sums[:, :, :6].astype(BF).reshape(condition.shape[0], -1)
    small = jnp.sum(sums[:, :, 6:], axis=(0, 1))
    gain_sum = join([small[:1], small[2:5], small[1:2]])
    gate_sum = small[5].reshape(team, -1)[:, :heads].reshape(-1)
    d_bias = jnp.sum(mod_low.astype(F32), axis=0)
    d_silu = dot(mod_low, modulation_weight, 1, 1)
    d_silu = lax.dynamic_update_slice_in_dim(
        jnp.zeros(condition.shape, F32), d_silu, device * shard_rows, 1
    )
    sum_input = to_shards(in_rows)
    if reps > 1:
        d_silu = lax.psum(d_silu, "rep")
    for axis in ("tc", "ty", "tz", "half", "clip"):
        d_silu = d_silu + swap(d_silu, axis)
    _, silu_back = jax.vjp(jax.nn.silu, condition)
    d_condition = silu_back(d_silu)[0]
    grad_mod = dot(silu_rows, mod_low, 0, 0)

    sum_input = head_columns(sum_input, 3)
    sum_ckey = head_columns(sum_cap[..., :part], 1)
    sum_cvalue = head_columns(sum_cap[..., part:], 1)
    sum_down, d_cap = together(sum_down, d_cap, d_attn_in)[:2]
    sum_down, d_cap = sum_down.astype(F32), d_cap.astype(F32)
    d_cap = d_cap.reshape(clips_here, slots_here, -1)
    d_caption = back_clip(join([pick(d_cap, half), pick(d_cap, 1 - half)]))
    return (
        result,
        d_tokens,
        d_caption,
        d_condition,
        grad_mod,
        d_bias,
        gain_sum,
        gate_sum,
        sum_input,
        sum_output,
        sum_ckey,
        sum_cvalue,
        sum_gate,
        sum_up,
        sum_down,
    )


def solution(mesh):
    clip_count, seq_count = mesh.shape["clip"], mesh.shape["seq"]

    def program(*arrays):
        halves = arrays[0].shape[0] // clip_count
        shape = (clip_count, halves, seq_count // (halves * 8), 2, 2, 2)
        fine = Mesh(mesh.devices.reshape(shape), EVERY)
        rows = P("clip", SEQ, None)
        shard = P(EVERY, None)
        mapped = jax.shard_map(
            on_device,
            mesh=fine,
            in_specs=(
                rows,
                P(),
                rows,
                P("clip"),
                P(None, "clip", SEQ),
                shard,
                P(),
                P(),
                P(),
                shard,
                shard,
                shard,
                shard,
                shard,
                shard,
                shard,
                rows,
            ),
            out_specs=(rows, rows, rows, P(), shard, P(), P(), P()) + (shard,) * 7,
            check_vma=False,
        )
        return mapped(*arrays)

    return program
```

```python
import jax
import jax.numpy as jnp
from jax import lax
from jax.experimental import pallas as pl
from jax.experimental.pallas import tpu as pltpu
from jax.sharding import Mesh
from jax.sharding import PartitionSpec as P

EPSILON = 1e-06
NEGATIVE = -1e30
BF = jnp.bfloat16
F32 = jnp.float32
SEQ = ("half", "rep", "tz", "ty", "tc")
GROUPS = ("clip", "half", "rep")
TEAM = ("tc", "tz", "ty")
SHARDS = ("tz", "ty", "tc")
EVERY = ("clip",) + SEQ
KERNEL = pltpu.CompilerParams(
    vmem_limit_bytes=56 * 1024 * 1024, dimension_semantics=("arbitrary", "arbitrary")
)


def swap(block, axis):
    return lax.ppermute(block, axis, [(0, 1), (1, 0)])


def together(*values):
    return lax.optimization_barrier(values)


def after(value, *others):
    return lax.optimization_barrier((value,) + others)[0]


def dot(left, right, left_dim, right_dim):
    dims = (((left_dim,), (right_dim,)), ((), ()))
    return lax.dot_general(left, right, dims, preferred_element_type=F32)


def join(parts, axis=0):
    return jnp.concatenate(parts, axis=axis)


def upright(block):
    return jnp.transpose(block.astype(F32)).astype(BF)


def self_forward_kernel(q_ref, k_ref, v_ref, o_ref, log_ref, k_rows):
    @pl.when(pl.program_id(1) == 0)
    def _():
        k_rows[...] = upright(k_ref[0])

    scores = dot(k_rows[...], q_ref[0], 1, 0)
    peak = jnp.max(scores, axis=0, keepdims=True)
    weights = jnp.exp(scores - peak)
    total = jnp.sum(weights, axis=0, keepdims=True)
    o_ref[0] = dot(v_ref[0], weights.astype(BF), 1, 0) / total
    log_ref[0] = peak + jnp.log(total)


def self_backward_kernel(
    q_ref, g_ref, log_ref, delta_ref, k_ref, v_ref, dq_ref, dk_ref, dv_ref, k_rows, v_rows, dk, dv
):
    step = pl.program_id(1)

    @pl.when(step == 0)
    def _():
        k_rows[...] = upright(k_ref[0])
        v_rows[...] = upright(v_ref[0])
        dk[...] = jnp.zeros_like(dk)
        dv[...] = jnp.zeros_like(dv)

    q, g = q_ref[0], g_ref[0]
    probs = jnp.exp(dot(k_rows[...], q, 1, 0) - log_ref[0])
    ds = (probs * (dot(v_rows[...], g, 1, 0) - delta_ref[0])).astype(BF)
    dv[...] += dot(probs.astype(BF), g, 1, 1)
    dk[...] += dot(ds, q, 1, 1)
    dq_ref[0] = dot(k_ref[0], ds, 1, 0)

    @pl.when(step == pl.num_programs(1) - 1)
    def _():
        dk_ref[0] = jnp.transpose(dk[...])
        dv_ref[0] = jnp.transpose(dv[...])


def cross_forward_kernel(q_ref, k_ref, v_ref, mask_ref, o_ref):
    scores = dot(upright(k_ref[0]), q_ref[0], 1, 0) + mask_ref[...]
    weights = jnp.exp(scores - jnp.max(scores, axis=0, keepdims=True))
    total = jnp.sum(weights, axis=0, keepdims=True)
    o_ref[0] = dot(v_ref[0], weights.astype(BF), 1, 0) / total


def cross_backward_kernel(
    q_ref, g_ref, k_ref, v_ref, mask_ref, gate_ref, dq_ref, dk_ref, dv_ref, dg_ref
):
    q, g, gate = q_ref[0], g_ref[0], gate_ref[0, 0:1, 0:1]
    scores = dot(upright(k_ref[0]), q, 1, 0) + mask_ref[...]
    weights = jnp.exp(scores - jnp.max(scores, axis=0, keepdims=True))
    probs = weights / jnp.sum(weights, axis=0, keepdims=True)
    dp = dot(upright(v_ref[0]), g, 1, 0)
    inner = jnp.sum(probs * dp, axis=0, keepdims=True)
    ds = (probs * (gate * (dp - inner))).astype(BF)
    dg_ref[0] = inner
    dq_ref[0] = dot(k_ref[0], ds, 1, 0)
    dk = dot(q, ds, 1, 1)
    dv = dot(g, probs.astype(BF), 1, 1) * gate

    @pl.when(pl.program_id(1) == 0)
    def _():
        dk_ref[0] = dk
        dv_ref[0] = dv

    @pl.when(pl.program_id(1) > 0)
    def _():
        dk_ref[0] += dk
        dv_ref[0] += dv


def place_weight_kernel(bit_ref, mine_ref, other_ref, scale_ref, shift_ref, w_ref, scaled_ref, bias_ref):
    step = pl.program_id(0)

    def run(ref):
        values = ref[...].astype(F32)
        w_ref[...] = ref[...]
        scaled_ref[...] = (values * scale_ref[...]).astype(BF)
        bias = jnp.sum(values * shift_ref[...], axis=0, keepdims=True)

        @pl.when(step == 0)
        def _():
            bias_ref[...] = bias

        @pl.when(step > 0)
        def _():
            bias_ref[...] += bias

    @pl.when(step == bit_ref[0])
    def _():
        run(mine_ref)

    @pl.when(step != bit_ref[0])
    def _():
        run(other_ref)


def place_weight(bit, mine, other, scale, shift):
    rows, columns = mine.shape
    part = pl.BlockSpec((rows, columns), lambda i: (0, 0))
    out = pl.BlockSpec((rows, columns), lambda i: (i, 0))
    column = pl.BlockSpec((rows, 1), lambda i: (i, 0))
    return pl.pallas_call(
        place_weight_kernel,
        grid=(2,),
        in_specs=[pl.BlockSpec(memory_space=pltpu.SMEM), part, part, column, column],
        out_specs=[out, out, pl.BlockSpec((1, columns), lambda i: (0, 0))],
        out_shape=[
            jax.ShapeDtypeStruct((2 * rows, columns), BF),
            jax.ShapeDtypeStruct((2 * rows, columns), BF),
            f32(1, columns),
        ],
        compiler_params=pltpu.CompilerParams(vmem_limit_bytes=48 * 1024 * 1024),
    )(jnp.reshape(bit, (1,)).astype(jnp.int32), mine, other, scale, shift)


def input_grad_kernel(
    core_ref, grad_ref, w_ref, scale_ref, shift_ref, out_ref, moment_ref, sum_ref, column_sum
):
    @pl.when(pl.program_id(0) == 0)
    def _():
        column_sum[...] = jnp.sum(grad_ref[...].astype(F32), axis=1, keepdims=True)

    weight = w_ref[...].astype(F32)
    product = dot(grad_ref[...], core_ref[...], 1, 0)
    moment_ref[...] = jnp.sum(product * weight, axis=0, keepdims=True)
    sum_ref[...] = jnp.sum(column_sum[...] * weight, axis=0, keepdims=True)
    out_ref[...] = jnp.transpose(
        product * scale_ref[...] + column_sum[...] * shift_ref[...]
    ).astype(BF)


def input_grad(core, grad, weight_t, scale, shift):
    rows, width = core.shape
    columns = grad.shape[0]
    block = width // 4

    def across(count):
        return pl.BlockSpec((count, block), lambda i: (0, i))

    return pl.pallas_call(
        input_grad_kernel,
        grid=(4,),
        in_specs=[
            across(rows),
            pl.BlockSpec((columns, rows), lambda i: (0, 0)),
            across(columns),
            across(1),
            across(1),
        ],
        out_specs=[pl.BlockSpec((block, columns), lambda i: (i, 0)), across(1), across(1)],
        out_shape=[jax.ShapeDtypeStruct((width, columns), BF), f32(1, width), f32(1, width)],
        scratch_shapes=[pltpu.VMEM((columns, 1), F32)],
        compiler_params=pltpu.CompilerParams(vmem_limit_bytes=48 * 1024 * 1024),
        cost_estimate=pl.CostEstimate(
            flops=2 * rows * width * columns,
            transcendentals=0,
            bytes_accessed=2 * (rows * width + rows * columns + 2 * width * columns),
        ),
    )(core, grad, weight_t, scale, shift)


def norm_rows_kernel(rows_ref, core_ref, places_ref):
    rows = core_ref.shape[0] // 2
    for part in (0, 1):
        start = part * (rows + 8)
        values = rows_ref[start : start + rows].astype(F32)
        square = jnp.mean(values * values, axis=-1, keepdims=True)
        core_ref[part * rows : (part + 1) * rows] = (values * lax.rsqrt(square + EPSILON)).astype(BF)
        places_ref[0, part] = rows_ref[start + rows : start + rows + 8, :rows].astype(F32)


def norm_rows(blocks, rows):
    width = blocks.shape[1]
    pair = 2 * (rows + 8)
    count = blocks.shape[0] // pair
    return pl.pallas_call(
        norm_rows_kernel,
        grid=(count,),
        in_specs=[pl.BlockSpec((pair, width), lambda i: (i, 0))],
        out_specs=[
            pl.BlockSpec((2 * rows, width), lambda i: (i, 0)),
            pl.BlockSpec((1, 2, 8, rows), lambda i: (i, 0, 0, 0)),
        ],
        out_shape=[
            jax.ShapeDtypeStruct((2 * count * rows, width), BF),
            f32(count, 2, 8, rows),
        ],
        compiler_params=pltpu.CompilerParams(vmem_limit_bytes=32 * 1024 * 1024),
    )(blocks)


def by_query(rows, block, first=0):
    return pl.BlockSpec((1, rows, block), lambda h, i: (h + first, 0, i))


def whole_head(rows, columns, first=0):
    return pl.BlockSpec((1, rows, columns), lambda h, i: (h + first, 0, 0))


def mask_spec(rows):
    return pl.BlockSpec((rows, 1), lambda h, i: (0, 0))


def f32(*shape):
    return jax.ShapeDtypeStruct(shape, F32)


def query_block(rows, keys, most):
    block = rows
    while block > 128 and block * keys > most:
        block //= 2
    return block


def attention_cost(scores, products, heads=1):
    return pl.CostEstimate(
        flops=heads * scores * products * 2 * 256,
        transcendentals=heads * scores,
        bytes_accessed=heads * scores // 2,
    )


def one_head(kernel, head, kept, inputs, in_specs, out_specs, out_shape, scratch, steps, cost):
    extra = len(kept) if kept else 0

    def body(*refs):
        kernel(*refs[: len(inputs)], *refs[len(inputs) + extra :])

    return pl.pallas_call(
        body,
        grid=(1, steps),
        in_specs=in_specs + [pl.BlockSpec(memory_space=pl.ANY)] * extra,
        out_specs=out_specs,
        out_shape=out_shape,
        scratch_shapes=scratch,
        input_output_aliases={len(inputs) + i: i for i in range(extra)},
        compiler_params=KERNEL,
        cost_estimate=cost,
    )(*inputs, *(kept or ()))


def self_forward(q, k, v, head, kept):
    heads, dim, rows = q.shape
    keys = k.shape[2]
    block = query_block(rows, keys, 1 << 21)
    return one_head(
        self_forward_kernel,
        head,
        kept,
        (q, k, v),
        [by_query(dim, block, head), whole_head(dim, keys, head), whole_head(dim, keys, head)],
        [by_query(dim, block, head), by_query(1, block, head)],
        [f32(heads, dim, rows), f32(heads, 1, rows)],
        [pltpu.VMEM((keys, dim), BF)],
        rows // block,
        attention_cost(rows * keys, 2),
    )


def self_backward(q, g, log_total, delta, k, v, head, kept):
    heads, dim, rows = q.shape
    keys = k.shape[2]
    block = query_block(rows, keys, 1 << 20)
    return one_head(
        self_backward_kernel,
        head,
        kept,
        (q, g, log_total, delta, k, v),
        [by_query(dim, block, head)] * 2
        + [by_query(1, block, head)] * 2
        + [whole_head(dim, keys, head)] * 2,
        [by_query(dim, block, head), whole_head(dim, keys, head), whole_head(dim, keys, head)],
        [f32(heads, dim, rows), f32(heads, dim, keys), f32(heads, dim, keys)],
        [pltpu.VMEM((keys, dim), t) for t in (BF, BF, F32, F32)],
        rows // block,
        attention_cost(rows * keys, 5),
    )


def cross_forward(q, k, v, mask):
    heads, dim, rows = q.shape
    keys = k.shape[2]
    block = query_block(rows, keys, 1 << 19)
    return pl.pallas_call(
        cross_forward_kernel,
        grid=(heads, rows // block),
        in_specs=[
            by_query(dim, block),
            whole_head(dim, keys),
            whole_head(dim, keys),
            mask_spec(keys),
        ],
        out_specs=by_query(dim, block),
        out_shape=f32(heads, dim, rows),
        compiler_params=KERNEL,
        cost_estimate=attention_cost(rows * keys, 2, heads),
    )(q, k, v, mask)


def cross_backward(q, g, k, v, mask, gate):
    heads, dim, rows = q.shape
    keys = k.shape[2]
    block = query_block(rows, keys, 1 << 19)
    return pl.pallas_call(
        cross_backward_kernel,
        grid=(heads, rows // block),
        in_specs=[
            by_query(dim, block),
            by_query(dim, block),
            whole_head(dim, keys),
            whole_head(dim, keys),
            mask_spec(keys),
            whole_head(8, 128),
        ],
        out_specs=[
            by_query(dim, block),
            whole_head(dim, keys),
            whole_head(dim, keys),
            by_query(1, block),
        ],
        out_shape=[
            f32(heads, dim, rows),
            f32(heads, dim, keys),
            f32(heads, dim, keys),
            f32(heads, 1, rows),
        ],
        compiler_params=KERNEL,
        cost_estimate=attention_cost(rows * keys, 5, heads),
    )(q, g, k, v, mask, gate)


def halves(block):
    half = block.shape[0] // 2
    return block[:half], block[half:]


def pick(block, index, dim=0, keep=False):
    return lax.dynamic_index_in_dim(block, index, dim, keepdims=keep)


def both_sides(block, axis, bit, dim):
    other = swap(block, axis)
    return jnp.where(bit == 0, jnp.stack([block, other], dim), jnp.stack([other, block], dim))


def kept_sum(block, axis, bit, dim):
    other = swap(pick(block, 1 - bit, dim).astype(BF), axis)
    return pick(block, bit, dim).astype(F32) + other.astype(F32)


def team_sum(values):
    for axis in TEAM:
        values = values + swap(values, axis)
    return values


def chips_first(first, second, bits):
    return kept_sum(first, "tz", bits[0], 0), kept_sum(second, "ty", bits[1], 1)


def chips_last(first, second, bits):
    return kept_sum(first, "ty", bits[1], 0), kept_sum(second, "tz", bits[0], 0)


def row_factor(values):
    return lax.rsqrt(jnp.mean(values * values, axis=-1, keepdims=True) + EPSILON)


def rope_tables(places, head_dim):
    pair_count = head_dim // 2
    lead_pairs = pair_count // 4
    mid_pairs = (pair_count - lead_pairs) // 2
    last_pairs = pair_count - lead_pairs - mid_pairs
    angles = []
    for which, extent in enumerate((lead_pairs, mid_pairs, last_pairs)):
        offsets = jnp.arange(extent, dtype=F32)
        angles.append(jnp.power(10000.0, -offsets / extent)[:, None] * places[which][None])
    angles = join(angles)
    cosine, sine = jnp.cos(angles), jnp.sin(angles)
    return join([cosine, cosine]), join([-sine, sine])


def turn(vectors, cosine, sine):
    half = vectors.shape[1] // 2
    crossed = join([vectors[:, half:], vectors[:, :half]], axis=1)
    return vectors * cosine + crossed * sine


def on_device(
    tokens,
    condition,
    caption,
    caption_lengths,
    positions,
    modulation_weight,
    modulation_bias,
    norm_gains,
    cross_gate,
    input_weight,
    output_weight,
    caption_key_weight,
    caption_value_weight,
    gate_weight,
    up_weight,
    down_weight,
    cotangent,
):
    clips_here, clip_rows, width = tokens.shape
    head_count = cross_gate.shape[0]
    head_dim = width // head_count
    scale = head_dim ** (-0.5)
    team = 8
    heads = head_count // team
    rows_in = input_weight.shape[0]
    part = heads * head_dim
    groups = lax.axis_size(GROUPS)
    reps = lax.axis_size("rep")
    half = lax.axis_index("half")
    bits = tuple(lax.axis_index(axis) for axis in SHARDS)
    rank = lax.axis_index(TEAM)
    clip_pair = lax.axis_index("clip")
    device = lax.axis_index(EVERY)

    def own_clip(block):
        return pick(block, half), swap(pick(block, 1 - half), "half")

    def back_clip(block):
        rows = block.shape[0] // 2
        kept, other = block[:rows], block[rows:]
        other = swap(other.astype(BF), "half").astype(block.dtype)
        return jnp.where(half == 0, jnp.stack([kept, other]), jnp.stack([other, kept]))

    def own_columns(table):
        return lax.dynamic_slice_in_dim(table, rank * part, part, table.ndim - 1)

    def by_rank(weight, split, by_shard=False):
        rows = weight.shape[0]
        if by_shard:
            tiled = weight.reshape(rows, split, team, -1)
            return jnp.transpose(tiled, (2, 0, 1, 3)).reshape(team, rows, -1)
        tiled = weight.reshape(rows, split, 2, 2, 2, -1)
        return jnp.transpose(tiled, (3, 4, 2, 0, 1, 5)).reshape(team, rows, -1)

    def from_team(blocks):
        mine = lax.all_to_all(blocks, SHARDS, split_axis=0, concat_axis=0, tiled=True)
        return mine.reshape(-1, blocks.shape[2])

    def all_reps(block):
        return lax.all_gather(block, "rep", axis=0, tiled=True) if reps > 1 else block

    def across_half(block):
        return both_sides(all_reps(block), "half", half, 0)

    def across_clip(block):
        return both_sides(block, "clip", clip_pair, 0).reshape(-1, block.shape[-1])

    places = jnp.pad(
        jnp.transpose(positions, (1, 0, 2)).astype(BF),
        ((0, 0), (0, 5), (0, width - clip_rows)),
    )
    rows_a, rows_b = own_clip(join([tokens, places], axis=1))
    in_team = from_team(by_rank(input_weight, 3))
    shard_rows = modulation_weight.shape[0]
    silu_all = jax.nn.silu(condition).astype(BF)
    silu_rows = lax.dynamic_slice_in_dim(silu_all, device * shard_rows, shard_rows, 1)
    mod_part = dot(silu_rows, modulation_weight, 1, 0)
    mod_part = mod_part.reshape(lax.axis_size("clip"), clips_here, -1)
    mod_pair = pick(mod_part, clip_pair) + swap(pick(mod_part, 1 - clip_pair), "clip")
    mod_own = pick(mod_pair, half, keep=True) + swap(pick(mod_pair, 1 - half, keep=True), "half")
    rows_a, rows_b, mod_own, in_team = together(rows_a, rows_b, mod_own, in_team)

    rows_all = lax.all_gather(join([rows_a, rows_b]), TEAM, axis=0, tiled=True)
    in_half = across_half(in_team).reshape(-1, 3 * part)
    if reps > 1:
        mod_own = lax.psum(mod_own, "rep")
    mod_own = team_sum(mod_own)
    in_half, mod_own, caption, cotangent = together(in_half, mod_own, caption, cotangent)

    in_other = swap(in_half, "clip")
    rows_cap = caption_key_weight.shape[0]
    slots_here = caption.shape[1]
    cap_a, cap_b = own_clip(caption)
    cot_a, cot_b = own_clip(cotangent)
    modulation = mod_own + modulation_bias
    shift_attn, scale_attn, gate_attn, shift_ffn, scale_ffn, gate_ffn = (
        modulation[:, i * width : (i + 1) * width] for i in range(6)
    )
    token_vals = join([rows_a[:clip_rows], rows_b[:clip_rows]]).astype(F32)
    rows_here = token_vals.shape[0]
    team_rows = team * rows_here
    row_scale = (norm_gains[0] * (1.0 + scale_attn)).reshape(width, 1)
    row_shift = shift_attn.reshape(width, 1)
    w_in, w_scaled, bias = place_weight(clip_pair, in_half, in_other, row_scale, row_shift)
    bias = bias.reshape(3 * part, 1)
    w_scaled, bias, rows_all, cap_a, cap_b, out_shard, ckey_weight, cvalue_weight = together(
        w_scaled,
        bias,
        rows_all,
        cap_a,
        cap_b,
        output_weight,
        caption_key_weight,
        caption_value_weight,
    )
    cap_team = from_team(join([by_rank(ckey_weight, 1), by_rank(cvalue_weight, 1)], axis=2))
    w_out = across_half(out_shard)
    cap_rows = jnp.where(half == 0, join([cap_a, cap_b]), join([cap_b, cap_a]))
    core_all, all_places = norm_rows(rows_all, clip_rows)
    all_places = jnp.transpose(all_places[:, :, :3], (2, 0, 1, 3)).reshape(3, team_rows)

    def by_head(block):
        return block.reshape(heads, head_dim, block.shape[-1])

    raw_qk = dot(w_scaled[:, : 2 * part], core_all, 0, 1) + bias[: 2 * part]
    raw_qk = raw_qk.reshape(2, heads, head_dim, team_rows)
    squares = jnp.sum(raw_qk * raw_qk, axis=(1, 2))
    squares, raw_qk, cap_team, cap_rows, cot_a, cot_b, w_out = together(
        team_sum(squares), raw_qk, cap_team, cap_rows, cot_a, cot_b, w_out
    )
    cap_half = across_half(cap_team)
    cap_all = lax.all_gather(cap_rows, TEAM, axis=0, tiled=True)
    w_out = both_sides(w_out, "clip", clip_pair, 0).reshape(-1, width)
    factors = lax.rsqrt(squares / width + EPSILON)[:, None, None]
    cosine, sine = rope_tables(all_places, head_dim)
    values = by_head((dot(w_scaled[:, 2 * part :], core_all, 0, 1) + bias[2 * part :]).astype(BF))
    gains = jnp.stack([own_columns(norm_gains[i]) for i in (1, 2, 3)])
    gains = gains.reshape(3, heads, head_dim, 1)
    normed_qk = raw_qk * factors
    turned = normed_qk * gains[:2]
    queries = (turn(turned[0], cosine, sine) * scale).astype(BF)
    keys = turn(turned[1], cosine, sine).astype(BF)
    all_keys, all_values = keys, values
    if reps > 1:
        all_keys, all_values = (lax.all_gather(v, "rep", axis=2, tiled=True) for v in (keys, values))

    queries, all_keys, all_values, gate_shard, up_shard, w_out, w_in_t = together(
        queries, all_keys, all_values, gate_weight, up_weight, w_out, jnp.transpose(w_in)
    )
    w_out = lax.all_gather(w_out, SHARDS, axis=0, tiled=True)
    ff_block = down_weight.shape[0]
    ff_part = groups * ff_block
    up_team = from_team(
        join([by_rank(gate_shard, groups, True), by_rank(up_shard, groups, True)], axis=2)
    )
    o_self, logs = self_forward(queries, all_keys, all_values, 0, None)
    o_self, logs = self_forward(queries, all_keys, all_values, 1, (o_self, logs))
    o_self, logs, cap_half, up_team, cap_all = together(o_self, logs, cap_half, up_team, cap_all)
    w_cap = across_clip(cap_half)
    grad_out = join([cot_a, cot_b]).astype(F32)
    d_ffn = (gate_ffn * grad_out).astype(BF)
    d_ffn_all = lax.all_gather(d_ffn, TEAM, axis=0, tiled=True)
    up_half = across_half(up_team)
    o_self, logs = self_forward(queries, all_keys, all_values, 2, (o_self, logs))
    o_self, w_cap, up_half, down_shard = together(o_self, w_cap, up_half, down_weight)
    w_gate_up = across_clip(up_half)
    down_half = across_half(down_shard)
    craw = dot(w_cap, cap_all, 0, 1)
    craw_key = by_head(craw[:part])
    square_c = jnp.sum(craw_key * craw_key, axis=(0, 1))[None]
    square_c = team_sum(square_c)
    factor_c = lax.rsqrt(square_c / width + EPSILON)[None]
    normed_c = craw_key * factor_c
    ckeys = (normed_c * gains[2]).astype(BF)
    cvalues = by_head(craw[part:]).astype(BF)
    all_ckeys, all_cvalues = ckeys, cvalues
    step = lax.axis_index("rep")
    order = jnp.arange(team * clips_here * slots_here, dtype=jnp.int32)
    in_rank = order // slots_here % clips_here
    from_rank = order // (slots_here * clips_here)
    from_shard = from_rank % 4 * 2 + from_rank // 4
    slots = ((in_rank * reps + step) * team + from_shard) * slots_here + order % slots_here
    if reps > 1:
        all_ckeys, all_cvalues = (
            lax.all_gather(v, "rep", axis=2, tiled=True) for v in (ckeys, cvalues)
        )
        slots = join([slots + (r - step) * team * slots_here for r in range(reps)])
    mask = jnp.where(slots < pick(caption_lengths, half), 0.0, NEGATIVE).astype(F32)[:, None]
    o_cross = cross_forward(queries, all_ckeys, all_cvalues, mask)
    tanh_gate = jnp.tanh(lax.dynamic_slice_in_dim(cross_gate, rank * heads, heads))
    tanh_wide = tanh_gate[:, None, None]
    mixed = (o_self + tanh_wide * o_cross).astype(BF).reshape(part, team, rows_here)
    mixed, w_out, down_half = together(jnp.transpose(mixed, (1, 0, 2)), w_out, down_half)
    w_down = across_clip(down_half)
    mixed = lax.all_to_all(mixed, TEAM, split_axis=0, concat_axis=0, tiled=True)
    out_rows = output_weight.shape[0]

    def by_shard(features):
        tiled = features.reshape(groups, team, out_rows, -1)
        return jnp.transpose(tiled, (1, 0, 2, 3)).reshape(width, -1)

    def by_group(features):
        tiled = features.reshape(team, groups, out_rows, -1)
        return jnp.transpose(tiled, (1, 0, 2, 3)).reshape(width, -1)

    combined = by_shard(mixed.reshape(width, rows_here))

    branch = dot(combined, w_out, 0, 0)
    middle = token_vals + gate_attn * branch
    factor_f = row_factor(middle)
    core_f = middle * factor_f
    ffn_in = (core_f * norm_gains[4] * (1.0 + scale_ffn) + shift_ffn).astype(BF)
    ffn_in, w_down, d_ffn_all = together(ffn_in, w_down, d_ffn_all)
    ffn_all = lax.all_gather(ffn_in, TEAM, axis=0, tiled=True)
    w_gate_up, w_down, ffn_all = together(w_gate_up, w_down, ffn_all)
    gate_up = dot(ffn_all, w_gate_up, 1, 0)
    gate_vals, up_vals = gate_up[:, :ff_part], gate_up[:, ff_part:]
    d_hidden = dot(d_ffn_all, w_down, 1, 1)
    sig = jax.nn.sigmoid(gate_vals)
    silu_gate = gate_vals * sig
    hidden = (silu_gate * up_vals).astype(BF)
    d_gate = (d_hidden * up_vals * (sig + silu_gate * (1.0 - sig))).astype(BF)
    d_up = (d_hidden * silu_gate).astype(BF)
    d_gate_up = join([d_gate, d_up], axis=1)

    def core_side(block, which, dim=0):
        count = block.shape[dim] // 2
        return lax.dynamic_slice_in_dim(block, which * count, count, dim)

    def ffn_side(which):
        return dot(core_side(d_gate_up, which), w_gate_up, 1, 1).astype(BF)

    def by_chip(mine):
        tiled = mine.reshape(2, 2, 2, clip_rows, width)
        return tiled[:, :, 0], tiled[:, :, 1]

    def add_core(kept, sent):
        return (kept.astype(F32) + swap(sent, "tc").astype(F32)).astype(BF)

    def team_parts(slice_grad):
        tiled = slice_grad.reshape(lax.axis_size("clip"), clips_here, -1, slice_grad.shape[-1])
        return kept_sum(tiled, "clip", clip_pair, 0).astype(BF)

    def half_parts(tiled):
        summed = kept_sum(tiled, "half", half, 0)
        if reps > 1:
            summed = lax.psum_scatter(summed, "rep", scatter_dimension=0, tiled=True)
        return summed

    def to_shards(summed):
        ranked = summed.astype(BF).reshape(team, -1, summed.shape[-1])
        return lax.all_to_all(ranked, SHARDS, split_axis=0, concat_axis=0, tiled=True)

    def head_columns(blocks, split):
        rows = blocks.shape[1]
        tiled = blocks.reshape(2, 2, 2, rows, split, part)
        return jnp.transpose(tiled, (3, 4, 2, 0, 1, 5)).reshape(rows, -1).astype(F32)

    def ff_columns(blocks):
        rows = blocks.shape[1]
        tiled = blocks.reshape(team, rows, groups, ff_block)
        return jnp.transpose(tiled, (1, 2, 0, 3)).reshape(rows, -1).astype(F32)

    def all_parts(slice_grad):
        return lax.psum_scatter(slice_grad, GROUPS, scatter_dimension=0, tiled=True)

    side_sent = ffn_side(1 - bits[2])
    mine = add_core(ffn_side(bits[2]), side_sent)
    pair = chips_first(*by_chip(mine), bits)
    grad_down = dot(after(hidden, mine), d_ffn_all, 0, 0).astype(BF)
    *pair, grad_down = together(*pair, grad_down)
    d_ffn_in = join(chips_last(*pair, bits))
    late_hidden = after(hidden, grad_down)
    out_sent = dot(core_side(late_hidden, 1 - bits[2]), w_down, 1, 0).astype(BF)
    out_kept = dot(core_side(late_hidden, bits[2]), w_down, 1, 0).astype(BF)
    d_ffn_in, out_sent, out_kept = together(d_ffn_in, out_sent, out_kept)

    out_mine = add_core(out_kept, out_sent)
    down_half = team_parts(after(grad_down, d_ffn_in))
    d_shift_ffn = jnp.sum(d_ffn_in, axis=0, keepdims=True)
    moment_f = jnp.sum(d_ffn_in * core_f, axis=0, keepdims=True)
    d_scale_ffn = moment_f * norm_gains[4]
    d_gain_ffn = moment_f * (1.0 + scale_ffn)
    d_core = d_ffn_in * (norm_gains[4] * (1.0 + scale_ffn))
    d_middle = grad_out + factor_f * (
        d_core - core_f * jnp.mean(d_core * core_f, axis=-1, keepdims=True)
    )
    d_branch = (gate_attn * d_middle).astype(BF)
    d_gate_attn = jnp.sum(d_middle * branch, axis=0, keepdims=True)
    d_combined = by_group(dot(w_out, d_branch, 1, 1).astype(BF))
    d_mixed = lax.all_to_all(
        d_combined.reshape(team, part, rows_here), TEAM, split_axis=0, concat_axis=0, tiled=True
    )
    late_ffn, late_gate, out_mine = together(ffn_all, d_gate_up, out_mine, d_combined)[:3]
    grad_gate_up = dot(late_ffn, late_gate, 0, 0).astype(BF)
    d_mixed, grad_gate_up = together(d_mixed, grad_gate_up)
    up_rows = all_parts(grad_gate_up)
    d_self = by_head(jnp.transpose(d_mixed, (1, 0, 2)).reshape(part, team_rows))

    out_pair = chips_first(*by_chip(out_mine), bits)
    gate_tile = jnp.broadcast_to(tanh_wide, (heads, 8, 128))
    dq_cross, d_ckeys, d_cvalues, gate_rows = cross_backward(
        queries, d_self, all_ckeys, all_cvalues, mask, gate_tile
    )
    d_cross_gate = jnp.sum(gate_rows, axis=(1, 2)) * (1.0 - tanh_gate * tanh_gate)
    if reps > 1:
        d_ckeys, d_cvalues = (
            lax.psum_scatter(v, "rep", scatter_dimension=2, tiled=True)
            for v in (d_ckeys, d_cvalues)
        )

    def team_mean(block):
        return jnp.sum(block, axis=(-3, -2))

    scaled_c = d_ckeys * gains[2]
    mean_c = team_mean(scaled_c * normed_c)[None]
    mean_c = mean_c + swap(mean_c, "tc")
    grad_output = dot(after(combined, dq_cross), d_branch, 1, 0).astype(BF)
    delta = jnp.sum(d_self.astype(F32) * o_self, axis=1, keepdims=True)
    delta, grad_output, mean_c, down_half, *out_pair = together(
        delta, grad_output, mean_c, down_half, *out_pair
    )
    sum_down = half_parts(down_half)
    sum_output = lax.psum_scatter(grad_output, SHARDS, scatter_dimension=0, tiled=True)
    ffn_out = join(chips_last(*out_pair, bits))
    mean_c = mean_c + swap(mean_c, "ty")
    mean_c = mean_c + swap(mean_c, "tz")
    backs = self_backward(queries, d_self, logs, delta, all_keys, all_values, 0, None)
    *backs, delta, mean_c, ffn_out = together(*backs, delta, mean_c, ffn_out)
    result = back_clip((middle + gate_ffn * ffn_out).astype(BF))
    d_gate_ffn = jnp.sum(grad_out * ffn_out, axis=0, keepdims=True)
    mean_c = mean_c[None] / width
    d_craw = factor_c * (scaled_c - normed_c * mean_c)
    d_gain_c = jnp.sum(d_ckeys * normed_c, axis=2).reshape(1, part)
    cap_low = join([d_craw, d_cvalues]).reshape(2 * part, -1).astype(BF)
    cap_half = team_parts(dot(cap_all, cap_low, 0, 1).astype(BF))
    d_cap = dot(cap_low, w_cap, 0, 1).astype(BF)
    d_cap = d_cap.reshape(2, 2, 2, clips_here * slots_here, -1)
    d_cap = kept_sum(d_cap, "tc", bits[2], 0).astype(BF)
    backs = self_backward(queries, d_self, logs, delta, all_keys, all_values, 1, backs)
    *backs, delta, up_rows, sum_down, d_cap, cap_half = together(
        *backs, delta, up_rows, sum_down, d_cap, cap_half
    )
    cap_rows = half_parts(cap_half)
    d_cap = kept_sum(d_cap, "tz", bits[0], 0).astype(BF)
    sum_gate_up = to_shards(up_rows)
    backs = self_backward(queries, d_self, logs, delta, all_keys, all_values, 2, backs)
    *backs, result, sum_gate_up, d_cap = together(*backs, result, sum_gate_up, d_cap)
    d_cap = kept_sum(d_cap, "ty", bits[1], 0).astype(BF)
    dq_self, dk, dv = backs
    if reps > 1:
        dk, dv = (lax.psum_scatter(v, "rep", scatter_dimension=2, tiled=True) for v in (dk, dv))

    turned_grad = jnp.stack(
        [turn((dq_self + dq_cross) * scale, cosine, -sine), turn(dk, cosine, -sine)]
    )
    scaled_qk = turned_grad * gains[:2]
    mean_qk = team_sum(team_mean(scaled_qk * normed_qk))[:, None, None] / width
    d_gain_qk = jnp.sum(turned_grad * normed_qk, axis=3).reshape(2, part)
    d_qk = (factors * (scaled_qk - normed_qk * mean_qk)).reshape(2 * part, team_rows)
    d_projected = join([d_qk, dv.reshape(part, team_rows)]).astype(BF)

    def attn_side(which):
        return dot(core_side(d_projected, which, 1), w_in, 0, 1).astype(BF)

    side_sent = attn_side(1 - bits[2])
    mine = add_core(attn_side(bits[2]), side_sent)
    in_grad, moment_a, d_shift_attn = input_grad(
        core_all, d_projected, w_in_t, row_scale.reshape(1, width), row_shift.reshape(1, width)
    )
    mine, in_grad, cap_rows = together(mine, in_grad, cap_rows)
    in_half = team_parts(in_grad)
    pair = chips_first(*by_chip(mine), bits)
    d_scale_attn = moment_a * norm_gains[0]
    d_gain_attn = moment_a * (1.0 + scale_attn)

    def placed(values):
        wide = jnp.tile(values, (1, width // values.shape[1]))
        spot = jnp.arange(width, dtype=jnp.int32) // values.shape[1]
        return jnp.where(spot == rank, wide, 0.0)

    gate_row = jnp.pad(d_cross_gate[None], ((0, 0), (0, width // team - heads)))
    sums = join(
        [
            d_shift_attn,
            d_scale_attn,
            d_gate_attn,
            d_shift_ffn,
            d_scale_ffn,
            d_gate_ffn,
            d_gain_attn,
            d_gain_ffn,
            placed(join([d_gain_qk, d_gain_c, gate_row])),
        ]
    )
    for axis in ("tc", "ty"):
        sums = sums + swap(sums, axis)
    sums = both_sides(sums, "clip", clip_pair, 0)
    *pair, sums, in_half = together(*pair, sums, in_half)
    in_rows = half_parts(in_half)
    d_attn_in = join(chips_last(*pair, bits))
    sum_output = after(sum_output, *pair).reshape(lax.axis_size("clip"), clips_here, -1, width)
    sum_output = kept_sum(sum_output, "clip", clip_pair, 0)
    sums = sums + swap(sums, "tz")
    if reps > 1:
        sums = lax.psum(sums, "rep")
    sums = both_sides(sums, "half", half, 1)
    d_attn_in, sums, sum_gate_up = together(d_attn_in, sums, sum_gate_up)
    sum_gate, sum_up = ff_columns(sum_gate_up[..., :ff_part]), ff_columns(sum_gate_up[..., ff_part:])
    sum_cap = to_shards(cap_rows)
    factor_a = row_factor(token_vals)
    core_a = token_vals * factor_a
    d_core = d_attn_in * (norm_gains[0] * (1.0 + scale_attn))
    d_tokens = back_clip(
        d_middle
        + factor_a * (d_core - core_a * jnp.mean(d_core * core_a, axis=-1, keepdims=True))
    )
    mod_low = sums[:, :, :6].astype(BF).reshape(condition.shape[0], -1)
    small = jnp.sum(sums[:, :, 6:], axis=(0, 1))
    gain_sum = join([small[:1], small[2:5], small[1:2]])
    gate_sum = small[5].reshape(team, -1)[:, :heads].reshape(-1)
    d_bias = jnp.sum(mod_low.astype(F32), axis=0)
    d_silu = dot(mod_low, modulation_weight, 1, 1)
    d_silu = lax.dynamic_update_slice_in_dim(
        jnp.zeros(condition.shape, F32), d_silu, device * shard_rows, 1
    )
    sum_input = to_shards(in_rows)
    if reps > 1:
        d_silu = lax.psum(d_silu, "rep")
    for axis in ("tc", "ty", "tz", "half", "clip"):
        d_silu = d_silu + swap(d_silu, axis)
    _, silu_back = jax.vjp(jax.nn.silu, condition)
    d_condition = silu_back(d_silu)[0]
    grad_mod = dot(silu_rows, mod_low, 0, 0)

    sum_input = head_columns(sum_input, 3)
    sum_ckey = head_columns(sum_cap[..., :part], 1)
    sum_cvalue = head_columns(sum_cap[..., part:], 1)
    sum_output = half_parts(after(sum_output, d_attn_in))
    d_cap = after(d_cap, d_attn_in).astype(F32)
    d_cap = d_cap.reshape(clips_here, slots_here, -1)
    d_caption = back_clip(join([pick(d_cap, half), pick(d_cap, 1 - half)]))
    return (
        result,
        d_tokens,
        d_caption,
        d_condition,
        grad_mod,
        d_bias,
        gain_sum,
        gate_sum,
        sum_input,
        sum_output,
        sum_ckey,
        sum_cvalue,
        sum_gate,
        sum_up,
        sum_down,
    )


def solution(mesh):
    clip_count, seq_count = mesh.shape["clip"], mesh.shape["seq"]

    def program(*arrays):
        halves = arrays[0].shape[0] // clip_count
        shape = (clip_count, halves, seq_count // (halves * 8), 2, 2, 2)
        fine = Mesh(mesh.devices.reshape(shape), EVERY)
        rows = P("clip", SEQ, None)
        shard = P(EVERY, None)
        mapped = jax.shard_map(
            on_device,
            mesh=fine,
            in_specs=(
                rows,
                P(),
                rows,
                P("clip"),
                P(None, "clip", SEQ),
                shard,
                P(),
                P(),
                P(),
                shard,
                shard,
                shard,
                shard,
                shard,
                shard,
                shard,
                rows,
            ),
            out_specs=(rows, rows, rows, P(), shard, P(), P(), P()) + (shard,) * 7,
            check_vma=False,
        )
        return mapped(*arrays)

    return program
```

```python
import jax
import jax.numpy as jnp
from jax import lax
from jax.experimental import pallas as pl
from jax.experimental.pallas import tpu as pltpu
from jax.sharding import Mesh
from jax.sharding import PartitionSpec as P

EPSILON = 1e-06
NEGATIVE = -1e30
BF = jnp.bfloat16
F32 = jnp.float32
SEQ = ("half", "rep", "tz", "ty", "tc")
GROUPS = ("clip", "half", "rep")
TEAM = ("tc", "tz", "ty")
SHARDS = ("tz", "ty", "tc")
EVERY = ("clip",) + SEQ
KERNEL = pltpu.CompilerParams(
    vmem_limit_bytes=56 * 1024 * 1024, dimension_semantics=("arbitrary", "arbitrary")
)


def swap(block, axis):
    return lax.ppermute(block, axis, [(0, 1), (1, 0)])


def together(*values):
    return lax.optimization_barrier(values)


def after(value, *others):
    return lax.optimization_barrier((value,) + others)[0]


def dot(left, right, left_dim, right_dim):
    dims = (((left_dim,), (right_dim,)), ((), ()))
    return lax.dot_general(left, right, dims, preferred_element_type=F32)


def join(parts, axis=0):
    return jnp.concatenate(parts, axis=axis)


def upright(block):
    return jnp.transpose(block.astype(F32)).astype(BF)


def self_forward_kernel(q_ref, k_ref, v_ref, o_ref, log_ref, k_rows):
    @pl.when(pl.program_id(1) == 0)
    def _():
        k_rows[...] = upright(k_ref[0])

    scores = dot(k_rows[...], q_ref[0], 1, 0)
    peak = jnp.max(scores, axis=0, keepdims=True)
    weights = jnp.exp(scores - peak)
    total = jnp.sum(weights, axis=0, keepdims=True)
    o_ref[0] = dot(v_ref[0], weights.astype(BF), 1, 0) / total
    log_ref[0] = peak + jnp.log(total)


def self_backward_kernel(
    q_ref, g_ref, log_ref, delta_ref, k_ref, v_ref, dq_ref, dk_ref, dv_ref, k_rows, v_rows, dk, dv
):
    step = pl.program_id(1)

    @pl.when(step == 0)
    def _():
        k_rows[...] = upright(k_ref[0])
        v_rows[...] = upright(v_ref[0])
        dk[...] = jnp.zeros_like(dk)
        dv[...] = jnp.zeros_like(dv)

    q, g = q_ref[0], g_ref[0]
    probs = jnp.exp(dot(k_rows[...], q, 1, 0) - log_ref[0])
    ds = (probs * (dot(v_rows[...], g, 1, 0) - delta_ref[0])).astype(BF)
    dv[...] += dot(probs.astype(BF), g, 1, 1)
    dk[...] += dot(ds, q, 1, 1)
    dq_ref[0] = dot(k_ref[0], ds, 1, 0)

    @pl.when(step == pl.num_programs(1) - 1)
    def _():
        dk_ref[0] = jnp.transpose(dk[...])
        dv_ref[0] = jnp.transpose(dv[...])


def cross_forward_kernel(q_ref, k_ref, v_ref, mask_ref, o_ref):
    scores = dot(upright(k_ref[0]), q_ref[0], 1, 0) + mask_ref[...]
    weights = jnp.exp(scores - jnp.max(scores, axis=0, keepdims=True))
    total = jnp.sum(weights, axis=0, keepdims=True)
    o_ref[0] = dot(v_ref[0], weights.astype(BF), 1, 0) / total


def cross_backward_kernel(
    q_ref, g_ref, k_ref, v_ref, mask_ref, gate_ref, dq_ref, dk_ref, dv_ref, dg_ref
):
    q, g, gate = q_ref[0], g_ref[0], gate_ref[0, 0:1, 0:1]
    scores = dot(upright(k_ref[0]), q, 1, 0) + mask_ref[...]
    weights = jnp.exp(scores - jnp.max(scores, axis=0, keepdims=True))
    probs = weights / jnp.sum(weights, axis=0, keepdims=True)
    dp = dot(upright(v_ref[0]), g, 1, 0)
    inner = jnp.sum(probs * dp, axis=0, keepdims=True)
    ds = (probs * (gate * (dp - inner))).astype(BF)
    dg_ref[0] = inner
    dq_ref[0] = dot(k_ref[0], ds, 1, 0)
    dk = dot(q, ds, 1, 1)
    dv = dot(g, probs.astype(BF), 1, 1) * gate

    @pl.when(pl.program_id(1) == 0)
    def _():
        dk_ref[0] = dk
        dv_ref[0] = dv

    @pl.when(pl.program_id(1) > 0)
    def _():
        dk_ref[0] += dk
        dv_ref[0] += dv


def place_weight_kernel(bit_ref, mine_ref, other_ref, scale_ref, shift_ref, w_ref, scaled_ref, bias_ref):
    step = pl.program_id(0)

    def run(ref):
        values = ref[...].astype(F32)
        w_ref[...] = ref[...]
        scaled_ref[...] = (values * scale_ref[...]).astype(BF)
        bias = jnp.sum(values * shift_ref[...], axis=0, keepdims=True)

        @pl.when(step == 0)
        def _():
            bias_ref[...] = bias

        @pl.when(step > 0)
        def _():
            bias_ref[...] += bias

    @pl.when(step == bit_ref[0])
    def _():
        run(mine_ref)

    @pl.when(step != bit_ref[0])
    def _():
        run(other_ref)


def place_weight(bit, mine, other, scale, shift):
    rows, columns = mine.shape
    part = pl.BlockSpec((rows, columns), lambda i: (0, 0))
    out = pl.BlockSpec((rows, columns), lambda i: (i, 0))
    column = pl.BlockSpec((rows, 1), lambda i: (i, 0))
    return pl.pallas_call(
        place_weight_kernel,
        grid=(2,),
        in_specs=[pl.BlockSpec(memory_space=pltpu.SMEM), part, part, column, column],
        out_specs=[out, out, pl.BlockSpec((1, columns), lambda i: (0, 0))],
        out_shape=[
            jax.ShapeDtypeStruct((2 * rows, columns), BF),
            jax.ShapeDtypeStruct((2 * rows, columns), BF),
            f32(1, columns),
        ],
        compiler_params=pltpu.CompilerParams(vmem_limit_bytes=48 * 1024 * 1024),
    )(jnp.reshape(bit, (1,)).astype(jnp.int32), mine, other, scale, shift)


def input_grad_kernel(
    core_ref, grad_ref, w_ref, scale_ref, shift_ref, out_ref, moment_ref, sum_ref, column_sum
):
    @pl.when(pl.program_id(0) == 0)
    def _():
        column_sum[...] = jnp.sum(grad_ref[...].astype(F32), axis=1, keepdims=True)

    weight = w_ref[...].astype(F32)
    product = dot(grad_ref[...], core_ref[...], 1, 0)
    moment_ref[...] = jnp.sum(product * weight, axis=0, keepdims=True)
    sum_ref[...] = jnp.sum(column_sum[...] * weight, axis=0, keepdims=True)
    out_ref[...] = jnp.transpose(
        product * scale_ref[...] + column_sum[...] * shift_ref[...]
    ).astype(BF)


def input_grad(core, grad, weight_t, scale, shift):
    rows, width = core.shape
    columns = grad.shape[0]
    block = width // 4

    def across(count):
        return pl.BlockSpec((count, block), lambda i: (0, i))

    return pl.pallas_call(
        input_grad_kernel,
        grid=(4,),
        in_specs=[
            across(rows),
            pl.BlockSpec((columns, rows), lambda i: (0, 0)),
            across(columns),
            across(1),
            across(1),
        ],
        out_specs=[pl.BlockSpec((block, columns), lambda i: (i, 0)), across(1), across(1)],
        out_shape=[jax.ShapeDtypeStruct((width, columns), BF), f32(1, width), f32(1, width)],
        scratch_shapes=[pltpu.VMEM((columns, 1), F32)],
        compiler_params=pltpu.CompilerParams(vmem_limit_bytes=48 * 1024 * 1024),
        cost_estimate=pl.CostEstimate(
            flops=2 * rows * width * columns,
            transcendentals=0,
            bytes_accessed=2 * (rows * width + rows * columns + 2 * width * columns),
        ),
    )(core, grad, weight_t, scale, shift)


def norm_rows_kernel(rows_ref, core_ref, places_ref):
    rows = core_ref.shape[0] // 2
    for part in (0, 1):
        start = part * (rows + 8)
        values = rows_ref[start : start + rows].astype(F32)
        square = jnp.mean(values * values, axis=-1, keepdims=True)
        core_ref[part * rows : (part + 1) * rows] = (values * lax.rsqrt(square + EPSILON)).astype(BF)
        places_ref[0, part] = rows_ref[start + rows : start + rows + 8, :rows].astype(F32)


def norm_rows(blocks, rows):
    width = blocks.shape[1]
    pair = 2 * (rows + 8)
    count = blocks.shape[0] // pair
    return pl.pallas_call(
        norm_rows_kernel,
        grid=(count,),
        in_specs=[pl.BlockSpec((pair, width), lambda i: (i, 0))],
        out_specs=[
            pl.BlockSpec((2 * rows, width), lambda i: (i, 0)),
            pl.BlockSpec((1, 2, 8, rows), lambda i: (i, 0, 0, 0)),
        ],
        out_shape=[
            jax.ShapeDtypeStruct((2 * count * rows, width), BF),
            f32(count, 2, 8, rows),
        ],
        compiler_params=pltpu.CompilerParams(vmem_limit_bytes=32 * 1024 * 1024),
    )(blocks)


def by_query(rows, block, first=0):
    return pl.BlockSpec((1, rows, block), lambda h, i: (h + first, 0, i))


def whole_head(rows, columns, first=0):
    return pl.BlockSpec((1, rows, columns), lambda h, i: (h + first, 0, 0))


def mask_spec(rows):
    return pl.BlockSpec((rows, 1), lambda h, i: (0, 0))


def f32(*shape):
    return jax.ShapeDtypeStruct(shape, F32)


def query_block(rows, keys, most):
    block = rows
    while block > 128 and block * keys > most:
        block //= 2
    return block


def attention_cost(scores, products, heads=1):
    return pl.CostEstimate(
        flops=heads * scores * products * 2 * 256,
        transcendentals=heads * scores,
        bytes_accessed=heads * scores // 2,
    )


def one_head(kernel, head, kept, inputs, in_specs, out_specs, out_shape, scratch, steps, cost):
    extra = len(kept) if kept else 0

    def body(*refs):
        kernel(*refs[: len(inputs)], *refs[len(inputs) + extra :])

    return pl.pallas_call(
        body,
        grid=(1, steps),
        in_specs=in_specs + [pl.BlockSpec(memory_space=pl.ANY)] * extra,
        out_specs=out_specs,
        out_shape=out_shape,
        scratch_shapes=scratch,
        input_output_aliases={len(inputs) + i: i for i in range(extra)},
        compiler_params=KERNEL,
        cost_estimate=cost,
    )(*inputs, *(kept or ()))


def self_forward(q, k, v, head, kept):
    heads, dim, rows = q.shape
    keys = k.shape[2]
    block = query_block(rows, keys, 1 << 21)
    return one_head(
        self_forward_kernel,
        head,
        kept,
        (q, k, v),
        [by_query(dim, block, head), whole_head(dim, keys, head), whole_head(dim, keys, head)],
        [by_query(dim, block, head), by_query(1, block, head)],
        [f32(heads, dim, rows), f32(heads, 1, rows)],
        [pltpu.VMEM((keys, dim), BF)],
        rows // block,
        attention_cost(rows * keys, 2),
    )


def self_backward(q, g, log_total, delta, k, v, head, kept):
    heads, dim, rows = q.shape
    keys = k.shape[2]
    block = query_block(rows, keys, 1 << 20)
    return one_head(
        self_backward_kernel,
        head,
        kept,
        (q, g, log_total, delta, k, v),
        [by_query(dim, block, head)] * 2
        + [by_query(1, block, head)] * 2
        + [whole_head(dim, keys, head)] * 2,
        [by_query(dim, block, head), whole_head(dim, keys, head), whole_head(dim, keys, head)],
        [f32(heads, dim, rows), f32(heads, dim, keys), f32(heads, dim, keys)],
        [pltpu.VMEM((keys, dim), t) for t in (BF, BF, F32, F32)],
        rows // block,
        attention_cost(rows * keys, 5),
    )


def cross_forward(q, k, v, mask):
    heads, dim, rows = q.shape
    keys = k.shape[2]
    block = query_block(rows, keys, 1 << 19)
    return pl.pallas_call(
        cross_forward_kernel,
        grid=(heads, rows // block),
        in_specs=[
            by_query(dim, block),
            whole_head(dim, keys),
            whole_head(dim, keys),
            mask_spec(keys),
        ],
        out_specs=by_query(dim, block),
        out_shape=f32(heads, dim, rows),
        compiler_params=KERNEL,
        cost_estimate=attention_cost(rows * keys, 2, heads),
    )(q, k, v, mask)


def cross_backward(q, g, k, v, mask, gate):
    heads, dim, rows = q.shape
    keys = k.shape[2]
    block = query_block(rows, keys, 1 << 19)
    return pl.pallas_call(
        cross_backward_kernel,
        grid=(heads, rows // block),
        in_specs=[
            by_query(dim, block),
            by_query(dim, block),
            whole_head(dim, keys),
            whole_head(dim, keys),
            mask_spec(keys),
            whole_head(8, 128),
        ],
        out_specs=[
            by_query(dim, block),
            whole_head(dim, keys),
            whole_head(dim, keys),
            by_query(1, block),
        ],
        out_shape=[
            f32(heads, dim, rows),
            f32(heads, dim, keys),
            f32(heads, dim, keys),
            f32(heads, 1, rows),
        ],
        compiler_params=KERNEL,
        cost_estimate=attention_cost(rows * keys, 5, heads),
    )(q, g, k, v, mask, gate)


def halves(block):
    half = block.shape[0] // 2
    return block[:half], block[half:]


def pick(block, index, dim=0, keep=False):
    return lax.dynamic_index_in_dim(block, index, dim, keepdims=keep)


def both_sides(block, axis, bit, dim):
    other = swap(block, axis)
    return jnp.where(bit == 0, jnp.stack([block, other], dim), jnp.stack([other, block], dim))


def kept_sum(block, axis, bit, dim):
    other = swap(pick(block, 1 - bit, dim).astype(BF), axis)
    return pick(block, bit, dim).astype(F32) + other.astype(F32)


def team_sum(values):
    for axis in TEAM:
        values = values + swap(values, axis)
    return values


def chips_first(first, second, bits):
    return kept_sum(first, "tz", bits[0], 0), kept_sum(second, "ty", bits[1], 1)


def chips_last(first, second, bits):
    return kept_sum(first, "ty", bits[1], 0), kept_sum(second, "tz", bits[0], 0)


def row_factor(values):
    return lax.rsqrt(jnp.mean(values * values, axis=-1, keepdims=True) + EPSILON)


def rope_tables(places, head_dim):
    pair_count = head_dim // 2
    lead_pairs = pair_count // 4
    mid_pairs = (pair_count - lead_pairs) // 2
    last_pairs = pair_count - lead_pairs - mid_pairs
    angles = []
    for which, extent in enumerate((lead_pairs, mid_pairs, last_pairs)):
        offsets = jnp.arange(extent, dtype=F32)
        angles.append(jnp.power(10000.0, -offsets / extent)[:, None] * places[which][None])
    angles = join(angles)
    cosine, sine = jnp.cos(angles), jnp.sin(angles)
    return join([cosine, cosine]), join([-sine, sine])


def turn(vectors, cosine, sine):
    half = vectors.shape[1] // 2
    crossed = join([vectors[:, half:], vectors[:, :half]], axis=1)
    return vectors * cosine + crossed * sine


def on_device(
    tokens,
    condition,
    caption,
    caption_lengths,
    positions,
    modulation_weight,
    modulation_bias,
    norm_gains,
    cross_gate,
    input_weight,
    output_weight,
    caption_key_weight,
    caption_value_weight,
    gate_weight,
    up_weight,
    down_weight,
    cotangent,
):
    clips_here, clip_rows, width = tokens.shape
    head_count = cross_gate.shape[0]
    head_dim = width // head_count
    scale = head_dim ** (-0.5)
    team = 8
    heads = head_count // team
    rows_in = input_weight.shape[0]
    part = heads * head_dim
    groups = lax.axis_size(GROUPS)
    reps = lax.axis_size("rep")
    half = lax.axis_index("half")
    bits = tuple(lax.axis_index(axis) for axis in SHARDS)
    rank = lax.axis_index(TEAM)
    clip_pair = lax.axis_index("clip")
    device = lax.axis_index(EVERY)

    def own_clip(block):
        return pick(block, half), swap(pick(block, 1 - half), "half")

    def back_clip(block):
        rows = block.shape[0] // 2
        kept, other = block[:rows], block[rows:]
        other = swap(other.astype(BF), "half").astype(block.dtype)
        return jnp.where(half == 0, jnp.stack([kept, other]), jnp.stack([other, kept]))

    def own_columns(table):
        return lax.dynamic_slice_in_dim(table, rank * part, part, table.ndim - 1)

    def by_rank(weight, split, by_shard=False):
        rows = weight.shape[0]
        if by_shard:
            tiled = weight.reshape(rows, split, team, -1)
            return jnp.transpose(tiled, (2, 0, 1, 3)).reshape(team, rows, -1)
        tiled = weight.reshape(rows, split, 2, 2, 2, -1)
        return jnp.transpose(tiled, (3, 4, 2, 0, 1, 5)).reshape(team, rows, -1)

    def from_team(blocks):
        mine = lax.all_to_all(blocks, SHARDS, split_axis=0, concat_axis=0, tiled=True)
        return mine.reshape(-1, blocks.shape[2])

    def all_reps(block):
        return lax.all_gather(block, "rep", axis=0, tiled=True) if reps > 1 else block

    def across_half(block):
        return both_sides(all_reps(block), "half", half, 0)

    def across_clip(block):
        return both_sides(block, "clip", clip_pair, 0).reshape(-1, block.shape[-1])

    places = jnp.pad(
        jnp.transpose(positions, (1, 0, 2)).astype(BF),
        ((0, 0), (0, 5), (0, width - clip_rows)),
    )
    rows_a, rows_b = own_clip(join([tokens, places], axis=1))
    in_team = from_team(by_rank(input_weight, 3))
    shard_rows = modulation_weight.shape[0]
    silu_all = jax.nn.silu(condition).astype(BF)
    silu_rows = lax.dynamic_slice_in_dim(silu_all, device * shard_rows, shard_rows, 1)
    mod_part = dot(silu_rows, modulation_weight, 1, 0)
    mod_part = mod_part.reshape(lax.axis_size("clip"), clips_here, -1)
    mod_pair = pick(mod_part, clip_pair) + swap(pick(mod_part, 1 - clip_pair), "clip")
    mod_own = pick(mod_pair, half, keep=True) + swap(pick(mod_pair, 1 - half, keep=True), "half")
    rows_a, rows_b, mod_own, in_team = together(rows_a, rows_b, mod_own, in_team)

    rows_all = lax.all_gather(join([rows_a, rows_b]), TEAM, axis=0, tiled=True)
    in_half = across_half(in_team).reshape(-1, 3 * part)
    if reps > 1:
        mod_own = lax.psum(mod_own, "rep")
    mod_own = team_sum(mod_own)
    in_half, mod_own, caption, cotangent = together(in_half, mod_own, caption, cotangent)

    in_other = swap(in_half, "clip")
    rows_cap = caption_key_weight.shape[0]
    slots_here = caption.shape[1]
    cap_a, cap_b = own_clip(caption)
    cot_a, cot_b = own_clip(cotangent)
    modulation = mod_own + modulation_bias
    shift_attn, scale_attn, gate_attn, shift_ffn, scale_ffn, gate_ffn = (
        modulation[:, i * width : (i + 1) * width] for i in range(6)
    )
    token_vals = join([rows_a[:clip_rows], rows_b[:clip_rows]]).astype(F32)
    rows_here = token_vals.shape[0]
    team_rows = team * rows_here
    row_scale = (norm_gains[0] * (1.0 + scale_attn)).reshape(width, 1)
    row_shift = shift_attn.reshape(width, 1)
    w_in, w_scaled, bias = place_weight(clip_pair, in_half, in_other, row_scale, row_shift)
    bias = bias.reshape(3 * part, 1)
    w_scaled, bias, rows_all, cap_a, cap_b, out_shard, ckey_weight, cvalue_weight = together(
        w_scaled,
        bias,
        rows_all,
        cap_a,
        cap_b,
        output_weight,
        caption_key_weight,
        caption_value_weight,
    )
    cap_team = from_team(join([by_rank(ckey_weight, 1), by_rank(cvalue_weight, 1)], axis=2))
    w_out = across_half(out_shard)
    cap_rows = jnp.where(half == 0, join([cap_a, cap_b]), join([cap_b, cap_a]))
    core_all, all_places = norm_rows(rows_all, clip_rows)
    all_places = jnp.transpose(all_places[:, :, :3], (2, 0, 1, 3)).reshape(3, team_rows)

    def by_head(block):
        return block.reshape(heads, head_dim, block.shape[-1])

    raw_qk = dot(w_scaled[:, : 2 * part], core_all, 0, 1) + bias[: 2 * part]
    raw_qk = raw_qk.reshape(2, heads, head_dim, team_rows)
    squares = jnp.sum(raw_qk * raw_qk, axis=(1, 2))
    squares, raw_qk, cap_team, cap_rows, cot_a, cot_b, w_out = together(
        team_sum(squares), raw_qk, cap_team, cap_rows, cot_a, cot_b, w_out
    )
    cap_half = across_half(cap_team)
    cap_all = lax.all_gather(cap_rows, TEAM, axis=0, tiled=True)
    w_out = both_sides(w_out, "clip", clip_pair, 0).reshape(-1, width)
    factors = lax.rsqrt(squares / width + EPSILON)[:, None, None]
    cosine, sine = rope_tables(all_places, head_dim)
    values = by_head((dot(w_scaled[:, 2 * part :], core_all, 0, 1) + bias[2 * part :]).astype(BF))
    gains = jnp.stack([own_columns(norm_gains[i]) for i in (1, 2, 3)])
    gains = gains.reshape(3, heads, head_dim, 1)
    normed_qk = raw_qk * factors
    turned = normed_qk * gains[:2]
    queries = (turn(turned[0], cosine, sine) * scale).astype(BF)
    keys = turn(turned[1], cosine, sine).astype(BF)
    all_keys, all_values = keys, values
    if reps > 1:
        all_keys, all_values = (lax.all_gather(v, "rep", axis=2, tiled=True) for v in (keys, values))

    queries, all_keys, all_values, gate_shard, up_shard, w_out, w_in_t = together(
        queries, all_keys, all_values, gate_weight, up_weight, w_out, jnp.transpose(w_in)
    )
    w_out = lax.all_gather(w_out, SHARDS, axis=0, tiled=True)
    ff_block = down_weight.shape[0]
    ff_part = groups * ff_block
    up_team = from_team(
        join([by_rank(gate_shard, groups, True), by_rank(up_shard, groups, True)], axis=2)
    )
    o_self, logs = self_forward(queries, all_keys, all_values, 0, None)
    o_self, logs = self_forward(queries, all_keys, all_values, 1, (o_self, logs))
    o_self, logs, cap_half, up_team, cap_all = together(o_self, logs, cap_half, up_team, cap_all)
    w_cap = across_clip(cap_half)
    grad_out = join([cot_a, cot_b]).astype(F32)
    d_ffn = (gate_ffn * grad_out).astype(BF)
    d_ffn_all = lax.all_gather(d_ffn, TEAM, axis=0, tiled=True)
    up_half = across_half(up_team)
    o_self, logs = self_forward(queries, all_keys, all_values, 2, (o_self, logs))
    o_self, w_cap, up_half, down_shard = together(o_self, w_cap, up_half, down_weight)
    w_gate_up = across_clip(up_half)
    down_half = across_half(down_shard)
    craw = dot(w_cap, cap_all, 0, 1)
    craw_key = by_head(craw[:part])
    square_c = jnp.sum(craw_key * craw_key, axis=(0, 1))[None]
    square_c = team_sum(square_c)
    factor_c = lax.rsqrt(square_c / width + EPSILON)[None]
    normed_c = craw_key * factor_c
    ckeys = (normed_c * gains[2]).astype(BF)
    cvalues = by_head(craw[part:]).astype(BF)
    all_ckeys, all_cvalues = ckeys, cvalues
    step = lax.axis_index("rep")
    order = jnp.arange(team * clips_here * slots_here, dtype=jnp.int32)
    in_rank = order // slots_here % clips_here
    from_rank = order // (slots_here * clips_here)
    from_shard = from_rank % 4 * 2 + from_rank // 4
    slots = ((in_rank * reps + step) * team + from_shard) * slots_here + order % slots_here
    if reps > 1:
        all_ckeys, all_cvalues = (
            lax.all_gather(v, "rep", axis=2, tiled=True) for v in (ckeys, cvalues)
        )
        slots = join([slots + (r - step) * team * slots_here for r in range(reps)])
    mask = jnp.where(slots < pick(caption_lengths, half), 0.0, NEGATIVE).astype(F32)[:, None]
    o_cross = cross_forward(queries, all_ckeys, all_cvalues, mask)
    tanh_gate = jnp.tanh(lax.dynamic_slice_in_dim(cross_gate, rank * heads, heads))
    tanh_wide = tanh_gate[:, None, None]
    mixed = (o_self + tanh_wide * o_cross).astype(BF).reshape(part, team, rows_here)
    mixed, w_out, down_half = together(jnp.transpose(mixed, (1, 0, 2)), w_out, down_half)
    w_down = across_clip(down_half)
    mixed = lax.all_to_all(mixed, TEAM, split_axis=0, concat_axis=0, tiled=True)
    out_rows = output_weight.shape[0]

    def by_shard(features):
        tiled = features.reshape(groups, team, out_rows, -1)
        return jnp.transpose(tiled, (1, 0, 2, 3)).reshape(width, -1)

    def by_group(features):
        tiled = features.reshape(team, groups, out_rows, -1)
        return jnp.transpose(tiled, (1, 0, 2, 3)).reshape(width, -1)

    combined = by_shard(mixed.reshape(width, rows_here))

    branch = dot(combined, w_out, 0, 0)
    middle = token_vals + gate_attn * branch
    factor_f = row_factor(middle)
    core_f = middle * factor_f
    ffn_in = (core_f * norm_gains[4] * (1.0 + scale_ffn) + shift_ffn).astype(BF)
    ffn_in, w_down, d_ffn_all = together(ffn_in, w_down, d_ffn_all)
    ffn_all = lax.all_gather(ffn_in, TEAM, axis=0, tiled=True)
    w_gate_up, w_down, ffn_all = together(w_gate_up, w_down, ffn_all)
    gate_up = dot(ffn_all, w_gate_up, 1, 0)
    gate_vals, up_vals = gate_up[:, :ff_part], gate_up[:, ff_part:]
    d_hidden = dot(d_ffn_all, w_down, 1, 1)
    sig = jax.nn.sigmoid(gate_vals)
    silu_gate = gate_vals * sig
    hidden = (silu_gate * up_vals).astype(BF)
    d_gate = (d_hidden * up_vals * (sig + silu_gate * (1.0 - sig))).astype(BF)
    d_up = (d_hidden * silu_gate).astype(BF)
    d_gate_up = join([d_gate, d_up], axis=1)

    def core_side(block, which, dim=0):
        count = block.shape[dim] // 2
        return lax.dynamic_slice_in_dim(block, which * count, count, dim)

    def ffn_side(which):
        return dot(core_side(d_gate_up, which), w_gate_up, 1, 1).astype(BF)

    def by_chip(mine):
        tiled = mine.reshape(2, 2, 2, clip_rows, width)
        return tiled[:, :, 0], tiled[:, :, 1]

    def add_core(kept, sent):
        return (kept.astype(F32) + swap(sent, "tc").astype(F32)).astype(BF)

    def team_parts(slice_grad):
        tiled = slice_grad.reshape(lax.axis_size("clip"), clips_here, -1, slice_grad.shape[-1])
        return kept_sum(tiled, "clip", clip_pair, 0).astype(BF)

    def half_parts(tiled):
        summed = kept_sum(tiled, "half", half, 0)
        if reps > 1:
            summed = lax.psum_scatter(summed, "rep", scatter_dimension=0, tiled=True)
        return summed

    def to_shards(summed):
        ranked = summed.astype(BF).reshape(team, -1, summed.shape[-1])
        return lax.all_to_all(ranked, SHARDS, split_axis=0, concat_axis=0, tiled=True)

    def head_columns(blocks, split):
        rows = blocks.shape[1]
        tiled = blocks.reshape(2, 2, 2, rows, split, part)
        return jnp.transpose(tiled, (3, 4, 2, 0, 1, 5)).reshape(rows, -1).astype(F32)

    def ff_columns(blocks):
        rows = blocks.shape[1]
        tiled = blocks.reshape(team, rows, groups, ff_block)
        return jnp.transpose(tiled, (1, 2, 0, 3)).reshape(rows, -1).astype(F32)

    def all_parts(slice_grad):
        return lax.psum_scatter(slice_grad, GROUPS, scatter_dimension=0, tiled=True)

    side_sent = ffn_side(1 - bits[2])
    mine = add_core(ffn_side(bits[2]), side_sent)
    pair = chips_first(*by_chip(mine), bits)
    grad_down = dot(after(hidden, mine), d_ffn_all, 0, 0).astype(BF)
    *pair, grad_down = together(*pair, grad_down)
    d_ffn_in = join(chips_last(*pair, bits))
    late_hidden = after(hidden, grad_down)
    out_sent = dot(core_side(late_hidden, 1 - bits[2]), w_down, 1, 0).astype(BF)
    out_kept = dot(core_side(late_hidden, bits[2]), w_down, 1, 0).astype(BF)
    d_ffn_in, out_sent, out_kept = together(d_ffn_in, out_sent, out_kept)

    out_mine = add_core(out_kept, out_sent)
    down_half = team_parts(after(grad_down, d_ffn_in))
    d_shift_ffn = jnp.sum(d_ffn_in, axis=0, keepdims=True)
    moment_f = jnp.sum(d_ffn_in * core_f, axis=0, keepdims=True)
    d_scale_ffn = moment_f * norm_gains[4]
    d_gain_ffn = moment_f * (1.0 + scale_ffn)
    d_core = d_ffn_in * (norm_gains[4] * (1.0 + scale_ffn))
    d_middle = grad_out + factor_f * (
        d_core - core_f * jnp.mean(d_core * core_f, axis=-1, keepdims=True)
    )
    d_branch = (gate_attn * d_middle).astype(BF)
    d_gate_attn = jnp.sum(d_middle * branch, axis=0, keepdims=True)
    d_combined = by_group(dot(w_out, d_branch, 1, 1).astype(BF))
    d_mixed = lax.all_to_all(
        d_combined.reshape(team, part, rows_here), TEAM, split_axis=0, concat_axis=0, tiled=True
    )
    late_ffn, late_gate, out_mine = together(ffn_all, d_gate_up, out_mine, d_combined)[:3]
    grad_gate_up = dot(late_ffn, late_gate, 0, 0).astype(BF)
    d_mixed, grad_gate_up = together(d_mixed, grad_gate_up)
    up_rows = all_parts(grad_gate_up)
    d_self = by_head(jnp.transpose(d_mixed, (1, 0, 2)).reshape(part, team_rows))

    out_pair = chips_first(*by_chip(out_mine), bits)
    gate_tile = jnp.broadcast_to(tanh_wide, (heads, 8, 128))
    dq_cross, d_ckeys, d_cvalues, gate_rows = cross_backward(
        queries, d_self, all_ckeys, all_cvalues, mask, gate_tile
    )
    d_cross_gate = jnp.sum(gate_rows, axis=(1, 2)) * (1.0 - tanh_gate * tanh_gate)
    if reps > 1:
        d_ckeys, d_cvalues = (
            lax.psum_scatter(v, "rep", scatter_dimension=2, tiled=True)
            for v in (d_ckeys, d_cvalues)
        )

    def team_mean(block):
        return jnp.sum(block, axis=(-3, -2))

    scaled_c = d_ckeys * gains[2]
    mean_c = team_mean(scaled_c * normed_c)[None]
    mean_c = mean_c + swap(mean_c, "tc")
    grad_output = dot(after(combined, dq_cross), d_branch, 1, 0).astype(BF)
    delta = jnp.sum(d_self.astype(F32) * o_self, axis=1, keepdims=True)
    delta, grad_output, mean_c, down_half, *out_pair = together(
        delta, grad_output, mean_c, down_half, *out_pair
    )
    sum_down = half_parts(down_half)
    sum_output = lax.psum_scatter(grad_output, SHARDS, scatter_dimension=0, tiled=True)
    ffn_out = join(chips_last(*out_pair, bits))
    mean_c = mean_c + swap(mean_c, "ty")
    mean_c = mean_c + swap(mean_c, "tz")
    backs = self_backward(queries, d_self, logs, delta, all_keys, all_values, 0, None)
    *backs, delta, mean_c, ffn_out, up_rows = together(*backs, delta, mean_c, ffn_out, up_rows)
    result = back_clip((middle + gate_ffn * ffn_out).astype(BF))
    d_gate_ffn = jnp.sum(grad_out * ffn_out, axis=0, keepdims=True)
    mean_c = mean_c[None] / width
    d_craw = factor_c * (scaled_c - normed_c * mean_c)
    d_gain_c = jnp.sum(d_ckeys * normed_c, axis=2).reshape(1, part)
    cap_low = join([d_craw, d_cvalues]).reshape(2 * part, -1).astype(BF)
    cap_half = team_parts(dot(cap_all, cap_low, 0, 1).astype(BF))
    d_cap = dot(cap_low, w_cap, 0, 1).astype(BF)
    d_cap = d_cap.reshape(2, 2, 2, clips_here * slots_here, -1)
    d_cap = kept_sum(d_cap, "tc", bits[2], 0).astype(BF)
    backs = self_backward(queries, d_self, logs, delta, all_keys, all_values, 1, backs)
    *backs, delta, up_rows, sum_down, d_cap, cap_half = together(
        *backs, delta, up_rows, sum_down, d_cap, cap_half
    )
    cap_rows = half_parts(cap_half)
    d_cap = kept_sum(d_cap, "tz", bits[0], 0).astype(BF)
    sum_gate_up = to_shards(up_rows)
    backs = self_backward(queries, d_self, logs, delta, all_keys, all_values, 2, backs)
    *backs, result, sum_gate_up, d_cap = together(*backs, result, sum_gate_up, d_cap)
    d_cap = kept_sum(d_cap, "ty", bits[1], 0).astype(BF)
    dq_self, dk, dv = backs
    if reps > 1:
        dk, dv = (lax.psum_scatter(v, "rep", scatter_dimension=2, tiled=True) for v in (dk, dv))

    turned_grad = jnp.stack(
        [turn((dq_self + dq_cross) * scale, cosine, -sine), turn(dk, cosine, -sine)]
    )
    scaled_qk = turned_grad * gains[:2]
    mean_qk = team_sum(team_mean(scaled_qk * normed_qk))[:, None, None] / width
    d_gain_qk = jnp.sum(turned_grad * normed_qk, axis=3).reshape(2, part)
    d_qk = (factors * (scaled_qk - normed_qk * mean_qk)).reshape(2 * part, team_rows)
    d_projected = join([d_qk, dv.reshape(part, team_rows)]).astype(BF)

    def attn_side(which):
        return dot(core_side(d_projected, which, 1), w_in, 0, 1).astype(BF)

    side_sent = attn_side(1 - bits[2])
    mine = add_core(attn_side(bits[2]), side_sent)
    in_grad, moment_a, d_shift_attn = input_grad(
        core_all, d_projected, w_in_t, row_scale.reshape(1, width), row_shift.reshape(1, width)
    )
    mine, in_grad, cap_rows = together(mine, in_grad, cap_rows)
    in_half = team_parts(in_grad)
    pair = chips_first(*by_chip(mine), bits)
    d_scale_attn = moment_a * norm_gains[0]
    d_gain_attn = moment_a * (1.0 + scale_attn)

    def placed(values):
        wide = jnp.tile(values, (1, width // values.shape[1]))
        spot = jnp.arange(width, dtype=jnp.int32) // values.shape[1]
        return jnp.where(spot == rank, wide, 0.0)

    gate_row = jnp.pad(d_cross_gate[None], ((0, 0), (0, width // team - heads)))
    sums = join(
        [
            d_shift_attn,
            d_scale_attn,
            d_gate_attn,
            d_shift_ffn,
            d_scale_ffn,
            d_gate_ffn,
            d_gain_attn,
            d_gain_ffn,
            placed(join([d_gain_qk, d_gain_c, gate_row])),
        ]
    )
    for axis in ("tc", "ty"):
        sums = sums + swap(sums, axis)
    sums = both_sides(sums, "clip", clip_pair, 0)
    *pair, sums, in_half = together(*pair, sums, in_half)
    in_rows = half_parts(in_half)
    d_attn_in = join(chips_last(*pair, bits))
    sum_output = after(sum_output, *pair).reshape(lax.axis_size("clip"), clips_here, -1, width)
    sum_output = kept_sum(sum_output, "clip", clip_pair, 0)
    sums = sums + swap(sums, "tz")
    if reps > 1:
        sums = lax.psum(sums, "rep")
    sums = both_sides(sums, "half", half, 1)
    d_attn_in, sums, sum_gate_up = together(d_attn_in, sums, sum_gate_up)
    sum_gate, sum_up = ff_columns(sum_gate_up[..., :ff_part]), ff_columns(sum_gate_up[..., ff_part:])
    sum_cap = to_shards(cap_rows)
    factor_a = row_factor(token_vals)
    core_a = token_vals * factor_a
    d_core = d_attn_in * (norm_gains[0] * (1.0 + scale_attn))
    d_tokens = back_clip(
        d_middle
        + factor_a * (d_core - core_a * jnp.mean(d_core * core_a, axis=-1, keepdims=True))
    )
    mod_low = sums[:, :, :6].astype(BF).reshape(condition.shape[0], -1)
    small = jnp.sum(sums[:, :, 6:], axis=(0, 1))
    gain_sum = join([small[:1], small[2:5], small[1:2]])
    gate_sum = small[5].reshape(team, -1)[:, :heads].reshape(-1)
    d_bias = jnp.sum(mod_low.astype(F32), axis=0)
    d_silu = dot(mod_low, modulation_weight, 1, 1)
    d_silu = lax.dynamic_update_slice_in_dim(
        jnp.zeros(condition.shape, F32), d_silu, device * shard_rows, 1
    )
    d_silu, in_rows = together(d_silu, in_rows)
    sum_input = to_shards(in_rows)
    if reps > 1:
        d_silu = lax.psum(d_silu, "rep")
    for axis in ("tc", "ty", "tz", "half", "clip"):
        d_silu = d_silu + swap(d_silu, axis)
    _, silu_back = jax.vjp(jax.nn.silu, condition)
    d_condition = silu_back(d_silu)[0]
    grad_mod = dot(silu_rows, mod_low, 0, 0)

    sum_input = head_columns(sum_input, 3)
    sum_ckey = head_columns(sum_cap[..., :part], 1)
    sum_cvalue = head_columns(sum_cap[..., part:], 1)
    sum_output = half_parts(after(sum_output, d_attn_in))
    d_cap = after(d_cap, d_attn_in).astype(F32)
    d_cap = d_cap.reshape(clips_here, slots_here, -1)
    d_caption = back_clip(join([pick(d_cap, half), pick(d_cap, 1 - half)]))
    return (
        result,
        d_tokens,
        d_caption,
        d_condition,
        grad_mod,
        d_bias,
        gain_sum,
        gate_sum,
        sum_input,
        sum_output,
        sum_ckey,
        sum_cvalue,
        sum_gate,
        sum_up,
        sum_down,
    )


def solution(mesh):
    clip_count, seq_count = mesh.shape["clip"], mesh.shape["seq"]

    def program(*arrays):
        halves = arrays[0].shape[0] // clip_count
        shape = (clip_count, halves, seq_count // (halves * 8), 2, 2, 2)
        fine = Mesh(mesh.devices.reshape(shape), EVERY)
        rows = P("clip", SEQ, None)
        shard = P(EVERY, None)
        mapped = jax.shard_map(
            on_device,
            mesh=fine,
            in_specs=(
                rows,
                P(),
                rows,
                P("clip"),
                P(None, "clip", SEQ),
                shard,
                P(),
                P(),
                P(),
                shard,
                shard,
                shard,
                shard,
                shard,
                shard,
                shard,
                rows,
            ),
            out_specs=(rows, rows, rows, P(), shard, P(), P(), P()) + (shard,) * 7,
            check_vma=False,
        )
        return mapped(*arrays)

    return program
```
